256 devices in a mesh: seq: 16 (over z, core), ch: 16 (over y, x).
Axes of the slice: x: 4, y: 4, z: 8, core: 2. Of those that a mesh axis runs over, the one named last changes fastest.
Arguments:
- query: bfloat16 [2048, 8192], P('seq', 'ch'), may hold values from -6 to 6
- key: bfloat16 [2048, 8192], P('seq', 'ch'), may hold values from -6 to 6
- value: bfloat16 [2048, 8192], P('seq', 'ch'), may hold values from -6 to 6
- short_taps: float32 [3, 3, 8192], P(None, None, 'ch'), may hold values from -3 to 3
- decay_rate: float32 [16, 8192], P(None, 'ch'), may hold values from 0.00012207031 to 0.05
- residue: float32 [16, 8192], P(None, 'ch'), may hold values from -2 to 2
- skip_gain: float32 [8192], P('ch'), may hold values from -4 to 4
- out_weight: bfloat16 [8192, 8192], P('ch', 'seq'), may hold values from -0.09375 to 0.09375
- grad_out: bfloat16 [2048, 8192], P('seq', 'ch'), may hold values from -6 to 6
Outputs:
- mixed: bfloat16 [2048, 8192], P('seq', 'ch')
- grad_query: bfloat16 [2048, 8192], P('seq', 'ch')
- grad_key: bfloat16 [2048, 8192], P('seq', 'ch')
- grad_value: bfloat16 [2048, 8192], P('seq', 'ch')
The draws below stay inside these ranges and needn't reach their ends.
All inputs are finite; a program needn't handle non-finite values.
Results may differ from the reference program's by a relative error of at most 0.017.
Values may be sent and summed in bfloat16 or wider, within the bound.
A program may use at most 128 MiB of HBM per device.

```python
import math
import jax
import jax.numpy as jnp
from jax import lax

D = 8192
MODES = 16
SHORT = 3
SEQLEN = 2048
N_CH = 16


def with_spikes(values, stream_key, source, target, shards_of, factor):
    owner, partner = [(jnp.arange(values.shape[position]) // (values.shape[position] // shards_of)).reshape([-1 if axis == position else 1 for axis in range(values.ndim)]) for position in (source, target)]
    chosen = jax.random.permutation(stream_key, shards_of)[partner]
    strong = (owner == chosen) | (owner == (partner + shards_of // 2) % shards_of)
    return jnp.where(strong, factor * values, values)


def block_levels(rng, extent, cuts, low, largest):
    gain = 1.0
    for axis_at, blocks in cuts:
        draws = jax.random.uniform(jax.random.fold_in(jax.random.fold_in(rng, 6), axis_at), (blocks,), jnp.float32, low / len(cuts), largest / len(cuts))
        gain = gain * jnp.repeat(jnp.exp(draws), extent[axis_at] // blocks).reshape((-1,) + (1,) * (len(extent) - 1 - axis_at))
    return gain


def centred(own_key, extent, deviation, most, split=(), kind=jnp.bfloat16):
    level = block_levels(own_key, extent, split, -0.22, 0.18) if split else 1.0
    drawn = jax.random.normal(own_key, extent, jnp.float32) * deviation * level
    return jnp.minimum(jnp.maximum(drawn, -most), most).astype(kind)


def gaussian_with(rng, dims, width, most, pieces, heavy, dtype=jnp.bfloat16):
    values = width * jax.random.normal(rng, dims, jnp.float32)
    if pieces:
        values = values * block_levels(rng, dims, pieces, -0.22, 0.18)
    return jnp.clip(with_spikes(values, jax.random.fold_in(rng, 3), *heavy), -most, most).astype(dtype)


def setup_inputs(seed: int = 0) -> dict:
    streams_of = jax.random.split(jax.random.key(seed), 10)
    query = centred(streams_of[0], (SEQLEN, D), 1.0, 6.0, ((0, 16), (1, 16)))
    key = centred(streams_of[1], (SEQLEN, D), 1.0, 6.0, ((0, 16), (1, 16)))
    value = centred(streams_of[2], (SEQLEN, D), 1.0, 6.0, ((0, 16), (1, 16)))
    short_taps = centred(streams_of[3], (SHORT, 3, D), 0.6, 3.0, ((2, 16),), jnp.float32)
    decay_rate = jnp.clip(jnp.exp(math.log(0.05) - 6.015181 * jax.random.uniform(streams_of[4], (MODES, D), jnp.float32) ** block_levels(streams_of[4], (MODES, D), ((1, 16),), -0.2, 0.2)), 0.00012207031, 0.05)
    residue = centred(streams_of[5], (MODES, D), 0.3, 2.0, ((1, 16),), jnp.float32)
    skip_gain = centred(streams_of[6], (D,), 1.0, 4.0, ((0, 16),), jnp.float32)
    out_weight = gaussian_with(streams_of[7], (D, D), D ** -0.5, 0.09375, ((0, 16), (1, 16)), (0, 1, 16, 2.0))
    grad_out = centred(streams_of[8], (SEQLEN, D), 1.0, 6.0, ((0, 16), (1, 16)))
    return {"query": query, "key": key, "value": value, "short_taps": short_taps, "decay_rate": decay_rate, "residue": residue, "skip_gain": skip_gain, "out_weight": out_weight, "grad_out": grad_out}


def short_forward(stream, taps):
    length = stream.shape[0]
    padded = jnp.pad(stream.astype(jnp.float32), ((SHORT - 1, 0), (0, 0)))
    result = jnp.zeros(stream.shape, jnp.float32)
    for tap_index in range(SHORT):
        begin = SHORT - 1 - tap_index
        result = result + taps[tap_index][None, :] * padded[begin:begin + length]
    return result

def short_backward(grads, taps):
    length = grads.shape[0]
    padded = jnp.pad(grads, ((0, SHORT - 1), (0, 0)))
    result = jnp.zeros(grads.shape, jnp.float32)
    for tap_index in range(SHORT):
        result = result + taps[tap_index][None, :] * padded[tap_index:tap_index + length]
    return result

def filter_table(decay_rate, residue, length):
    mode_scale = residue * jnp.sqrt(-jnp.expm1(-2.0 * decay_rate))
    offsets = jnp.arange(length).astype(jnp.float32)
    table = jnp.zeros((length, decay_rate.shape[1]), jnp.float32)
    for mode in range(MODES):
        table = table + mode_scale[mode][None, :] * jnp.exp(-decay_rate[mode][None, :] * offsets[:, None])
    return table

def causal_conv(signal, table):
    length = signal.shape[0]
    group = D // N_CH
    sig_groups = signal.reshape(length, N_CH, group).transpose(1, 0, 2)
    tab_groups = table.reshape(length, N_CH, group).transpose(1, 0, 2)

    def one_group(pair):
        sig_part, tab_part = pair
        spectrum = jnp.fft.rfft(sig_part, 2 * length, axis=0) * jnp.fft.rfft(tab_part, 2 * length, axis=0)
        return jnp.fft.irfft(spectrum, 2 * length, axis=0)[:length].astype(jnp.float32)
    result = lax.map(one_group, (sig_groups, tab_groups))
    return result.transpose(1, 0, 2).reshape(length, D)

def reference(query, key, value, short_taps, decay_rate, residue, skip_gain, out_weight, grad_out):
    length = query.shape[0]
    group = D // N_CH
    q_short = short_forward(query, short_taps[:, 0, :])
    k_short = short_forward(key, short_taps[:, 1, :])
    v_short = short_forward(value, short_taps[:, 2, :])
    gated = k_short * v_short
    table = filter_table(decay_rate, residue, length)
    long_out = causal_conv(gated, table) + skip_gain[None, :] * gated
    mixer = (q_short * long_out).astype(jnp.bfloat16)

    def add_group(index, total):
        start = (index * group).astype(jnp.int32)
        cols = lax.dynamic_slice_in_dim(mixer, start, group, 1)
        rows_w = lax.dynamic_slice_in_dim(out_weight, start, group, 0)
        part = jnp.dot(cols, rows_w, preferred_element_type=jnp.float32)
        return total + lax.optimization_barrier(part.astype(jnp.bfloat16)).astype(jnp.float32)
    mixed = lax.fori_loop(0, N_CH, add_group, jnp.zeros((length, D), jnp.float32)).astype(jnp.bfloat16)
    grad_mixer = jnp.dot(grad_out, out_weight.T, preferred_element_type=jnp.float32)
    grad_qshort = grad_mixer * long_out
    grad_long = grad_mixer * q_short
    grad_gated = jnp.flip(causal_conv(jnp.flip(grad_long, 0), table), 0) + skip_gain[None, :] * grad_long
    grad_kshort = grad_gated * v_short
    grad_vshort = grad_gated * k_short
    grad_query = short_backward(grad_qshort, short_taps[:, 0, :]).astype(jnp.bfloat16)
    grad_key = short_backward(grad_kshort, short_taps[:, 1, :]).astype(jnp.bfloat16)
    grad_value = short_backward(grad_vshort, short_taps[:, 2, :]).astype(jnp.bfloat16)
    return (mixed, grad_query, grad_key, grad_value)
```

```python
import jax
import jax.numpy as jnp
from jax import lax
from jax.sharding import PartitionSpec as P


def from_behind(block, axis, distance):
    devices = range(lax.axis_size(axis))
    route = [(i - distance, i) for i in devices if i - distance in devices]
    return lax.ppermute(block, axis, route)


def per_device(query, key, value, short_taps, decay_rate, residue, skip_gain, out_weight, grad_out):
    tok_rows, chan_width = query.shape
    tap_count = short_taps.shape[0]
    mode_count = decay_rate.shape[0]
    highest = lax.Precision.HIGHEST
    count = lax.axis_size("seq")
    place = lax.axis_index("seq")

    columns = lax.all_gather(out_weight, "seq", axis=1, tiled=True)
    grad_full = lax.all_gather(grad_out, "ch", axis=1, tiled=True)

    streams = jnp.stack([query, key, value])
    before = from_behind(streams[:, tok_rows - (tap_count - 1) :, :], "seq", 1)
    extended = jnp.concatenate([before, streams], axis=1).astype(jnp.float32)
    featured = jnp.zeros((3, tok_rows, chan_width), jnp.float32)
    for tap_index in range(tap_count):
        begin = tap_count - 1 - tap_index
        featured = (
            featured + short_taps[tap_index][:, None, :] * extended[:, begin : begin + tok_rows, :]
        )
    q_short = featured[0]
    k_short = featured[1]
    v_short = featured[2]
    gated = k_short * v_short

    mode_scale = residue * jnp.sqrt(-jnp.expm1(-2.0 * decay_rate))
    offsets = jnp.arange(tok_rows).astype(jnp.float32)
    shrink = jnp.exp(-decay_rate[None, :, :] * offsets[:, None, None])
    grow = jnp.exp(decay_rate[None, :, :] * offsets[:, None, None])
    scaled_shrink = mode_scale[None] * shrink
    scaled_grow = mode_scale[None] * grow
    one_step = jnp.exp(-decay_rate)
    block_decay = jnp.exp(-decay_rate * tok_rows)
    rows = jnp.arange(tok_rows)
    lower = (rows[:, None] >= rows[None, :]).astype(jnp.float32)
    upper = (rows[:, None] <= rows[None, :]).astype(jnp.float32)

    def prefix(tri, weights, signal):
        spread = (weights * signal[:, None, :]).reshape(tok_rows, mode_count * chan_width)
        summed = jnp.dot(tri, spread, precision=highest, preferred_element_type=jnp.float32)
        return summed.reshape(tok_rows, mode_count, chan_width)

    fwd_sums = prefix(lower, grow, gated)
    fwd_final = shrink[tok_rows - 1] * fwd_sums[tok_rows - 1]

    grad_mixer = lax.dot_general(
        grad_full, columns, (((1,), (1,)), ((), ())), preferred_element_type=jnp.float32
    )
    grad_long = grad_mixer * q_short
    bwd_sums = prefix(upper, shrink, grad_long)
    bwd_final = bwd_sums[0]

    finals = jnp.stack([fwd_final, bwd_final]).astype(jnp.bfloat16)
    gathered = lax.all_gather(finals, "seq").astype(jnp.float32)
    source = jnp.arange(count)
    fwd_gap = place - 1 - source
    bwd_gap = source - place - 1
    fwd_weight = jnp.where(
        (fwd_gap >= 0)[:, None, None],
        jnp.exp(-decay_rate[None] * (tok_rows * jnp.maximum(fwd_gap, 0)).astype(jnp.float32)[:, None, None]),
        0.0,
    )
    bwd_weight = jnp.where(
        (bwd_gap >= 0)[:, None, None],
        jnp.exp(-decay_rate[None] * (tok_rows * jnp.maximum(bwd_gap, 0)).astype(jnp.float32)[:, None, None]),
        0.0,
    )
    fwd_entry = jnp.sum(fwd_weight * gathered[:, 0], axis=0) * one_step
    bwd_entry = jnp.sum(bwd_weight * gathered[:, 1], axis=0) * block_decay

    long_out = (
        jnp.sum(scaled_shrink * (fwd_sums + fwd_entry[None]), axis=1) + skip_gain[None, :] * gated
    )
    mixer = (q_short * long_out).astype(jnp.bfloat16)
    partial_value = jnp.dot(mixer, columns, preferred_element_type=jnp.float32)
    mixed = lax.psum_scatter(
        partial_value.astype(jnp.bfloat16), "ch", scatter_dimension=1, tiled=True
    )

    grad_qshort = grad_mixer * long_out
    grad_gated = (
        jnp.sum(scaled_grow * (bwd_sums + bwd_entry[None]), axis=1) + skip_gain[None, :] * grad_long
    )
    grad_stack = jnp.stack([grad_qshort, grad_gated * v_short, grad_gated * k_short])
    after = from_behind(grad_stack[:, : tap_count - 1, :], "seq", -1)
    extended_back = jnp.concatenate([grad_stack, after], axis=1)
    grads = jnp.zeros((3, tok_rows, chan_width), jnp.float32)
    for tap_index in range(tap_count):
        grads = (
            grads
            + short_taps[tap_index][:, None, :]
            * extended_back[:, tap_index : tap_index + tok_rows, :]
        )
    grads = grads.astype(jnp.bfloat16)
    return (mixed, grads[0], grads[1], grads[2])


def solution(mesh):
    in_specs = (
        P("seq", "ch"),
        P("seq", "ch"),
        P("seq", "ch"),
        P(None, None, "ch"),
        P(None, "ch"),
        P(None, "ch"),
        P("ch"),
        P("ch", "seq"),
        P("seq", "ch"),
    )
    out_specs = (P("seq", "ch"), P("seq", "ch"), P("seq", "ch"), P("seq", "ch"))
    return jax.shard_map(
        per_device, mesh=mesh, in_specs=in_specs, out_specs=out_specs, check_vma=False
    )
```

```python
import jax
import jax.numpy as jnp
from jax import lax
from jax.sharding import PartitionSpec as P


def from_behind(block, axis, distance):
    devices = range(lax.axis_size(axis))
    route = [(i - distance, i) for i in devices if i - distance in devices]
    return lax.ppermute(block, axis, route)


def per_device(query, key, value, short_taps, decay_rate, residue, skip_gain, out_weight, grad_out):
    tok_rows, chan_width = query.shape
    tap_count = short_taps.shape[0]
    mode_count = decay_rate.shape[0]
    highest = lax.Precision.HIGHEST
    count = lax.axis_size("seq")
    place = lax.axis_index("seq")

    core = place % 2
    half = count // 2
    groups = [[side + 2 * step for step in range(half)] for side in range(2)]
    mine = lax.all_gather(out_weight, "seq", axis_index_groups=groups)
    other = lax.ppermute(mine, "seq", [(i, i ^ 1) for i in range(count)])
    grad_full = lax.all_gather(grad_out, "ch", axis=1, tiled=True)
    grad_split = grad_full.reshape(tok_rows, half, 2, chan_width)
    grad_mine = lax.dynamic_index_in_dim(grad_split, core, 2, False)
    grad_other = lax.dynamic_index_in_dim(grad_split, 1 - core, 2, False)

    streams = jnp.stack([query, key, value])
    before = from_behind(streams[:, tok_rows - (tap_count - 1) :, :], "seq", 1)
    extended = jnp.concatenate([before, streams], axis=1).astype(jnp.float32)
    featured = jnp.zeros((3, tok_rows, chan_width), jnp.float32)
    for tap_index in range(tap_count):
        begin = tap_count - 1 - tap_index
        featured = (
            featured + short_taps[tap_index][:, None, :] * extended[:, begin : begin + tok_rows, :]
        )
    q_short = featured[0]
    k_short = featured[1]
    v_short = featured[2]
    gated = k_short * v_short

    mode_scale = residue * jnp.sqrt(-jnp.expm1(-2.0 * decay_rate))
    offsets = jnp.arange(tok_rows).astype(jnp.float32)
    shrink = jnp.exp(-decay_rate[None, :, :] * offsets[:, None, None])
    grow = jnp.exp(decay_rate[None, :, :] * offsets[:, None, None])
    scaled_shrink = mode_scale[None] * shrink
    scaled_grow = mode_scale[None] * grow
    one_step = jnp.exp(-decay_rate)
    block_decay = jnp.exp(-decay_rate * tok_rows)
    rows = jnp.arange(tok_rows)
    lower = (rows[:, None] >= rows[None, :]).astype(jnp.float32)
    upper = (rows[:, None] <= rows[None, :]).astype(jnp.float32)

    def prefix(tri, weights, signal):
        spread = (weights * signal[:, None, :]).reshape(tok_rows, mode_count * chan_width)
        summed = jnp.dot(tri, spread, precision=highest, preferred_element_type=jnp.float32)
        return summed.reshape(tok_rows, mode_count, chan_width)

    fwd_sums = prefix(lower, grow, gated)
    fwd_final = shrink[tok_rows - 1] * fwd_sums[tok_rows - 1]

    grad_mixer = jnp.einsum(
        "tzc,zrc->tr", grad_mine, mine, preferred_element_type=jnp.float32
    ) + jnp.einsum("tzc,zrc->tr", grad_other, other, preferred_element_type=jnp.float32)
    grad_long = grad_mixer * q_short
    bwd_sums = prefix(upper, shrink, grad_long)
    bwd_final = bwd_sums[0]

    def shift(block, distance):
        route = [(i, i + distance) for i in range(count) if 0 <= i + distance < count]
        return lax.ppermute(block, "seq", route)

    def entering(final, direction):
        state = shift(final, direction)
        distance = 1
        while distance < count:
            jump = jnp.exp(-decay_rate * float(tok_rows * distance))
            state = state + jump * shift(state, direction * distance)
            distance *= 2
        return state

    fwd_entry = entering(fwd_final, 1) * one_step
    bwd_entry = entering(bwd_final, -1) * block_decay

    long_out = (
        jnp.sum(scaled_shrink * (fwd_sums + fwd_entry[None]), axis=1) + skip_gain[None, :] * gated
    )
    mixer = (q_short * long_out).astype(jnp.bfloat16)
    part_mine = jnp.einsum("tr,zrc->ztc", mixer, mine, preferred_element_type=jnp.float32)
    part_other = jnp.einsum("tr,zrc->ztc", mixer, other, preferred_element_type=jnp.float32)
    part_mine = part_mine.astype(jnp.bfloat16)
    part_other = part_other.astype(jnp.bfloat16)
    parts = jnp.where(
        core == 0,
        jnp.stack([part_mine, part_other], axis=1),
        jnp.stack([part_other, part_mine], axis=1),
    ).reshape(count, tok_rows, chan_width)
    received = lax.all_to_all(parts, "ch", 0, 0, tiled=True)
    mixed = jnp.sum(received.astype(jnp.float32), axis=0).astype(jnp.bfloat16)

    grad_qshort = grad_mixer * long_out
    grad_gated = (
        jnp.sum(scaled_grow * (bwd_sums + bwd_entry[None]), axis=1) + skip_gain[None, :] * grad_long
    )
    grad_stack = jnp.stack([grad_qshort, grad_gated * v_short, grad_gated * k_short])
    after = from_behind(grad_stack[:, : tap_count - 1, :], "seq", -1)
    extended_back = jnp.concatenate([grad_stack, after], axis=1)
    grads = jnp.zeros((3, tok_rows, chan_width), jnp.float32)
    for tap_index in range(tap_count):
        grads = (
            grads
            + short_taps[tap_index][:, None, :]
            * extended_back[:, tap_index : tap_index + tok_rows, :]
        )
    grads = grads.astype(jnp.bfloat16)
    return (mixed, grads[0], grads[1], grads[2])


def solution(mesh):
    in_specs = (
        P("seq", "ch"),
        P("seq", "ch"),
        P("seq", "ch"),
        P(None, None, "ch"),
        P(None, "ch"),
        P(None, "ch"),
        P("ch"),
        P("ch", "seq"),
        P("seq", "ch"),
    )
    out_specs = (P("seq", "ch"), P("seq", "ch"), P("seq", "ch"), P("seq", "ch"))
    return jax.shard_map(
        per_device, mesh=mesh, in_specs=in_specs, out_specs=out_specs, check_vma=False
    )
```

```python
import jax
import jax.numpy as jnp
from jax import lax
from jax.sharding import PartitionSpec as P


def per_device(query, key, value, short_taps, decay_rate, residue, skip_gain, out_weight, grad_out):
    tok_rows, chan_width = query.shape
    tap_count = short_taps.shape[0]
    mode_count = decay_rate.shape[0]
    highest = lax.Precision.HIGHEST
    count = lax.axis_size("seq")
    lanes = lax.axis_size("ch")
    place = lax.axis_index("seq")
    core = place % 2
    half = count // 2

    def shift(block, distance):
        route = [(i, i + distance) for i in range(count) if 0 <= i + distance < count]
        return lax.ppermute(block, "seq", route)

    def transpose(block):
        route = [(j * lanes + k, k * lanes + j) for j in range(count) for k in range(lanes)]
        return lax.ppermute(block, ("seq", "ch"), route)

    grad_cols = lax.all_gather(transpose(grad_out), "ch", axis=0, tiled=True)

    streams = jnp.stack([query, key, value])
    before = shift(streams[:, tok_rows - (tap_count - 1) :, :], 1)
    extended = jnp.concatenate([before, streams], axis=1).astype(jnp.float32)
    featured = jnp.zeros((3, tok_rows, chan_width), jnp.float32)
    for tap_index in range(tap_count):
        begin = tap_count - 1 - tap_index
        featured = (
            featured + short_taps[tap_index][:, None, :] * extended[:, begin : begin + tok_rows, :]
        )
    q_short = featured[0]
    k_short = featured[1]
    v_short = featured[2]
    gated = k_short * v_short

    mode_scale = residue * jnp.sqrt(-jnp.expm1(-2.0 * decay_rate))
    offsets = jnp.arange(tok_rows).astype(jnp.float32)
    shrink = jnp.exp(-decay_rate[None, :, :] * offsets[:, None, None])
    grow = jnp.exp(decay_rate[None, :, :] * offsets[:, None, None])
    one_step = jnp.exp(-decay_rate)
    block_decay = jnp.exp(-decay_rate * tok_rows)
    rows = jnp.arange(tok_rows)
    lower = (rows[:, None] >= rows[None, :]).astype(jnp.float32)
    upper = (rows[:, None] <= rows[None, :]).astype(jnp.float32)

    def prefix(tri, weights, signal):
        spread = (weights * signal[:, None, :]).reshape(tok_rows, mode_count * chan_width)
        summed = jnp.dot(tri, spread, precision=highest, preferred_element_type=jnp.float32)
        return summed.reshape(tok_rows, mode_count, chan_width)

    def entering(final, direction):
        state = shift(final, direction)
        distance = 1
        while distance < count:
            jump = jnp.exp(-decay_rate * float(tok_rows * distance))
            state = state + jump * shift(state, direction * distance)
            distance *= 2
        return state

    fwd_sums = prefix(lower, grow, gated)
    fwd_entry = entering(shrink[tok_rows - 1] * fwd_sums[tok_rows - 1], 1) * one_step
    long_out = (
        jnp.sum((mode_scale[None] * shrink) * (fwd_sums + fwd_entry[None]), axis=1)
        + skip_gain[None, :] * gated
    )
    mixer = (q_short * long_out).astype(jnp.bfloat16)

    groups = [[side + 2 * step for step in range(half)] for side in range(2)]
    mine = lax.all_gather(mixer, "seq", axis_index_groups=groups)
    other = lax.ppermute(mine, "seq", [(i, i ^ 1) for i in range(count)])
    part_mine = jnp.einsum("ztr,rc->ztc", mine, out_weight, preferred_element_type=jnp.float32)
    part_other = jnp.einsum("ztr,rc->ztc", other, out_weight, preferred_element_type=jnp.float32)
    part_mine = part_mine.astype(jnp.bfloat16)
    part_other = part_other.astype(jnp.bfloat16)
    parts = jnp.where(
        core == 0,
        jnp.stack([part_mine, part_other], axis=1),
        jnp.stack([part_other, part_mine], axis=1),
    ).reshape(count, tok_rows, chan_width)
    received = lax.all_to_all(parts, "ch", 0, 0, tiled=True)
    mixed = transpose(jnp.sum(received.astype(jnp.float32), axis=0).astype(jnp.bfloat16))

    partial_grad = lax.dot_general(
        grad_cols, out_weight, (((1,), (1,)), ((), ())), preferred_element_type=jnp.float32
    )
    partial_grad = partial_grad.astype(jnp.bfloat16).reshape(count, tok_rows, chan_width)
    grad_parts = lax.all_to_all(partial_grad, "seq", 0, 0, tiled=True)
    grad_mixer = jnp.sum(grad_parts.astype(jnp.float32), axis=0)

    grad_qshort = grad_mixer * long_out
    grad_long = grad_mixer * q_short
    bwd_sums = prefix(upper, shrink, grad_long)
    bwd_entry = entering(bwd_sums[0], -1) * block_decay
    grad_gated = (
        jnp.sum((mode_scale[None] * grow) * (bwd_sums + bwd_entry[None]), axis=1)
        + skip_gain[None, :] * grad_long
    )
    grad_stack = jnp.stack([grad_qshort, grad_gated * v_short, grad_gated * k_short])
    after = shift(grad_stack[:, : tap_count - 1, :], -1)
    extended_back = jnp.concatenate([grad_stack, after], axis=1)
    grads = jnp.zeros((3, tok_rows, chan_width), jnp.float32)
    for tap_index in range(tap_count):
        grads = (
            grads
            + short_taps[tap_index][:, None, :]
            * extended_back[:, tap_index : tap_index + tok_rows, :]
        )
    grads = grads.astype(jnp.bfloat16)
    return (mixed, grads[0], grads[1], grads[2])


def solution(mesh):
    in_specs = (
        P("seq", "ch"),
        P("seq", "ch"),
        P("seq", "ch"),
        P(None, None, "ch"),
        P(None, "ch"),
        P(None, "ch"),
        P("ch"),
        P("ch", "seq"),
        P("seq", "ch"),
    )
    out_specs = (P("seq", "ch"), P("seq", "ch"), P("seq", "ch"), P("seq", "ch"))
    return jax.shard_map(
        per_device, mesh=mesh, in_specs=in_specs, out_specs=out_specs, check_vma=False
    )
```

```python
import functools

import jax
import jax.numpy as jnp
from jax import lax
from jax.experimental import pallas as pl
from jax.experimental.pallas import tpu as pltpu
from jax.sharding import PartitionSpec as P

MESH = pl.DeviceIdType.MESH


def exchange_kernel(count, final_ref, out_ref, slots, send_sems, recv_sems):
    me = lax.axis_index("seq")
    lane = lax.axis_index("ch")
    barrier = pltpu.get_barrier_semaphore()
    for peer in range(count):

        @pl.when(me != peer)
        def _():
            pl.semaphore_signal(barrier, inc=1, device_id=(peer, lane), device_id_type=MESH)

    pl.semaphore_wait(barrier, count - 1)

    def link(peer, slot):
        return pltpu.make_async_remote_copy(
            src_ref=final_ref,
            dst_ref=slots.at[slot],
            send_sem=send_sems.at[peer],
            recv_sem=recv_sems.at[slot],
            device_id=(peer, lane),
            device_id_type=MESH,
        )

    for peer in range(count):

        @pl.when(me != peer)
        def _():
            link(peer, me).start()

    slots[me] = final_ref[...]
    for peer in range(count):

        @pl.when(me != peer)
        def _():
            link(peer, me).wait_send()
            link(peer, peer).wait_recv()

    out_ref[...] = slots[...]


def exchange(final, count):
    shape = (count,) + final.shape
    return pl.pallas_call(
        functools.partial(exchange_kernel, count),
        out_shape=jax.ShapeDtypeStruct(shape, final.dtype),
        in_specs=[pl.BlockSpec(memory_space=pltpu.VMEM)],
        out_specs=pl.BlockSpec(memory_space=pltpu.VMEM),
        scratch_shapes=[
            pltpu.VMEM(shape, final.dtype),
            pltpu.SemaphoreType.DMA((count,)),
            pltpu.SemaphoreType.DMA((count,)),
        ],
        compiler_params=pltpu.CompilerParams(collective_id=0, has_side_effects=True),
    )(final)


def from_behind(block, axis, distance):
    devices = range(lax.axis_size(axis))
    route = [(i - distance, i) for i in devices if i - distance in devices]
    return lax.ppermute(block, axis, route)


def per_device(query, key, value, short_taps, decay_rate, residue, skip_gain, out_weight, grad_out):
    tok_rows, chan_width = query.shape
    tap_count = short_taps.shape[0]
    mode_count = decay_rate.shape[0]
    highest = lax.Precision.HIGHEST
    count = lax.axis_size("seq")
    place = lax.axis_index("seq")

    core = place % 2
    half = count // 2
    groups = [[side + 2 * step for step in range(half)] for side in range(2)]
    mine = lax.all_gather(out_weight, "seq", axis_index_groups=groups)
    other = lax.ppermute(mine, "seq", [(i, i ^ 1) for i in range(count)])
    lanes = lax.axis_size("ch")
    grad_copies = jnp.broadcast_to(grad_out[None], (lanes,) + grad_out.shape)
    grad_blocks = lax.all_to_all(grad_copies, "ch", 0, 0, tiled=True)
    grad_split = jnp.transpose(grad_blocks, (1, 0, 2)).reshape(tok_rows, half, 2, chan_width)
    grad_mine = lax.dynamic_index_in_dim(grad_split, core, 2, False)
    grad_other = lax.dynamic_index_in_dim(grad_split, 1 - core, 2, False)

    streams = jnp.stack([query, key, value])
    before = from_behind(streams[:, tok_rows - (tap_count - 1) :, :], "seq", 1)
    extended = jnp.concatenate([before, streams], axis=1).astype(jnp.float32)
    featured = jnp.zeros((3, tok_rows, chan_width), jnp.float32)
    for tap_index in range(tap_count):
        begin = tap_count - 1 - tap_index
        featured = (
            featured + short_taps[tap_index][:, None, :] * extended[:, begin : begin + tok_rows, :]
        )
    q_short = featured[0]
    k_short = featured[1]
    v_short = featured[2]
    gated = k_short * v_short

    mode_scale = residue * jnp.sqrt(-jnp.expm1(-2.0 * decay_rate))
    offsets = jnp.arange(tok_rows).astype(jnp.float32)
    shrink = jnp.exp(-decay_rate[None, :, :] * offsets[:, None, None])
    grow = jnp.exp(decay_rate[None, :, :] * offsets[:, None, None])
    scaled_shrink = mode_scale[None] * shrink
    scaled_grow = mode_scale[None] * grow
    one_step = jnp.exp(-decay_rate)
    block_decay = jnp.exp(-decay_rate * tok_rows)
    rows = jnp.arange(tok_rows)
    lower = (rows[:, None] >= rows[None, :]).astype(jnp.float32)
    upper = (rows[:, None] <= rows[None, :]).astype(jnp.float32)

    def prefix(tri, weights, signal):
        spread = (weights * signal[:, None, :]).reshape(tok_rows, mode_count * chan_width)
        summed = jnp.dot(tri, spread, precision=highest, preferred_element_type=jnp.float32)
        return summed.reshape(tok_rows, mode_count, chan_width)

    fwd_sums = prefix(lower, grow, gated)
    fwd_final = shrink[tok_rows - 1] * fwd_sums[tok_rows - 1]

    grad_mixer = jnp.einsum(
        "tzc,zrc->tr", grad_mine, mine, preferred_element_type=jnp.float32
    ) + jnp.einsum("tzc,zrc->tr", grad_other, other, preferred_element_type=jnp.float32)
    grad_long = grad_mixer * q_short
    bwd_sums = prefix(upper, shrink, grad_long)
    bwd_final = bwd_sums[0]

    finals = jnp.stack([fwd_final, bwd_final])
    gathered = exchange(finals, count)
    source = jnp.arange(count)
    fwd_gap = place - 1 - source
    bwd_gap = source - place - 1

    def weights(gap):
        span = (tok_rows * jnp.maximum(gap, 0)).astype(jnp.float32)[:, None, None]
        return jnp.where((gap >= 0)[:, None, None], jnp.exp(-decay_rate[None] * span), 0.0)

    fwd_entry = jnp.sum(weights(fwd_gap) * gathered[:, 0], axis=0) * one_step
    bwd_entry = jnp.sum(weights(bwd_gap) * gathered[:, 1], axis=0) * block_decay

    long_out = (
        jnp.sum(scaled_shrink * (fwd_sums + fwd_entry[None]), axis=1) + skip_gain[None, :] * gated
    )
    mixer = (q_short * long_out).astype(jnp.bfloat16)
    part_mine = jnp.einsum("tr,zrc->ztc", mixer, mine, preferred_element_type=jnp.float32)
    part_other = jnp.einsum("tr,zrc->ztc", mixer, other, preferred_element_type=jnp.float32)
    part_mine = part_mine.astype(jnp.bfloat16)
    part_other = part_other.astype(jnp.bfloat16)
    parts = jnp.where(
        core == 0,
        jnp.stack([part_mine, part_other], axis=1),
        jnp.stack([part_other, part_mine], axis=1),
    ).reshape(count, tok_rows, chan_width)
    received = lax.all_to_all(parts, "ch", 0, 0, tiled=True)
    mixed = jnp.sum(received.astype(jnp.float32), axis=0).astype(jnp.bfloat16)

    grad_qshort = grad_mixer * long_out
    grad_gated = (
        jnp.sum(scaled_grow * (bwd_sums + bwd_entry[None]), axis=1) + skip_gain[None, :] * grad_long
    )
    grad_stack = jnp.stack([grad_qshort, grad_gated * v_short, grad_gated * k_short])
    after = from_behind(grad_stack[:, : tap_count - 1, :], "seq", -1)
    extended_back = jnp.concatenate([grad_stack, after], axis=1)
    grads = jnp.zeros((3, tok_rows, chan_width), jnp.float32)
    for tap_index in range(tap_count):
        grads = (
            grads
            + short_taps[tap_index][:, None, :]
            * extended_back[:, tap_index : tap_index + tok_rows, :]
        )
    grads = grads.astype(jnp.bfloat16)
    return (mixed, grads[0], grads[1], grads[2])


def solution(mesh):
    in_specs = (
        P("seq", "ch"),
        P("seq", "ch"),
        P("seq", "ch"),
        P(None, None, "ch"),
        P(None, "ch"),
        P(None, "ch"),
        P("ch"),
        P("ch", "seq"),
        P("seq", "ch"),
    )
    out_specs = (P("seq", "ch"), P("seq", "ch"), P("seq", "ch"), P("seq", "ch"))
    return jax.shard_map(
        per_device, mesh=mesh, in_specs=in_specs, out_specs=out_specs, check_vma=False
    )
```

```python
import functools

import jax
import jax.numpy as jnp
from jax import lax
from jax.experimental import pallas as pl
from jax.experimental.pallas import tpu as pltpu
from jax.sharding import PartitionSpec as P

MESH = pl.DeviceIdType.MESH


def exchange_kernel(count, final_ref, out_ref, slots, send_sems, recv_sems):
    me = lax.axis_index("seq")
    lane = lax.axis_index("ch")
    barrier = pltpu.get_barrier_semaphore()
    for peer in range(count):

        @pl.when(me != peer)
        def _():
            pl.semaphore_signal(barrier, inc=1, device_id=(peer, lane), device_id_type=MESH)

    pl.semaphore_wait(barrier, count - 1)

    def link(peer, slot):
        return pltpu.make_async_remote_copy(
            src_ref=final_ref,
            dst_ref=slots.at[slot],
            send_sem=send_sems.at[peer],
            recv_sem=recv_sems.at[slot],
            device_id=(peer, lane),
            device_id_type=MESH,
        )

    for peer in range(count):

        @pl.when(me != peer)
        def _():
            link(peer, me).start()

    slots[me] = final_ref[...]
    for peer in range(count):

        @pl.when(me != peer)
        def _():
            link(peer, me).wait_send()
            link(peer, peer).wait_recv()

    out_ref[...] = slots[...]


def exchange(final, count):
    shape = (count,) + final.shape
    return pl.pallas_call(
        functools.partial(exchange_kernel, count),
        out_shape=jax.ShapeDtypeStruct(shape, final.dtype),
        in_specs=[pl.BlockSpec(memory_space=pltpu.VMEM)],
        out_specs=pl.BlockSpec(memory_space=pltpu.VMEM),
        scratch_shapes=[
            pltpu.VMEM(shape, final.dtype),
            pltpu.SemaphoreType.DMA((count,)),
            pltpu.SemaphoreType.DMA((count,)),
        ],
        compiler_params=pltpu.CompilerParams(collective_id=0, has_side_effects=True),
    )(final)


def from_behind(block, axis, distance):
    devices = range(lax.axis_size(axis))
    route = [(i - distance, i) for i in devices if i - distance in devices]
    return lax.ppermute(block, axis, route)


def per_device(query, key, value, short_taps, decay_rate, residue, skip_gain, out_weight, grad_out):
    tok_rows, chan_width = query.shape
    tap_count = short_taps.shape[0]
    mode_count = decay_rate.shape[0]
    highest = lax.Precision.HIGHEST
    count = lax.axis_size("seq")
    place = lax.axis_index("seq")

    core = place % 2
    half = count // 2
    groups = [[side + 2 * step for step in range(half)] for side in range(2)]
    mine = lax.all_gather(out_weight, "seq", axis_index_groups=groups)
    other = lax.ppermute(mine, "seq", [(i, i ^ 1) for i in range(count)])
    lanes = lax.axis_size("ch")
    lane = lax.axis_index("ch")
    arrivals = [grad_out]
    for distance in range(1, lanes):
        route = [(k, (k + distance) % lanes) for k in range(lanes)]
        arrivals.append(lax.ppermute(grad_out, "ch", route))
    by_distance = jnp.stack(arrivals)
    order = (lane - jnp.arange(lanes)) % lanes
    grad_blocks = jnp.take(by_distance, order, axis=0)
    grad_split = jnp.transpose(grad_blocks, (1, 0, 2)).reshape(tok_rows, half, 2, chan_width)
    grad_mine = lax.dynamic_index_in_dim(grad_split, core, 2, False)
    grad_other = lax.dynamic_index_in_dim(grad_split, 1 - core, 2, False)

    streams = jnp.stack([query, key, value])
    before = from_behind(streams[:, tok_rows - (tap_count - 1) :, :], "seq", 1)
    extended = jnp.concatenate([before, streams], axis=1).astype(jnp.float32)
    featured = jnp.zeros((3, tok_rows, chan_width), jnp.float32)
    for tap_index in range(tap_count):
        begin = tap_count - 1 - tap_index
        featured = (
            featured + short_taps[tap_index][:, None, :] * extended[:, begin : begin + tok_rows, :]
        )
    q_short = featured[0]
    k_short = featured[1]
    v_short = featured[2]
    gated = k_short * v_short

    mode_scale = residue * jnp.sqrt(-jnp.expm1(-2.0 * decay_rate))
    offsets = jnp.arange(tok_rows).astype(jnp.float32)
    shrink = jnp.exp(-decay_rate[:, None, :] * offsets[None, :, None])
    grow = jnp.exp(decay_rate[:, None, :] * offsets[None, :, None])
    scaled_shrink = mode_scale[:, None, :] * shrink
    scaled_grow = mode_scale[:, None, :] * grow
    one_step = jnp.exp(-decay_rate)
    block_decay = jnp.exp(-decay_rate * tok_rows)
    rows = jnp.arange(tok_rows)
    lower = (rows[:, None] >= rows[None, :]).astype(jnp.float32)
    upper = (rows[:, None] <= rows[None, :]).astype(jnp.float32)

    def prefix(tri, weights, signal):
        spread = weights * signal[None, :, :]
        return jnp.einsum(
            "ts,nsc->ntc", tri, spread, precision=highest, preferred_element_type=jnp.float32
        )

    fwd_sums = prefix(lower, grow, gated)
    fwd_final = shrink[:, tok_rows - 1] * fwd_sums[:, tok_rows - 1]

    grad_mixer = jnp.einsum(
        "tzc,zrc->tr", grad_mine, mine, preferred_element_type=jnp.float32
    ) + jnp.einsum("tzc,zrc->tr", grad_other, other, preferred_element_type=jnp.float32)
    grad_long = grad_mixer * q_short
    bwd_sums = prefix(upper, shrink, grad_long)
    bwd_final = bwd_sums[:, 0]

    finals = jnp.stack([fwd_final, bwd_final])
    gathered = exchange(finals, count)
    source = jnp.arange(count)
    fwd_gap = place - 1 - source
    bwd_gap = source - place - 1

    def weights(gap):
        span = (tok_rows * jnp.maximum(gap, 0)).astype(jnp.float32)[:, None, None]
        return jnp.where((gap >= 0)[:, None, None], jnp.exp(-decay_rate[None] * span), 0.0)

    fwd_entry = jnp.sum(weights(fwd_gap) * gathered[:, 0], axis=0) * one_step
    bwd_entry = jnp.sum(weights(bwd_gap) * gathered[:, 1], axis=0) * block_decay

    long_out = (
        jnp.sum(scaled_shrink * (fwd_sums + fwd_entry[:, None, :]), axis=0) + skip_gain[None, :] * gated
    )
    mixer = (q_short * long_out).astype(jnp.bfloat16)
    part_mine = jnp.einsum("tr,zrc->ztc", mixer, mine, preferred_element_type=jnp.float32)
    part_other = jnp.einsum("tr,zrc->ztc", mixer, other, preferred_element_type=jnp.float32)
    part_mine = part_mine.astype(jnp.bfloat16)
    part_other = part_other.astype(jnp.bfloat16)
    parts = jnp.where(
        core == 0,
        jnp.stack([part_mine, part_other], axis=1),
        jnp.stack([part_other, part_mine], axis=1),
    ).reshape(count, tok_rows, chan_width)
    received = lax.all_to_all(parts, "ch", 0, 0, tiled=True)
    mixed = jnp.sum(received.astype(jnp.float32), axis=0).astype(jnp.bfloat16)

    grad_qshort = grad_mixer * long_out
    grad_gated = (
        jnp.sum(scaled_grow * (bwd_sums + bwd_entry[:, None, :]), axis=0) + skip_gain[None, :] * grad_long
    )
    grad_stack = jnp.stack([grad_qshort, grad_gated * v_short, grad_gated * k_short])
    after = from_behind(grad_stack[:, : tap_count - 1, :], "seq", -1)
    extended_back = jnp.concatenate([grad_stack, after], axis=1)
    grads = jnp.zeros((3, tok_rows, chan_width), jnp.float32)
    for tap_index in range(tap_count):
        grads = (
            grads
            + short_taps[tap_index][:, None, :]
            * extended_back[:, tap_index : tap_index + tok_rows, :]
        )
    grads = grads.astype(jnp.bfloat16)
    return (mixed, grads[0], grads[1], grads[2])


def solution(mesh):
    in_specs = (
        P("seq", "ch"),
        P("seq", "ch"),
        P("seq", "ch"),
        P(None, None, "ch"),
        P(None, "ch"),
        P(None, "ch"),
        P("ch"),
        P("ch", "seq"),
        P("seq", "ch"),
    )
    out_specs = (P("seq", "ch"), P("seq", "ch"), P("seq", "ch"), P("seq", "ch"))
    return jax.shard_map(
        per_device, mesh=mesh, in_specs=in_specs, out_specs=out_specs, check_vma=False
    )
```

```python
import functools

import jax
import jax.numpy as jnp
from jax import lax
from jax.experimental import pallas as pl
from jax.experimental.pallas import tpu as pltpu
from jax.sharding import PartitionSpec as P

MESH = pl.DeviceIdType.MESH


def exchange_kernel(count, final_ref, out_ref, slots, send_sems, recv_sems):
    me = lax.axis_index("seq")
    lane = lax.axis_index("ch")
    barrier = pltpu.get_barrier_semaphore()
    for peer in range(count):

        @pl.when(me != peer)
        def _():
            pl.semaphore_signal(barrier, inc=1, device_id=(peer, lane), device_id_type=MESH)

    pl.semaphore_wait(barrier, count - 1)

    def link(peer, slot):
        return pltpu.make_async_remote_copy(
            src_ref=final_ref,
            dst_ref=slots.at[slot],
            send_sem=send_sems.at[peer],
            recv_sem=recv_sems.at[slot],
            device_id=(peer, lane),
            device_id_type=MESH,
        )

    for peer in range(count):

        @pl.when(me != peer)
        def _():
            link(peer, me).start()

    slots[me] = final_ref[...]
    for peer in range(count):

        @pl.when(me != peer)
        def _():
            link(peer, me).wait_send()
            link(peer, peer).wait_recv()

    out_ref[...] = slots[...]


def exchange(final, count):
    shape = (count,) + final.shape
    return pl.pallas_call(
        functools.partial(exchange_kernel, count),
        out_shape=jax.ShapeDtypeStruct(shape, final.dtype),
        in_specs=[pl.BlockSpec(memory_space=pltpu.VMEM)],
        out_specs=pl.BlockSpec(memory_space=pltpu.VMEM),
        scratch_shapes=[
            pltpu.VMEM(shape, final.dtype),
            pltpu.SemaphoreType.DMA((count,)),
            pltpu.SemaphoreType.DMA((count,)),
        ],
        compiler_params=pltpu.CompilerParams(collective_id=0, has_side_effects=True),
    )(final)


def from_behind(block, axis, distance):
    devices = range(lax.axis_size(axis))
    route = [(i - distance, i) for i in devices if i - distance in devices]
    return lax.ppermute(block, axis, route)


def fetch_kernel(count, lanes, w_ref, g_ref, w_all, g_all, w_send, w_recv, g_send, g_recv, own_sem):
    me = lax.axis_index("seq")
    lane = lax.axis_index("ch")
    half = count // 2
    core = me % 2
    ring = me // 2
    right = 2 * ((ring + 1) % half) + core
    left = 2 * ((ring + half - 1) % half) + core
    partner = me + 1 - 2 * core
    right_steps = half // 2
    left_steps = half - 1 - right_steps

    barrier = pltpu.get_barrier_semaphore()
    for peer in (right, left, partner):
        pl.semaphore_signal(barrier, inc=1, device_id=(peer, lane), device_id_type=MESH)
    for other in range(lanes):

        @pl.when(lane != other)
        def _():
            pl.semaphore_signal(barrier, inc=1, device_id=(me, other), device_id_type=MESH)

    pl.semaphore_wait(barrier, 3 + lanes - 1)

    def grad_link(other):
        return pltpu.make_async_remote_copy(
            src_ref=g_ref,
            dst_ref=g_all.at[lane],
            send_sem=g_send.at[other],
            recv_sem=g_recv.at[lane],
            device_id=(me, other),
            device_id_type=MESH,
        )

    def grad_arrival(other):
        return pltpu.make_async_remote_copy(
            src_ref=g_ref,
            dst_ref=g_all.at[other],
            send_sem=g_send.at[other],
            recv_sem=g_recv.at[other],
            device_id=(me, other),
            device_id_type=MESH,
        )

    for other in range(lanes):

        @pl.when(lane != other)
        def _():
            grad_link(other).start()

    own_w = pltpu.make_async_copy(w_ref, w_all.at[me], own_sem.at[0])
    own_g = pltpu.make_async_copy(g_ref, g_all.at[lane], own_sem.at[1])
    own_w.start()
    own_g.start()

    sends = []

    def send(source, origin, peer):
        copy = pltpu.make_async_remote_copy(
            src_ref=source,
            dst_ref=w_all.at[origin],
            send_sem=w_send.at[len(sends)],
            recv_sem=w_recv.at[origin],
            device_id=(peer, lane),
            device_id_type=MESH,
        )
        copy.start()
        sends.append(copy)

    def arrived(origin):
        pltpu.make_async_remote_copy(
            src_ref=w_all.at[origin],
            dst_ref=w_all.at[origin],
            send_sem=w_send.at[0],
            recv_sem=w_recv.at[origin],
            device_id=(me, lane),
            device_id_type=MESH,
        ).wait_recv()

    def right_origin(step):
        return 2 * ((ring - step + 1 + half) % half) + core

    def left_origin(step):
        return 2 * ((ring + step - 1) % half) + core

    send(w_ref, me, partner)
    if right_steps >= 1:
        send(w_ref, me, right)
    if left_steps >= 1:
        send(w_ref, me, left)
    for step in range(2, max(right_steps, left_steps) + 2):
        if step <= right_steps + 1:
            origin = right_origin(step)
            arrived(origin)
            if step <= right_steps:
                send(w_all.at[origin], origin, right)
            send(w_all.at[origin], origin, partner)
        if step <= left_steps + 1:
            origin = left_origin(step)
            arrived(origin)
            if step <= left_steps:
                send(w_all.at[origin], origin, left)
            send(w_all.at[origin], origin, partner)

    for twin in range(half):
        arrived(2 * twin + 1 - core)
    for copy in sends:
        copy.wait_send()
    for other in range(lanes):

        @pl.when(lane != other)
        def _():
            grad_link(other).wait_send()
            grad_arrival(other).wait_recv()

    own_w.wait()
    own_g.wait()


def fetch(out_weight, grad_out, count, lanes):
    half = count // 2
    sends = half + half // 2 + (half - 1 - half // 2)
    return pl.pallas_call(
        functools.partial(fetch_kernel, count, lanes),
        out_shape=(
            jax.ShapeDtypeStruct((count,) + out_weight.shape, out_weight.dtype),
            jax.ShapeDtypeStruct((lanes,) + grad_out.shape, grad_out.dtype),
        ),
        in_specs=[pl.BlockSpec(memory_space=pl.ANY)] * 2,
        out_specs=(pl.BlockSpec(memory_space=pl.ANY), pl.BlockSpec(memory_space=pl.ANY)),
        scratch_shapes=[
            pltpu.SemaphoreType.DMA((sends,)),
            pltpu.SemaphoreType.DMA((count,)),
            pltpu.SemaphoreType.DMA((lanes,)),
            pltpu.SemaphoreType.DMA((lanes,)),
            pltpu.SemaphoreType.DMA((2,)),
        ],
        compiler_params=pltpu.CompilerParams(collective_id=1, has_side_effects=True),
    )(out_weight, grad_out)


def per_device(query, key, value, short_taps, decay_rate, residue, skip_gain, out_weight, grad_out):
    tok_rows, chan_width = query.shape
    tap_count = short_taps.shape[0]
    mode_count = decay_rate.shape[0]
    highest = lax.Precision.HIGHEST
    count = lax.axis_size("seq")
    place = lax.axis_index("seq")

    lanes = lax.axis_size("ch")
    w_all, g_all = fetch(out_weight, grad_out, count, lanes)

    streams = jnp.stack([query, key, value])
    before = from_behind(streams[:, tok_rows - (tap_count - 1) :, :], "seq", 1)
    extended = jnp.concatenate([before, streams], axis=1).astype(jnp.float32)
    featured = jnp.zeros((3, tok_rows, chan_width), jnp.float32)
    for tap_index in range(tap_count):
        begin = tap_count - 1 - tap_index
        featured = (
            featured + short_taps[tap_index][:, None, :] * extended[:, begin : begin + tok_rows, :]
        )
    q_short = featured[0]
    k_short = featured[1]
    v_short = featured[2]
    gated = k_short * v_short

    mode_scale = residue * jnp.sqrt(-jnp.expm1(-2.0 * decay_rate))
    offsets = jnp.arange(tok_rows).astype(jnp.float32)
    shrink = jnp.exp(-decay_rate[None, :, :] * offsets[:, None, None])
    grow = jnp.exp(decay_rate[None, :, :] * offsets[:, None, None])
    scaled_shrink = mode_scale[None] * shrink
    scaled_grow = mode_scale[None] * grow
    one_step = jnp.exp(-decay_rate)
    block_decay = jnp.exp(-decay_rate * tok_rows)
    rows = jnp.arange(tok_rows)
    lower = (rows[:, None] >= rows[None, :]).astype(jnp.float32)
    upper = (rows[:, None] <= rows[None, :]).astype(jnp.float32)

    def prefix(tri, weights, signal):
        spread = (weights * signal[:, None, :]).reshape(tok_rows, mode_count * chan_width)
        summed = jnp.dot(tri, spread, precision=highest, preferred_element_type=jnp.float32)
        return summed.reshape(tok_rows, mode_count, chan_width)

    fwd_sums = prefix(lower, grow, gated)
    fwd_final = shrink[tok_rows - 1] * fwd_sums[tok_rows - 1]

    grad_mixer = jnp.einsum("jtc,jrc->tr", g_all, w_all, preferred_element_type=jnp.float32)
    grad_long = grad_mixer * q_short
    bwd_sums = prefix(upper, shrink, grad_long)
    bwd_final = bwd_sums[0]

    finals = jnp.stack([fwd_final, bwd_final])
    gathered = exchange(finals, count)
    source = jnp.arange(count)
    fwd_gap = place - 1 - source
    bwd_gap = source - place - 1

    def weights(gap):
        span = (tok_rows * jnp.maximum(gap, 0)).astype(jnp.float32)[:, None, None]
        return jnp.where((gap >= 0)[:, None, None], jnp.exp(-decay_rate[None] * span), 0.0)

    fwd_entry = jnp.sum(weights(fwd_gap) * gathered[:, 0], axis=0) * one_step
    bwd_entry = jnp.sum(weights(bwd_gap) * gathered[:, 1], axis=0) * block_decay

    long_out = (
        jnp.sum(scaled_shrink * (fwd_sums + fwd_entry[None]), axis=1) + skip_gain[None, :] * gated
    )
    mixer = (q_short * long_out).astype(jnp.bfloat16)
    parts = jnp.einsum("tr,jrc->jtc", mixer, w_all, preferred_element_type=jnp.float32)
    parts = parts.astype(jnp.bfloat16)
    received = lax.all_to_all(parts, "ch", 0, 0, tiled=True)
    mixed = jnp.sum(received.astype(jnp.float32), axis=0).astype(jnp.bfloat16)

    grad_qshort = grad_mixer * long_out
    grad_gated = (
        jnp.sum(scaled_grow * (bwd_sums + bwd_entry[None]), axis=1) + skip_gain[None, :] * grad_long
    )
    grad_stack = jnp.stack([grad_qshort, grad_gated * v_short, grad_gated * k_short])
    after = from_behind(grad_stack[:, : tap_count - 1, :], "seq", -1)
    extended_back = jnp.concatenate([grad_stack, after], axis=1)
    grads = jnp.zeros((3, tok_rows, chan_width), jnp.float32)
    for tap_index in range(tap_count):
        grads = (
            grads
            + short_taps[tap_index][:, None, :]
            * extended_back[:, tap_index : tap_index + tok_rows, :]
        )
    grads = grads.astype(jnp.bfloat16)
    return (mixed, grads[0], grads[1], grads[2])


def solution(mesh):
    in_specs = (
        P("seq", "ch"),
        P("seq", "ch"),
        P("seq", "ch"),
        P(None, None, "ch"),
        P(None, "ch"),
        P(None, "ch"),
        P("ch"),
        P("ch", "seq"),
        P("seq", "ch"),
    )
    out_specs = (P("seq", "ch"), P("seq", "ch"), P("seq", "ch"), P("seq", "ch"))
    return jax.shard_map(
        per_device, mesh=mesh, in_specs=in_specs, out_specs=out_specs, check_vma=False
    )
```

```python
import functools

import jax
import jax.numpy as jnp
from jax import lax
from jax.experimental import pallas as pl
from jax.experimental.pallas import tpu as pltpu
from jax.sharding import PartitionSpec as P

MESH = pl.DeviceIdType.MESH


def exchange_kernel(count, final_ref, fwd_ref, bwd_ref, send_sems, recv_sems):
    me = lax.axis_index("seq")
    lane = lax.axis_index("ch")
    barrier = pltpu.get_barrier_semaphore()
    for peer in range(count):

        @pl.when(me != peer)
        def _():
            pl.semaphore_signal(barrier, inc=1, device_id=(peer, lane), device_id_type=MESH)

    pl.semaphore_wait(barrier, count - 1)

    def link(peer, later, slot):
        return pltpu.make_async_remote_copy(
            src_ref=final_ref.at[0 if later else 1],
            dst_ref=(fwd_ref if later else bwd_ref).at[slot],
            send_sem=send_sems.at[peer],
            recv_sem=recv_sems.at[slot],
            device_id=(peer, lane),
            device_id_type=MESH,
        )

    for peer in range(count):

        @pl.when(me < peer)
        def _():
            link(peer, True, me).start()

        @pl.when(me > peer)
        def _():
            link(peer, False, me).start()

    for peer in range(count):

        @pl.when(me < peer)
        def _():
            link(peer, True, me).wait_send()
            link(peer, False, peer).wait_recv()

        @pl.when(me > peer)
        def _():
            link(peer, False, me).wait_send()
            link(peer, True, peer).wait_recv()


def exchange(final, count):
    shape = (count,) + final.shape[1:]
    return pl.pallas_call(
        functools.partial(exchange_kernel, count),
        out_shape=(
            jax.ShapeDtypeStruct(shape, final.dtype),
            jax.ShapeDtypeStruct(shape, final.dtype),
        ),
        in_specs=[pl.BlockSpec(memory_space=pltpu.VMEM)],
        out_specs=(pl.BlockSpec(memory_space=pltpu.VMEM), pl.BlockSpec(memory_space=pltpu.VMEM)),
        scratch_shapes=[
            pltpu.SemaphoreType.DMA((count,)),
            pltpu.SemaphoreType.DMA((count,)),
        ],
        compiler_params=pltpu.CompilerParams(collective_id=0, has_side_effects=True),
    )(final)


def scatter_kernel(lanes, parts_ref, out_ref, send_sems, recv_sems, own_sem):
    me = lax.axis_index("seq")
    lane = lax.axis_index("ch")
    barrier = pltpu.get_barrier_semaphore()
    for other in range(lanes):

        @pl.when(lane != other)
        def _():
            pl.semaphore_signal(barrier, inc=1, device_id=(me, other), device_id_type=MESH)

    pl.semaphore_wait(barrier, lanes - 1)

    def link(other, slot):
        return pltpu.make_async_remote_copy(
            src_ref=parts_ref.at[other],
            dst_ref=out_ref.at[slot],
            send_sem=send_sems.at[other],
            recv_sem=recv_sems.at[slot],
            device_id=(me, other),
            device_id_type=MESH,
        )

    for other in range(lanes):

        @pl.when(lane != other)
        def _():
            link(other, lane).start()

    own = pltpu.make_async_copy(parts_ref.at[lane], out_ref.at[lane], own_sem.at[0])
    own.start()
    for other in range(lanes):

        @pl.when(lane != other)
        def _():
            link(other, lane).wait_send()
            link(other, other).wait_recv()

    own.wait()


def scatter(parts, lanes):
    return pl.pallas_call(
        functools.partial(scatter_kernel, lanes),
        out_shape=jax.ShapeDtypeStruct(parts.shape, parts.dtype),
        in_specs=[pl.BlockSpec(memory_space=pl.ANY)],
        out_specs=pl.BlockSpec(memory_space=pl.ANY),
        scratch_shapes=[
            pltpu.SemaphoreType.DMA((lanes,)),
            pltpu.SemaphoreType.DMA((lanes,)),
            pltpu.SemaphoreType.DMA((1,)),
        ],
        compiler_params=pltpu.CompilerParams(collective_id=2, has_side_effects=True),
    )(parts)


def from_behind(block, axis, distance):
    devices = range(lax.axis_size(axis))
    route = [(i - distance, i) for i in devices if i - distance in devices]
    return lax.ppermute(block, axis, route)


def fetch_kernel(count, lanes, w_ref, g_ref, w_all, g_all, w_send, w_recv, g_send, g_recv, own_sem):
    me = lax.axis_index("seq")
    lane = lax.axis_index("ch")
    half = count // 2
    core = me % 2
    ring = me // 2
    right = 2 * ((ring + 1) % half) + core
    left = 2 * ((ring + half - 1) % half) + core
    partner = me + 1 - 2 * core
    right_steps = half // 2
    left_steps = half - 1 - right_steps

    barrier = pltpu.get_barrier_semaphore()
    for peer in (right, left, partner):
        pl.semaphore_signal(barrier, inc=1, device_id=(peer, lane), device_id_type=MESH)
    for other in range(lanes):

        @pl.when(lane != other)
        def _():
            pl.semaphore_signal(barrier, inc=1, device_id=(me, other), device_id_type=MESH)

    pl.semaphore_wait(barrier, 3 + lanes - 1)

    def grad_link(other):
        return pltpu.make_async_remote_copy(
            src_ref=g_ref,
            dst_ref=g_all.at[lane],
            send_sem=g_send.at[other],
            recv_sem=g_recv.at[lane],
            device_id=(me, other),
            device_id_type=MESH,
        )

    def grad_arrival(other):
        return pltpu.make_async_remote_copy(
            src_ref=g_ref,
            dst_ref=g_all.at[other],
            send_sem=g_send.at[other],
            recv_sem=g_recv.at[other],
            device_id=(me, other),
            device_id_type=MESH,
        )

    for other in range(lanes):

        @pl.when(lane != other)
        def _():
            grad_link(other).start()

    own_w = pltpu.make_async_copy(w_ref, w_all.at[me], own_sem.at[0])
    own_g = pltpu.make_async_copy(g_ref, g_all.at[lane], own_sem.at[1])
    own_w.start()
    own_g.start()

    sends = []

    def send(source, origin, peer):
        copy = pltpu.make_async_remote_copy(
            src_ref=source,
            dst_ref=w_all.at[origin],
            send_sem=w_send.at[len(sends)],
            recv_sem=w_recv.at[origin],
            device_id=(peer, lane),
            device_id_type=MESH,
        )
        copy.start()
        sends.append(copy)

    def arrived(origin):
        pltpu.make_async_remote_copy(
            src_ref=w_all.at[origin],
            dst_ref=w_all.at[origin],
            send_sem=w_send.at[0],
            recv_sem=w_recv.at[origin],
            device_id=(me, lane),
            device_id_type=MESH,
        ).wait_recv()

    def right_origin(step):
        return 2 * ((ring - step + 1 + half) % half) + core

    def left_origin(step):
        return 2 * ((ring + step - 1) % half) + core

    send(w_ref, me, partner)
    if right_steps >= 1:
        send(w_ref, me, right)
    if left_steps >= 1:
        send(w_ref, me, left)
    for step in range(2, max(right_steps, left_steps) + 2):
        if step <= right_steps + 1:
            origin = right_origin(step)
            arrived(origin)
            if step <= right_steps:
                send(w_all.at[origin], origin, right)
            send(w_all.at[origin], origin, partner)
        if step <= left_steps + 1:
            origin = left_origin(step)
            arrived(origin)
            if step <= left_steps:
                send(w_all.at[origin], origin, left)
            send(w_all.at[origin], origin, partner)

    for twin in range(half):
        arrived(2 * twin + 1 - core)
    for copy in sends:
        copy.wait_send()
    for other in range(lanes):

        @pl.when(lane != other)
        def _():
            grad_link(other).wait_send()
            grad_arrival(other).wait_recv()

    own_w.wait()
    own_g.wait()


def fetch(out_weight, grad_out, count, lanes):
    half = count // 2
    sends = half + half // 2 + (half - 1 - half // 2)
    return pl.pallas_call(
        functools.partial(fetch_kernel, count, lanes),
        out_shape=(
            jax.ShapeDtypeStruct((count,) + out_weight.shape, out_weight.dtype),
            jax.ShapeDtypeStruct((lanes,) + grad_out.shape, grad_out.dtype),
        ),
        in_specs=[pl.BlockSpec(memory_space=pl.ANY)] * 2,
        out_specs=(pl.BlockSpec(memory_space=pl.ANY), pl.BlockSpec(memory_space=pl.ANY)),
        scratch_shapes=[
            pltpu.SemaphoreType.DMA((sends,)),
            pltpu.SemaphoreType.DMA((count,)),
            pltpu.SemaphoreType.DMA((lanes,)),
            pltpu.SemaphoreType.DMA((lanes,)),
            pltpu.SemaphoreType.DMA((2,)),
        ],
        compiler_params=pltpu.CompilerParams(collective_id=1, has_side_effects=True),
    )(out_weight, grad_out)


def per_device(query, key, value, short_taps, decay_rate, residue, skip_gain, out_weight, grad_out):
    tok_rows, chan_width = query.shape
    tap_count = short_taps.shape[0]
    mode_count = decay_rate.shape[0]
    highest = lax.Precision.HIGHEST
    count = lax.axis_size("seq")
    place = lax.axis_index("seq")

    lanes = lax.axis_size("ch")
    w_all, g_all = fetch(out_weight, grad_out, count, lanes)

    streams = jnp.stack([query, key, value])
    before = from_behind(streams[:, tok_rows - (tap_count - 1) :, :], "seq", 1)
    extended = jnp.concatenate([before, streams], axis=1).astype(jnp.float32)
    featured = jnp.zeros((3, tok_rows, chan_width), jnp.float32)
    for tap_index in range(tap_count):
        begin = tap_count - 1 - tap_index
        featured = (
            featured + short_taps[tap_index][:, None, :] * extended[:, begin : begin + tok_rows, :]
        )
    q_short = featured[0]
    k_short = featured[1]
    v_short = featured[2]
    gated = k_short * v_short

    mode_scale = residue * jnp.sqrt(-jnp.expm1(-2.0 * decay_rate))
    offsets = jnp.arange(tok_rows).astype(jnp.float32)
    shrink = jnp.exp(-decay_rate[None, :, :] * offsets[:, None, None])
    grow = jnp.exp(decay_rate[None, :, :] * offsets[:, None, None])
    scaled_shrink = mode_scale[None] * shrink
    scaled_grow = mode_scale[None] * grow
    one_step = jnp.exp(-decay_rate)
    block_decay = jnp.exp(-decay_rate * tok_rows)
    rows = jnp.arange(tok_rows)
    lower = (rows[:, None] >= rows[None, :]).astype(jnp.float32)
    upper = (rows[:, None] <= rows[None, :]).astype(jnp.float32)

    def prefix(tri, weights, signal):
        spread = (weights * signal[:, None, :]).reshape(tok_rows, mode_count * chan_width)
        summed = jnp.dot(tri, spread, precision=highest, preferred_element_type=jnp.float32)
        return summed.reshape(tok_rows, mode_count, chan_width)

    fwd_sums = prefix(lower, grow, gated)
    fwd_final = shrink[tok_rows - 1] * fwd_sums[tok_rows - 1]

    grad_mixer = jnp.einsum("jtc,jrc->tr", g_all, w_all, preferred_element_type=jnp.float32)
    grad_long = grad_mixer * q_short
    bwd_sums = prefix(upper, shrink, grad_long)
    bwd_final = bwd_sums[0]

    finals = jnp.stack([fwd_final, bwd_final]).astype(jnp.bfloat16)
    fwd_got, bwd_got = exchange(finals, count)
    source = jnp.arange(count)
    fwd_gap = place - 1 - source
    bwd_gap = source - place - 1

    def entry(gap, got):
        span = (tok_rows * jnp.maximum(gap, 0)).astype(jnp.float32)[:, None, None]
        held = jnp.where((gap >= 0)[:, None, None], got.astype(jnp.float32), 0.0)
        return jnp.sum(jnp.exp(-decay_rate[None] * span) * held, axis=0)

    fwd_entry = entry(fwd_gap, fwd_got) * one_step
    bwd_entry = entry(bwd_gap, bwd_got) * block_decay

    long_out = (
        jnp.sum(scaled_shrink * (fwd_sums + fwd_entry[None]), axis=1) + skip_gain[None, :] * gated
    )
    mixer = (q_short * long_out).astype(jnp.bfloat16)
    parts = jnp.einsum("tr,jrc->jtc", mixer, w_all, preferred_element_type=jnp.float32)
    parts = parts.astype(jnp.bfloat16)
    received = scatter(parts, lanes)
    mixed = jnp.sum(received.astype(jnp.float32), axis=0).astype(jnp.bfloat16)

    grad_qshort = grad_mixer * long_out
    grad_gated = (
        jnp.sum(scaled_grow * (bwd_sums + bwd_entry[None]), axis=1) + skip_gain[None, :] * grad_long
    )
    grad_stack = jnp.stack([grad_qshort, grad_gated * v_short, grad_gated * k_short])
    after = from_behind(grad_stack[:, : tap_count - 1, :], "seq", -1)
    extended_back = jnp.concatenate([grad_stack, after], axis=1)
    grads = jnp.zeros((3, tok_rows, chan_width), jnp.float32)
    for tap_index in range(tap_count):
        grads = (
            grads
            + short_taps[tap_index][:, None, :]
            * extended_back[:, tap_index : tap_index + tok_rows, :]
        )
    grads = grads.astype(jnp.bfloat16)
    return (mixed, grads[0], grads[1], grads[2])


def solution(mesh):
    in_specs = (
        P("seq", "ch"),
        P("seq", "ch"),
        P("seq", "ch"),
        P(None, None, "ch"),
        P(None, "ch"),
        P(None, "ch"),
        P("ch"),
        P("ch", "seq"),
        P("seq", "ch"),
    )
    out_specs = (P("seq", "ch"), P("seq", "ch"), P("seq", "ch"), P("seq", "ch"))
    return jax.shard_map(
        per_device, mesh=mesh, in_specs=in_specs, out_specs=out_specs, check_vma=False
    )
```

```python
import functools

import jax
import jax.numpy as jnp
from jax import lax
from jax.experimental import pallas as pl
from jax.experimental.pallas import tpu as pltpu
from jax.sharding import PartitionSpec as P

MESH = pl.DeviceIdType.MESH


def exchange_kernel(count, final_ref, fwd_ref, bwd_ref, send_sems, recv_sems):
    me = lax.axis_index("seq")
    lane = lax.axis_index("ch")
    barrier = pltpu.get_barrier_semaphore()
    for peer in range(count):

        @pl.when(me != peer)
        def _():
            pl.semaphore_signal(barrier, inc=1, device_id=(peer, lane), device_id_type=MESH)

    pl.semaphore_wait(barrier, count - 1)

    def link(peer, later, slot):
        return pltpu.make_async_remote_copy(
            src_ref=final_ref.at[0 if later else 1],
            dst_ref=(fwd_ref if later else bwd_ref).at[slot],
            send_sem=send_sems.at[peer],
            recv_sem=recv_sems.at[slot],
            device_id=(peer, lane),
            device_id_type=MESH,
        )

    for peer in range(count):

        @pl.when(me < peer)
        def _():
            link(peer, True, me).start()

        @pl.when(me > peer)
        def _():
            link(peer, False, me).start()

    for peer in range(count):

        @pl.when(me < peer)
        def _():
            link(peer, True, me).wait_send()
            link(peer, False, peer).wait_recv()

        @pl.when(me > peer)
        def _():
            link(peer, False, me).wait_send()
            link(peer, True, peer).wait_recv()


def exchange(final, count):
    shape = (count,) + final.shape[1:]
    return pl.pallas_call(
        functools.partial(exchange_kernel, count),
        out_shape=(
            jax.ShapeDtypeStruct(shape, final.dtype),
            jax.ShapeDtypeStruct(shape, final.dtype),
        ),
        in_specs=[pl.BlockSpec(memory_space=pltpu.VMEM)],
        out_specs=(pl.BlockSpec(memory_space=pltpu.VMEM), pl.BlockSpec(memory_space=pltpu.VMEM)),
        scratch_shapes=[
            pltpu.SemaphoreType.DMA((count,)),
            pltpu.SemaphoreType.DMA((count,)),
        ],
        compiler_params=pltpu.CompilerParams(collective_id=0, has_side_effects=True),
    )(final)


def scatter_kernel(lanes, parts_ref, out_ref, send_sems, recv_sems, own_sem):
    me = lax.axis_index("seq")
    lane = lax.axis_index("ch")
    barrier = pltpu.get_barrier_semaphore()
    for other in range(lanes):

        @pl.when(lane != other)
        def _():
            pl.semaphore_signal(barrier, inc=1, device_id=(me, other), device_id_type=MESH)

    pl.semaphore_wait(barrier, lanes - 1)

    def link(other, slot):
        return pltpu.make_async_remote_copy(
            src_ref=parts_ref.at[other],
            dst_ref=out_ref.at[slot],
            send_sem=send_sems.at[other],
            recv_sem=recv_sems.at[slot],
            device_id=(me, other),
            device_id_type=MESH,
        )

    for other in range(lanes):

        @pl.when(lane != other)
        def _():
            link(other, lane).start()

    own = pltpu.make_async_copy(parts_ref.at[lane], out_ref.at[lane], own_sem.at[0])
    own.start()
    for other in range(lanes):

        @pl.when(lane != other)
        def _():
            link(other, lane).wait_send()
            link(other, other).wait_recv()

    own.wait()


def scatter(parts, lanes):
    return pl.pallas_call(
        functools.partial(scatter_kernel, lanes),
        out_shape=jax.ShapeDtypeStruct(parts.shape, parts.dtype),
        in_specs=[pl.BlockSpec(memory_space=pl.ANY)],
        out_specs=pl.BlockSpec(memory_space=pl.ANY),
        scratch_shapes=[
            pltpu.SemaphoreType.DMA((lanes,)),
            pltpu.SemaphoreType.DMA((lanes,)),
            pltpu.SemaphoreType.DMA((1,)),
        ],
        compiler_params=pltpu.CompilerParams(collective_id=2, has_side_effects=True),
    )(parts)


def from_behind(block, axis, distance):
    devices = range(lax.axis_size(axis))
    route = [(i - distance, i) for i in devices if i - distance in devices]
    return lax.ppermute(block, axis, route)


def fetch_kernel(count, lanes, w_ref, g_ref, w_all, g_all, w_send, w_recv, g_send, g_recv, own_sem):
    me = lax.axis_index("seq")
    lane = lax.axis_index("ch")
    half = count // 2
    core = me % 2
    ring = me // 2
    right = 2 * ((ring + 1) % half) + core
    left = 2 * ((ring + half - 1) % half) + core
    partner = me + 1 - 2 * core
    right_steps = half // 2
    left_steps = half - 1 - right_steps

    barrier = pltpu.get_barrier_semaphore()
    for peer in (right, left, partner):
        pl.semaphore_signal(barrier, inc=1, device_id=(peer, lane), device_id_type=MESH)
    for other in range(lanes):

        @pl.when(lane != other)
        def _():
            pl.semaphore_signal(barrier, inc=1, device_id=(me, other), device_id_type=MESH)

    pl.semaphore_wait(barrier, 3 + lanes - 1)

    def grad_link(other):
        return pltpu.make_async_remote_copy(
            src_ref=g_ref,
            dst_ref=g_all.at[lane],
            send_sem=g_send.at[other],
            recv_sem=g_recv.at[lane],
            device_id=(me, other),
            device_id_type=MESH,
        )

    def grad_arrival(other):
        return pltpu.make_async_remote_copy(
            src_ref=g_ref,
            dst_ref=g_all.at[other],
            send_sem=g_send.at[other],
            recv_sem=g_recv.at[other],
            device_id=(me, other),
            device_id_type=MESH,
        )

    for other in range(lanes):

        @pl.when(lane != other)
        def _():
            grad_link(other).start()

    own_w = pltpu.make_async_copy(w_ref, w_all.at[me], own_sem.at[0])
    own_g = pltpu.make_async_copy(g_ref, g_all.at[lane], own_sem.at[1])
    own_w.start()
    own_g.start()

    sends = []

    def send(source, origin, peer):
        copy = pltpu.make_async_remote_copy(
            src_ref=source,
            dst_ref=w_all.at[origin],
            send_sem=w_send.at[len(sends)],
            recv_sem=w_recv.at[origin],
            device_id=(peer, lane),
            device_id_type=MESH,
        )
        copy.start()
        sends.append(copy)

    def arrived(origin):
        pltpu.make_async_remote_copy(
            src_ref=w_all.at[origin],
            dst_ref=w_all.at[origin],
            send_sem=w_send.at[0],
            recv_sem=w_recv.at[origin],
            device_id=(me, lane),
            device_id_type=MESH,
        ).wait_recv()

    def right_origin(step):
        return 2 * ((ring - step + 1 + half) % half) + core

    def left_origin(step):
        return 2 * ((ring + step - 1) % half) + core

    send(w_ref, me, partner)
    if right_steps >= 1:
        send(w_ref, me, right)
    if left_steps >= 1:
        send(w_ref, me, left)
    for step in range(2, max(right_steps, left_steps) + 2):
        if step <= right_steps + 1:
            origin = right_origin(step)
            arrived(origin)
            if step <= right_steps:
                send(w_all.at[origin], origin, right)
            send(w_all.at[origin], origin, partner)
        if step <= left_steps + 1:
            origin = left_origin(step)
            arrived(origin)
            if step <= left_steps:
                send(w_all.at[origin], origin, left)
            send(w_all.at[origin], origin, partner)

    for twin in range(half):
        arrived(2 * twin + 1 - core)
    for copy in sends:
        copy.wait_send()
    for other in range(lanes):

        @pl.when(lane != other)
        def _():
            grad_link(other).wait_send()
            grad_arrival(other).wait_recv()

    own_w.wait()
    own_g.wait()


def fetch(out_weight, grad_out, count, lanes):
    half = count // 2
    sends = half + half // 2 + (half - 1 - half // 2)
    return pl.pallas_call(
        functools.partial(fetch_kernel, count, lanes),
        out_shape=(
            jax.ShapeDtypeStruct((count,) + out_weight.shape, out_weight.dtype),
            jax.ShapeDtypeStruct((lanes,) + grad_out.shape, grad_out.dtype),
        ),
        in_specs=[pl.BlockSpec(memory_space=pl.ANY)] * 2,
        out_specs=(pl.BlockSpec(memory_space=pl.ANY), pl.BlockSpec(memory_space=pl.ANY)),
        scratch_shapes=[
            pltpu.SemaphoreType.DMA((sends,)),
            pltpu.SemaphoreType.DMA((count,)),
            pltpu.SemaphoreType.DMA((lanes,)),
            pltpu.SemaphoreType.DMA((lanes,)),
            pltpu.SemaphoreType.DMA((2,)),
        ],
        compiler_params=pltpu.CompilerParams(collective_id=1, has_side_effects=True),
    )(out_weight, grad_out)


def per_device(query, key, value, short_taps, decay_rate, residue, skip_gain, out_weight, grad_out):
    tok_rows, chan_width = query.shape
    tap_count = short_taps.shape[0]
    mode_count = decay_rate.shape[0]
    highest = lax.Precision.HIGHEST
    count = lax.axis_size("seq")
    place = lax.axis_index("seq")

    lanes = lax.axis_size("ch")
    w_all, g_all = fetch(out_weight, grad_out, count, lanes)

    streams = jnp.stack([query, key, value])
    before = from_behind(streams[:, tok_rows - (tap_count - 1) :, :], "seq", 1)
    extended = jnp.concatenate([before, streams], axis=1).astype(jnp.float32)
    featured = jnp.zeros((3, tok_rows, chan_width), jnp.float32)
    for tap_index in range(tap_count):
        begin = tap_count - 1 - tap_index
        featured = (
            featured + short_taps[tap_index][:, None, :] * extended[:, begin : begin + tok_rows, :]
        )
    q_short = featured[0]
    k_short = featured[1]
    v_short = featured[2]
    gated = k_short * v_short

    mode_scale = residue * jnp.sqrt(-jnp.expm1(-2.0 * decay_rate))
    offsets = jnp.arange(tok_rows).astype(jnp.float32)
    shrink = jnp.exp(-decay_rate[None, :, :] * offsets[:, None, None])
    grow = jnp.exp(decay_rate[None, :, :] * offsets[:, None, None])
    scaled_shrink = mode_scale[None] * shrink
    scaled_grow = mode_scale[None] * grow
    one_step = jnp.exp(-decay_rate)
    block_decay = jnp.exp(-decay_rate * tok_rows)
    rows = jnp.arange(tok_rows)
    lower = (rows[:, None] >= rows[None, :]).astype(jnp.float32)
    upper = (rows[:, None] <= rows[None, :]).astype(jnp.float32)

    def prefix(tri, weights, signal):
        spread = (weights * signal[:, None, :]).reshape(tok_rows, mode_count * chan_width)
        summed = jnp.dot(tri, spread, precision=highest, preferred_element_type=jnp.float32)
        return summed.reshape(tok_rows, mode_count, chan_width)

    fwd_sums = prefix(lower, grow, gated)
    fwd_final = shrink[tok_rows - 1] * fwd_sums[tok_rows - 1]

    grad_mixer = jnp.einsum("jtc,jrc->tr", g_all, w_all, preferred_element_type=jnp.float32)
    grad_long = grad_mixer * q_short
    bwd_sums = prefix(upper, shrink, grad_long)
    bwd_final = bwd_sums[0]

    finals = jnp.stack([fwd_final, bwd_final]).astype(jnp.bfloat16)
    fwd_got, bwd_got = exchange(finals, count)
    source = jnp.arange(count)
    fwd_gap = place - 1 - source
    bwd_gap = source - place - 1

    def entry(gap, got):
        span = (tok_rows * jnp.maximum(gap, 0)).astype(jnp.float32)[:, None, None]
        held = jnp.where((gap >= 0)[:, None, None], got.astype(jnp.float32), 0.0)
        return jnp.sum(jnp.exp(-decay_rate[None] * span) * held, axis=0)

    fwd_entry = entry(fwd_gap, fwd_got) * one_step
    bwd_entry = entry(bwd_gap, bwd_got) * block_decay

    long_out = (
        jnp.sum(scaled_shrink * (fwd_sums + fwd_entry[None]), axis=1) + skip_gain[None, :] * gated
    )
    mixer = (q_short * long_out).astype(jnp.bfloat16)
    parts = jnp.einsum("tr,jrc->jtc", mixer, w_all, preferred_element_type=jnp.float32)
    parts = parts.astype(jnp.bfloat16)
    received = lax.all_to_all(parts, "ch", 0, 0, tiled=True)
    mixed = jnp.sum(received.astype(jnp.float32), axis=0).astype(jnp.bfloat16)

    grad_qshort = grad_mixer * long_out
    grad_gated = (
        jnp.sum(scaled_grow * (bwd_sums + bwd_entry[None]), axis=1) + skip_gain[None, :] * grad_long
    )
    grad_stack = jnp.stack([grad_qshort, grad_gated * v_short, grad_gated * k_short])
    after = from_behind(grad_stack[:, : tap_count - 1, :], "seq", -1)
    extended_back = jnp.concatenate([grad_stack, after], axis=1)
    grads = jnp.zeros((3, tok_rows, chan_width), jnp.float32)
    for tap_index in range(tap_count):
        grads = (
            grads
            + short_taps[tap_index][:, None, :]
            * extended_back[:, tap_index : tap_index + tok_rows, :]
        )
    grads = grads.astype(jnp.bfloat16)
    return (mixed, grads[0], grads[1], grads[2])


def solution(mesh):
    in_specs = (
        P("seq", "ch"),
        P("seq", "ch"),
        P("seq", "ch"),
        P(None, None, "ch"),
        P(None, "ch"),
        P(None, "ch"),
        P("ch"),
        P("ch", "seq"),
        P("seq", "ch"),
    )
    out_specs = (P("seq", "ch"), P("seq", "ch"), P("seq", "ch"), P("seq", "ch"))
    return jax.shard_map(
        per_device, mesh=mesh, in_specs=in_specs, out_specs=out_specs, check_vma=False
    )
```

```python
import functools

import jax
import jax.numpy as jnp
from jax import lax
from jax.experimental import pallas as pl
from jax.experimental.pallas import tpu as pltpu
from jax.sharding import PartitionSpec as P

MESH = pl.DeviceIdType.MESH


def exchange_kernel(count, later, final_ref, got_ref, send_sems, recv_sems):
    me = lax.axis_index("seq")
    lane = lax.axis_index("ch")
    barrier = pltpu.get_barrier_semaphore()
    for peer in range(count):

        @pl.when(me != peer)
        def _():
            pl.semaphore_signal(barrier, inc=1, device_id=(peer, lane), device_id_type=MESH)

    pl.semaphore_wait(barrier, count - 1)

    def link(peer, slot):
        return pltpu.make_async_remote_copy(
            src_ref=final_ref,
            dst_ref=got_ref.at[slot],
            send_sem=send_sems.at[peer],
            recv_sem=recv_sems.at[slot],
            device_id=(peer, lane),
            device_id_type=MESH,
        )

    def sends_to(peer):
        return me < peer if later else me > peer

    def hears_from(peer):
        return me > peer if later else me < peer

    for peer in range(count):

        @pl.when(sends_to(peer))
        def _():
            link(peer, me).start()

    for peer in range(count):

        @pl.when(sends_to(peer))
        def _():
            link(peer, me).wait_send()

        @pl.when(hears_from(peer))
        def _():
            link(peer, peer).wait_recv()


def exchange(final, count, later, collective):
    shape = (count,) + final.shape
    return pl.pallas_call(
        functools.partial(exchange_kernel, count, later),
        out_shape=jax.ShapeDtypeStruct(shape, final.dtype),
        in_specs=[pl.BlockSpec(memory_space=pltpu.VMEM)],
        out_specs=pl.BlockSpec(memory_space=pltpu.VMEM),
        scratch_shapes=[
            pltpu.SemaphoreType.DMA((count,)),
            pltpu.SemaphoreType.DMA((count,)),
        ],
        compiler_params=pltpu.CompilerParams(collective_id=collective, has_side_effects=True),
    )(final)


def from_behind(block, axis, distance):
    devices = range(lax.axis_size(axis))
    route = [(i - distance, i) for i in devices if i - distance in devices]
    return lax.ppermute(block, axis, route)


def fetch_kernel(count, lanes, w_ref, g_ref, w_all, g_all, w_send, w_recv, g_send, g_recv, own_sem):
    me = lax.axis_index("seq")
    lane = lax.axis_index("ch")
    half = count // 2
    core = me % 2
    ring = me // 2
    right = 2 * ((ring + 1) % half) + core
    left = 2 * ((ring + half - 1) % half) + core
    partner = me + 1 - 2 * core
    right_steps = half // 2
    left_steps = half - 1 - right_steps

    barrier = pltpu.get_barrier_semaphore()
    for peer in (right, left, partner):
        pl.semaphore_signal(barrier, inc=1, device_id=(peer, lane), device_id_type=MESH)
    for other in range(lanes):

        @pl.when(lane != other)
        def _():
            pl.semaphore_signal(barrier, inc=1, device_id=(me, other), device_id_type=MESH)

    pl.semaphore_wait(barrier, 3 + lanes - 1)

    def grad_link(other):
        return pltpu.make_async_remote_copy(
            src_ref=g_ref,
            dst_ref=g_all.at[lane],
            send_sem=g_send.at[other],
            recv_sem=g_recv.at[lane],
            device_id=(me, other),
            device_id_type=MESH,
        )

    def grad_arrival(other):
        return pltpu.make_async_remote_copy(
            src_ref=g_ref,
            dst_ref=g_all.at[other],
            send_sem=g_send.at[other],
            recv_sem=g_recv.at[other],
            device_id=(me, other),
            device_id_type=MESH,
        )

    for other in range(lanes):

        @pl.when(lane != other)
        def _():
            grad_link(other).start()

    own_w = pltpu.make_async_copy(w_ref, w_all.at[me], own_sem.at[0])
    own_g = pltpu.make_async_copy(g_ref, g_all.at[lane], own_sem.at[1])
    own_w.start()
    own_g.start()

    sends = []

    def send(source, origin, peer):
        copy = pltpu.make_async_remote_copy(
            src_ref=source,
            dst_ref=w_all.at[origin],
            send_sem=w_send.at[len(sends)],
            recv_sem=w_recv.at[origin],
            device_id=(peer, lane),
            device_id_type=MESH,
        )
        copy.start()
        sends.append(copy)

    def arrived(origin):
        pltpu.make_async_remote_copy(
            src_ref=w_all.at[origin],
            dst_ref=w_all.at[origin],
            send_sem=w_send.at[0],
            recv_sem=w_recv.at[origin],
            device_id=(me, lane),
            device_id_type=MESH,
        ).wait_recv()

    def right_origin(step):
        return 2 * ((ring - step + 1 + half) % half) + core

    def left_origin(step):
        return 2 * ((ring + step - 1) % half) + core

    send(w_ref, me, partner)
    if right_steps >= 1:
        send(w_ref, me, right)
    if left_steps >= 1:
        send(w_ref, me, left)
    for step in range(2, max(right_steps, left_steps) + 2):
        if step <= right_steps + 1:
            origin = right_origin(step)
            arrived(origin)
            if step <= right_steps:
                send(w_all.at[origin], origin, right)
            send(w_all.at[origin], origin, partner)
        if step <= left_steps + 1:
            origin = left_origin(step)
            arrived(origin)
            if step <= left_steps:
                send(w_all.at[origin], origin, left)
            send(w_all.at[origin], origin, partner)

    for twin in range(half):
        arrived(2 * twin + 1 - core)
    for copy in sends:
        copy.wait_send()
    for other in range(lanes):

        @pl.when(lane != other)
        def _():
            grad_link(other).wait_send()
            grad_arrival(other).wait_recv()

    own_w.wait()
    own_g.wait()


def fetch(out_weight, grad_out, count, lanes):
    half = count // 2
    sends = half + half // 2 + (half - 1 - half // 2)
    return pl.pallas_call(
        functools.partial(fetch_kernel, count, lanes),
        out_shape=(
            jax.ShapeDtypeStruct((count,) + out_weight.shape, out_weight.dtype),
            jax.ShapeDtypeStruct((lanes,) + grad_out.shape, grad_out.dtype),
        ),
        in_specs=[pl.BlockSpec(memory_space=pl.ANY)] * 2,
        out_specs=(pl.BlockSpec(memory_space=pl.ANY), pl.BlockSpec(memory_space=pl.ANY)),
        scratch_shapes=[
            pltpu.SemaphoreType.DMA((sends,)),
            pltpu.SemaphoreType.DMA((count,)),
            pltpu.SemaphoreType.DMA((lanes,)),
            pltpu.SemaphoreType.DMA((lanes,)),
            pltpu.SemaphoreType.DMA((2,)),
        ],
        compiler_params=pltpu.CompilerParams(collective_id=1, has_side_effects=True),
    )(out_weight, grad_out)


def per_device(query, key, value, short_taps, decay_rate, residue, skip_gain, out_weight, grad_out):
    tok_rows, chan_width = query.shape
    tap_count = short_taps.shape[0]
    mode_count = decay_rate.shape[0]
    highest = lax.Precision.HIGHEST
    count = lax.axis_size("seq")
    place = lax.axis_index("seq")

    lanes = lax.axis_size("ch")
    w_all, g_all = fetch(out_weight, grad_out, count, lanes)

    streams = jnp.stack([query, key, value])
    before = from_behind(streams[:, tok_rows - (tap_count - 1) :, :], "seq", 1)
    extended = jnp.concatenate([before, streams], axis=1).astype(jnp.float32)
    featured = jnp.zeros((3, tok_rows, chan_width), jnp.float32)
    for tap_index in range(tap_count):
        begin = tap_count - 1 - tap_index
        featured = (
            featured + short_taps[tap_index][:, None, :] * extended[:, begin : begin + tok_rows, :]
        )
    q_short = featured[0]
    k_short = featured[1]
    v_short = featured[2]
    gated = k_short * v_short

    mode_scale = residue * jnp.sqrt(-jnp.expm1(-2.0 * decay_rate))
    offsets = jnp.arange(tok_rows).astype(jnp.float32)
    shrink = jnp.exp(-decay_rate[None, :, :] * offsets[:, None, None])
    grow = jnp.exp(decay_rate[None, :, :] * offsets[:, None, None])
    scaled_shrink = mode_scale[None] * shrink
    scaled_grow = mode_scale[None] * grow
    one_step = jnp.exp(-decay_rate)
    block_decay = jnp.exp(-decay_rate * tok_rows)
    rows = jnp.arange(tok_rows)
    lower = (rows[:, None] >= rows[None, :]).astype(jnp.float32)
    upper = (rows[:, None] <= rows[None, :]).astype(jnp.float32)

    def prefix(tri, weights, signal):
        spread = (weights * signal[:, None, :]).reshape(tok_rows, mode_count * chan_width)
        summed = jnp.dot(tri, spread, precision=highest, preferred_element_type=jnp.float32)
        return summed.reshape(tok_rows, mode_count, chan_width)

    source = jnp.arange(count)

    def entry(gap, got):
        span = (tok_rows * jnp.maximum(gap, 0)).astype(jnp.float32)[:, None, None]
        held = jnp.where((gap >= 0)[:, None, None], got.astype(jnp.float32), 0.0)
        return jnp.sum(jnp.exp(-decay_rate[None] * span) * held, axis=0)

    fwd_sums = prefix(lower, grow, gated)
    fwd_final = (shrink[tok_rows - 1] * fwd_sums[tok_rows - 1]).astype(jnp.bfloat16)
    fwd_got = exchange(fwd_final, count, True, 0)
    fwd_entry = entry(place - 1 - source, fwd_got) * one_step
    long_out = (
        jnp.sum(scaled_shrink * (fwd_sums + fwd_entry[None]), axis=1) + skip_gain[None, :] * gated
    )
    mixer = (q_short * long_out).astype(jnp.bfloat16)
    parts = jnp.einsum("tr,jrc->jtc", mixer, w_all, preferred_element_type=jnp.float32)
    parts = parts.astype(jnp.bfloat16)
    parts, g_all, w_all = lax.optimization_barrier((parts, g_all, w_all))
    received = lax.all_to_all(parts, "ch", 0, 0, tiled=True)
    mixed = jnp.sum(received.astype(jnp.float32), axis=0).astype(jnp.bfloat16)

    grad_mixer = jnp.einsum("jtc,jrc->tr", g_all, w_all, preferred_element_type=jnp.float32)
    grad_long = grad_mixer * q_short
    bwd_sums = prefix(upper, shrink, grad_long)
    bwd_got = exchange(bwd_sums[0].astype(jnp.bfloat16), count, False, 3)
    bwd_entry = entry(source - place - 1, bwd_got) * block_decay

    grad_qshort = grad_mixer * long_out
    grad_gated = (
        jnp.sum(scaled_grow * (bwd_sums + bwd_entry[None]), axis=1) + skip_gain[None, :] * grad_long
    )
    grad_stack = jnp.stack([grad_qshort, grad_gated * v_short, grad_gated * k_short])
    after = from_behind(grad_stack[:, : tap_count - 1, :], "seq", -1)
    extended_back = jnp.concatenate([grad_stack, after], axis=1)
    grads = jnp.zeros((3, tok_rows, chan_width), jnp.float32)
    for tap_index in range(tap_count):
        grads = (
            grads
            + short_taps[tap_index][:, None, :]
            * extended_back[:, tap_index : tap_index + tok_rows, :]
        )
    grads = grads.astype(jnp.bfloat16)
    return (mixed, grads[0], grads[1], grads[2])


def solution(mesh):
    in_specs = (
        P("seq", "ch"),
        P("seq", "ch"),
        P("seq", "ch"),
        P(None, None, "ch"),
        P(None, "ch"),
        P(None, "ch"),
        P("ch"),
        P("ch", "seq"),
        P("seq", "ch"),
    )
    out_specs = (P("seq", "ch"), P("seq", "ch"), P("seq", "ch"), P("seq", "ch"))
    return jax.shard_map(
        per_device, mesh=mesh, in_specs=in_specs, out_specs=out_specs, check_vma=False
    )
```

```python
import functools

import jax
import jax.numpy as jnp
from jax import lax
from jax.experimental import pallas as pl
from jax.experimental.pallas import tpu as pltpu
from jax.sharding import PartitionSpec as P

MESH = pl.DeviceIdType.MESH


def exchange_kernel(count, later, final_ref, got_ref, send_sems, recv_sems):
    me = lax.axis_index("seq")
    lane = lax.axis_index("ch")
    barrier = pltpu.get_barrier_semaphore()
    for peer in range(count):

        @pl.when(me != peer)
        def _():
            pl.semaphore_signal(barrier, inc=1, device_id=(peer, lane), device_id_type=MESH)

    pl.semaphore_wait(barrier, count - 1)

    def link(peer, slot):
        return pltpu.make_async_remote_copy(
            src_ref=final_ref,
            dst_ref=got_ref.at[slot],
            send_sem=send_sems.at[peer],
            recv_sem=recv_sems.at[slot],
            device_id=(peer, lane),
            device_id_type=MESH,
        )

    def sends_to(peer):
        return me < peer if later else me > peer

    def hears_from(peer):
        return me > peer if later else me < peer

    for peer in range(count):

        @pl.when(sends_to(peer))
        def _():
            link(peer, me).start()

    for peer in range(count):

        @pl.when(sends_to(peer))
        def _():
            link(peer, me).wait_send()

        @pl.when(hears_from(peer))
        def _():
            link(peer, peer).wait_recv()


def exchange(final, count, later, collective):
    shape = (count,) + final.shape
    return pl.pallas_call(
        functools.partial(exchange_kernel, count, later),
        out_shape=jax.ShapeDtypeStruct(shape, final.dtype),
        in_specs=[pl.BlockSpec(memory_space=pltpu.VMEM)],
        out_specs=pl.BlockSpec(memory_space=pltpu.VMEM),
        scratch_shapes=[
            pltpu.SemaphoreType.DMA((count,)),
            pltpu.SemaphoreType.DMA((count,)),
        ],
        compiler_params=pltpu.CompilerParams(collective_id=collective, has_side_effects=True),
    )(final)


def from_behind(block, axis, distance):
    devices = range(lax.axis_size(axis))
    route = [(i - distance, i) for i in devices if i - distance in devices]
    return lax.ppermute(block, axis, route)


def fetch_kernel(count, lanes, w_ref, g_ref, w_all, g_all, w_send, w_recv, g_send, g_recv, own_sem):
    me = lax.axis_index("seq")
    lane = lax.axis_index("ch")
    half = count // 2
    core = me % 2
    ring = me // 2
    right = 2 * ((ring + 1) % half) + core
    left = 2 * ((ring + half - 1) % half) + core
    partner = me + 1 - 2 * core
    right_steps = half // 2
    left_steps = half - 1 - right_steps

    barrier = pltpu.get_barrier_semaphore()
    for peer in (right, left, partner):
        pl.semaphore_signal(barrier, inc=1, device_id=(peer, lane), device_id_type=MESH)
    for other in range(lanes):

        @pl.when(lane != other)
        def _():
            pl.semaphore_signal(barrier, inc=1, device_id=(me, other), device_id_type=MESH)

    pl.semaphore_wait(barrier, 3 + lanes - 1)

    def grad_link(other):
        return pltpu.make_async_remote_copy(
            src_ref=g_ref,
            dst_ref=g_all.at[lane],
            send_sem=g_send.at[other],
            recv_sem=g_recv.at[lane],
            device_id=(me, other),
            device_id_type=MESH,
        )

    def grad_arrival(other):
        return pltpu.make_async_remote_copy(
            src_ref=g_ref,
            dst_ref=g_all.at[other],
            send_sem=g_send.at[other],
            recv_sem=g_recv.at[other],
            device_id=(me, other),
            device_id_type=MESH,
        )

    for other in range(lanes):

        @pl.when(lane != other)
        def _():
            grad_link(other).start()

    own_w = pltpu.make_async_copy(w_ref, w_all.at[me], own_sem.at[0])
    own_g = pltpu.make_async_copy(g_ref, g_all.at[lane], own_sem.at[1])
    own_w.start()
    own_g.start()

    sends = []

    def send(source, origin, peer):
        copy = pltpu.make_async_remote_copy(
            src_ref=source,
            dst_ref=w_all.at[origin],
            send_sem=w_send.at[len(sends)],
            recv_sem=w_recv.at[origin],
            device_id=(peer, lane),
            device_id_type=MESH,
        )
        copy.start()
        sends.append(copy)

    def arrived(origin):
        pltpu.make_async_remote_copy(
            src_ref=w_all.at[origin],
            dst_ref=w_all.at[origin],
            send_sem=w_send.at[0],
            recv_sem=w_recv.at[origin],
            device_id=(me, lane),
            device_id_type=MESH,
        ).wait_recv()

    def right_origin(step):
        return 2 * ((ring - step + 1 + half) % half) + core

    def left_origin(step):
        return 2 * ((ring + step - 1) % half) + core

    send(w_ref, me, partner)
    if right_steps >= 1:
        send(w_ref, me, right)
    if left_steps >= 1:
        send(w_ref, me, left)
    for step in range(2, max(right_steps, left_steps) + 2):
        if step <= right_steps + 1:
            origin = right_origin(step)
            arrived(origin)
            if step <= right_steps:
                send(w_all.at[origin], origin, right)
            send(w_all.at[origin], origin, partner)
        if step <= left_steps + 1:
            origin = left_origin(step)
            arrived(origin)
            if step <= left_steps:
                send(w_all.at[origin], origin, left)
            send(w_all.at[origin], origin, partner)

    for twin in range(half):
        arrived(2 * twin + 1 - core)
    for copy in sends:
        copy.wait_send()
    for other in range(lanes):

        @pl.when(lane != other)
        def _():
            grad_link(other).wait_send()
            grad_arrival(other).wait_recv()

    own_w.wait()
    own_g.wait()


def fetch(out_weight, grad_out, count, lanes):
    half = count // 2
    sends = half + half // 2 + (half - 1 - half // 2)
    return pl.pallas_call(
        functools.partial(fetch_kernel, count, lanes),
        out_shape=(
            jax.ShapeDtypeStruct((count,) + out_weight.shape, out_weight.dtype),
            jax.ShapeDtypeStruct((lanes,) + grad_out.shape, grad_out.dtype),
        ),
        in_specs=[pl.BlockSpec(memory_space=pl.ANY)] * 2,
        out_specs=(pl.BlockSpec(memory_space=pl.ANY), pl.BlockSpec(memory_space=pl.ANY)),
        scratch_shapes=[
            pltpu.SemaphoreType.DMA((sends,)),
            pltpu.SemaphoreType.DMA((count,)),
            pltpu.SemaphoreType.DMA((lanes,)),
            pltpu.SemaphoreType.DMA((lanes,)),
            pltpu.SemaphoreType.DMA((2,)),
        ],
        compiler_params=pltpu.CompilerParams(collective_id=1, has_side_effects=True),
    )(out_weight, grad_out)


def per_device(query, key, value, short_taps, decay_rate, residue, skip_gain, out_weight, grad_out):
    tok_rows, chan_width = query.shape
    tap_count = short_taps.shape[0]
    mode_count = decay_rate.shape[0]
    highest = lax.Precision.HIGHEST
    count = lax.axis_size("seq")
    place = lax.axis_index("seq")

    lanes = lax.axis_size("ch")
    w_all, g_all = fetch(out_weight, grad_out, count, lanes)

    streams = jnp.stack([query, key, value])
    before = from_behind(streams[:, tok_rows - (tap_count - 1) :, :], "seq", 1)
    extended = jnp.concatenate([before, streams], axis=1).astype(jnp.float32)
    featured = jnp.zeros((3, tok_rows, chan_width), jnp.float32)
    for tap_index in range(tap_count):
        begin = tap_count - 1 - tap_index
        featured = (
            featured + short_taps[tap_index][:, None, :] * extended[:, begin : begin + tok_rows, :]
        )
    q_short = featured[0]
    k_short = featured[1]
    v_short = featured[2]
    gated = k_short * v_short

    width = mode_count * chan_width
    rate = decay_rate.reshape(1, width)
    mode_scale = (residue * jnp.sqrt(-jnp.expm1(-2.0 * decay_rate))).reshape(1, width)
    offsets = jnp.arange(tok_rows).astype(jnp.float32)[:, None]
    shrink = jnp.exp(-rate * offsets)
    grow = jnp.exp(rate * offsets)
    scaled_shrink = mode_scale * shrink
    scaled_grow = mode_scale * grow
    one_step = jnp.exp(-rate)
    block_decay = jnp.exp(-rate * tok_rows)
    rows = jnp.arange(tok_rows)
    lower = (rows[:, None] >= rows[None, :]).astype(jnp.float32)
    upper = (rows[:, None] <= rows[None, :]).astype(jnp.float32)

    def prefix(tri, weights, signal):
        spread = weights * jnp.concatenate([signal] * mode_count, axis=1)
        return jnp.dot(tri, spread, precision=highest, preferred_element_type=jnp.float32)

    def over_modes(table):
        total = table[:, :chan_width]
        for mode in range(1, mode_count):
            total = total + table[:, mode * chan_width : (mode + 1) * chan_width]
        return total

    source = jnp.arange(count)

    def entry(gap, got):
        span = (tok_rows * jnp.maximum(gap, 0)).astype(jnp.float32)[:, None]
        held = jnp.where((gap >= 0)[:, None], got.astype(jnp.float32), 0.0)
        return jnp.sum(jnp.exp(-rate * span) * held, axis=0, keepdims=True)

    fwd_sums = prefix(lower, grow, gated)
    fwd_final = (shrink[tok_rows - 1] * fwd_sums[tok_rows - 1]).astype(jnp.bfloat16)
    fwd_got = exchange(fwd_final.reshape(mode_count, chan_width), count, True, 0)
    fwd_got = fwd_got.reshape(count, width)
    fwd_entry = entry(place - 1 - source, fwd_got) * one_step
    long_out = over_modes(scaled_shrink * (fwd_sums + fwd_entry)) + skip_gain[None, :] * gated
    mixer = (q_short * long_out).astype(jnp.bfloat16)
    parts = jnp.einsum("tr,jrc->jtc", mixer, w_all, preferred_element_type=jnp.float32)
    parts = parts.astype(jnp.bfloat16)
    parts, g_all, w_all = lax.optimization_barrier((parts, g_all, w_all))
    received = lax.all_to_all(parts, "ch", 0, 0, tiled=True)
    mixed = jnp.sum(received.astype(jnp.float32), axis=0).astype(jnp.bfloat16)

    grad_mixer = jnp.einsum("jtc,jrc->tr", g_all, w_all, preferred_element_type=jnp.float32)
    grad_long = grad_mixer * q_short
    bwd_sums = prefix(upper, shrink, grad_long)
    bwd_final = bwd_sums[0].astype(jnp.bfloat16).reshape(mode_count, chan_width)
    bwd_got = exchange(bwd_final, count, False, 3).reshape(count, width)
    bwd_entry = entry(source - place - 1, bwd_got) * block_decay

    grad_qshort = grad_mixer * long_out
    grad_gated = (
        over_modes(scaled_grow * (bwd_sums + bwd_entry)) + skip_gain[None, :] * grad_long
    )
    grad_stack = jnp.stack([grad_qshort, grad_gated * v_short, grad_gated * k_short])
    after = from_behind(grad_stack[:, : tap_count - 1, :], "seq", -1)
    extended_back = jnp.concatenate([grad_stack, after], axis=1)
    grads = jnp.zeros((3, tok_rows, chan_width), jnp.float32)
    for tap_index in range(tap_count):
        grads = (
            grads
            + short_taps[tap_index][:, None, :]
            * extended_back[:, tap_index : tap_index + tok_rows, :]
        )
    grads = grads.astype(jnp.bfloat16)
    return (mixed, grads[0], grads[1], grads[2])


def solution(mesh):
    in_specs = (
        P("seq", "ch"),
        P("seq", "ch"),
        P("seq", "ch"),
        P(None, None, "ch"),
        P(None, "ch"),
        P(None, "ch"),
        P("ch"),
        P("ch", "seq"),
        P("seq", "ch"),
    )
    out_specs = (P("seq", "ch"), P("seq", "ch"), P("seq", "ch"), P("seq", "ch"))
    return jax.shard_map(
        per_device, mesh=mesh, in_specs=in_specs, out_specs=out_specs, check_vma=False
    )
```

```python
import functools

import jax
import jax.numpy as jnp
from jax import lax
from jax.experimental import pallas as pl
from jax.experimental.pallas import tpu as pltpu
from jax.sharding import PartitionSpec as P

MESH = pl.DeviceIdType.MESH


def exchange_kernel(count, later, final_ref, got_ref, send_sems, recv_sems):
    me = lax.axis_index("seq")
    lane = lax.axis_index("ch")
    barrier = pltpu.get_barrier_semaphore()
    for peer in range(count):

        @pl.when(me != peer)
        def _():
            pl.semaphore_signal(barrier, inc=1, device_id=(peer, lane), device_id_type=MESH)

    pl.semaphore_wait(barrier, count - 1)

    def link(peer, slot):
        return pltpu.make_async_remote_copy(
            src_ref=final_ref,
            dst_ref=got_ref.at[slot],
            send_sem=send_sems.at[peer],
            recv_sem=recv_sems.at[slot],
            device_id=(peer, lane),
            device_id_type=MESH,
        )

    def sends_to(peer):
        return me < peer if later else me > peer

    def hears_from(peer):
        return me > peer if later else me < peer

    for peer in range(count):

        @pl.when(sends_to(peer))
        def _():
            link(peer, me).start()

    for peer in range(count):

        @pl.when(sends_to(peer))
        def _():
            link(peer, me).wait_send()

        @pl.when(hears_from(peer))
        def _():
            link(peer, peer).wait_recv()


def exchange(final, count, later, collective):
    shape = (count,) + final.shape
    return pl.pallas_call(
        functools.partial(exchange_kernel, count, later),
        out_shape=jax.ShapeDtypeStruct(shape, final.dtype),
        in_specs=[pl.BlockSpec(memory_space=pltpu.VMEM)],
        out_specs=pl.BlockSpec(memory_space=pltpu.VMEM),
        scratch_shapes=[
            pltpu.SemaphoreType.DMA((count,)),
            pltpu.SemaphoreType.DMA((count,)),
        ],
        compiler_params=pltpu.CompilerParams(collective_id=collective, has_side_effects=True),
    )(final)


def from_behind(block, axis, distance):
    devices = range(lax.axis_size(axis))
    route = [(i - distance, i) for i in devices if i - distance in devices]
    return lax.ppermute(block, axis, route)


def fetch_kernel(count, lanes, w_ref, g_ref, w_all, g_all, w_send, w_recv, g_send, g_recv, own_sem):
    me = lax.axis_index("seq")
    lane = lax.axis_index("ch")
    half = count // 2
    core = me % 2
    ring = me // 2
    right = 2 * ((ring + 1) % half) + core
    left = 2 * ((ring + half - 1) % half) + core
    partner = me + 1 - 2 * core
    right_steps = half // 2
    left_steps = half - 1 - right_steps

    barrier = pltpu.get_barrier_semaphore()
    for peer in (right, left, partner):
        pl.semaphore_signal(barrier, inc=1, device_id=(peer, lane), device_id_type=MESH)
    for other in range(lanes):

        @pl.when(lane != other)
        def _():
            pl.semaphore_signal(barrier, inc=1, device_id=(me, other), device_id_type=MESH)

    pl.semaphore_wait(barrier, 3 + lanes - 1)

    def grad_link(other):
        return pltpu.make_async_remote_copy(
            src_ref=g_ref,
            dst_ref=g_all.at[lane],
            send_sem=g_send.at[other],
            recv_sem=g_recv.at[lane],
            device_id=(me, other),
            device_id_type=MESH,
        )

    def grad_arrival(other):
        return pltpu.make_async_remote_copy(
            src_ref=g_ref,
            dst_ref=g_all.at[other],
            send_sem=g_send.at[other],
            recv_sem=g_recv.at[other],
            device_id=(me, other),
            device_id_type=MESH,
        )

    for other in range(lanes):

        @pl.when(lane != other)
        def _():
            grad_link(other).start()

    own_w = pltpu.make_async_copy(w_ref, w_all.at[me], own_sem.at[0])
    own_g = pltpu.make_async_copy(g_ref, g_all.at[lane], own_sem.at[1])
    own_w.start()
    own_g.start()

    sends = []
    pieces = w_recv.shape[0] // count
    depth = w_ref.shape[0] // pieces

    def rows(piece):
        return pl.ds(piece * depth, depth)

    def send(origin, piece, peer, own):
        source = w_ref.at[rows(piece)] if own else w_all.at[origin, rows(piece)]
        copy = pltpu.make_async_remote_copy(
            src_ref=source,
            dst_ref=w_all.at[origin, rows(piece)],
            send_sem=w_send.at[len(sends)],
            recv_sem=w_recv.at[origin * pieces + piece],
            device_id=(peer, lane),
            device_id_type=MESH,
        )
        copy.start()
        sends.append(copy)

    def arrived(origin, piece):
        pltpu.make_async_remote_copy(
            src_ref=w_all.at[origin, rows(piece)],
            dst_ref=w_all.at[origin, rows(piece)],
            send_sem=w_send.at[0],
            recv_sem=w_recv.at[origin * pieces + piece],
            device_id=(me, lane),
            device_id_type=MESH,
        ).wait_recv()

    def right_origin(step):
        return 2 * ((ring - step + 1 + half) % half) + core

    def left_origin(step):
        return 2 * ((ring + step - 1) % half) + core

    for piece in range(pieces):
        if right_steps >= 1:
            send(me, piece, right, True)
        if left_steps >= 1:
            send(me, piece, left, True)
        send(me, piece, partner, True)
    for step in range(2, max(right_steps, left_steps) + 2):
        for piece in range(pieces):
            if step <= right_steps + 1:
                origin = right_origin(step)
                arrived(origin, piece)
                if step <= right_steps:
                    send(origin, piece, right, False)
                send(origin, piece, partner, False)
            if step <= left_steps + 1:
                origin = left_origin(step)
                arrived(origin, piece)
                if step <= left_steps:
                    send(origin, piece, left, False)
                send(origin, piece, partner, False)

    for twin in range(half):
        for piece in range(pieces):
            arrived(2 * twin + 1 - core, piece)
    for copy in sends:
        copy.wait_send()
    for other in range(lanes):

        @pl.when(lane != other)
        def _():
            grad_link(other).wait_send()
            grad_arrival(other).wait_recv()

    own_w.wait()
    own_g.wait()


def fetch(out_weight, grad_out, count, lanes, pieces=4):
    half = count // 2
    sends = (half + half // 2 + (half - 1 - half // 2)) * pieces
    return pl.pallas_call(
        functools.partial(fetch_kernel, count, lanes),
        out_shape=(
            jax.ShapeDtypeStruct((count,) + out_weight.shape, out_weight.dtype),
            jax.ShapeDtypeStruct((lanes,) + grad_out.shape, grad_out.dtype),
        ),
        in_specs=[pl.BlockSpec(memory_space=pl.ANY)] * 2,
        out_specs=(pl.BlockSpec(memory_space=pl.ANY), pl.BlockSpec(memory_space=pl.ANY)),
        scratch_shapes=[
            pltpu.SemaphoreType.DMA((sends,)),
            pltpu.SemaphoreType.DMA((count * pieces,)),
            pltpu.SemaphoreType.DMA((lanes,)),
            pltpu.SemaphoreType.DMA((lanes,)),
            pltpu.SemaphoreType.DMA((2,)),
        ],
        compiler_params=pltpu.CompilerParams(collective_id=1, has_side_effects=True),
    )(out_weight, grad_out)


def per_device(query, key, value, short_taps, decay_rate, residue, skip_gain, out_weight, grad_out):
    tok_rows, chan_width = query.shape
    tap_count = short_taps.shape[0]
    mode_count = decay_rate.shape[0]
    highest = lax.Precision.HIGHEST
    count = lax.axis_size("seq")
    place = lax.axis_index("seq")

    lanes = lax.axis_size("ch")
    w_all, g_all = fetch(out_weight, grad_out, count, lanes)

    streams = jnp.stack([query, key, value])
    before = from_behind(streams[:, tok_rows - (tap_count - 1) :, :], "seq", 1)
    extended = jnp.concatenate([before, streams], axis=1).astype(jnp.float32)
    featured = jnp.zeros((3, tok_rows, chan_width), jnp.float32)
    for tap_index in range(tap_count):
        begin = tap_count - 1 - tap_index
        featured = (
            featured + short_taps[tap_index][:, None, :] * extended[:, begin : begin + tok_rows, :]
        )
    q_short = featured[0]
    k_short = featured[1]
    v_short = featured[2]
    gated = k_short * v_short

    width = mode_count * chan_width
    rate = decay_rate.reshape(1, width)
    mode_scale = (residue * jnp.sqrt(-jnp.expm1(-2.0 * decay_rate))).reshape(1, width)
    offsets = jnp.arange(tok_rows).astype(jnp.float32)[:, None]
    shrink = jnp.exp(-rate * offsets)
    grow = jnp.exp(rate * offsets)
    scaled_shrink = mode_scale * shrink
    scaled_grow = mode_scale * grow
    one_step = jnp.exp(-rate)
    block_decay = jnp.exp(-rate * tok_rows)
    rows = jnp.arange(tok_rows)
    lower = (rows[:, None] >= rows[None, :]).astype(jnp.float32)
    upper = (rows[:, None] <= rows[None, :]).astype(jnp.float32)

    def prefix(tri, weights, signal):
        spread = weights * jnp.concatenate([signal] * mode_count, axis=1)
        return jnp.dot(tri, spread, precision=highest, preferred_element_type=jnp.float32)

    def over_modes(table):
        total = table[:, :chan_width]
        for mode in range(1, mode_count):
            total = total + table[:, mode * chan_width : (mode + 1) * chan_width]
        return total

    source = jnp.arange(count)

    def entry(gap, got):
        span = (tok_rows * jnp.maximum(gap, 0)).astype(jnp.float32)[:, None]
        held = jnp.where((gap >= 0)[:, None], got.astype(jnp.float32), 0.0)
        return jnp.sum(jnp.exp(-rate * span) * held, axis=0, keepdims=True)

    fwd_sums = prefix(lower, grow, gated)
    fwd_final = (shrink[tok_rows - 1] * fwd_sums[tok_rows - 1]).astype(jnp.bfloat16)
    fwd_got = exchange(fwd_final.reshape(mode_count, chan_width), count, True, 0)
    fwd_got = fwd_got.reshape(count, width)
    fwd_entry = entry(place - 1 - source, fwd_got) * one_step
    long_out = over_modes(scaled_shrink * (fwd_sums + fwd_entry)) + skip_gain[None, :] * gated
    mixer = (q_short * long_out).astype(jnp.bfloat16)
    parts = jnp.einsum("tr,jrc->jtc", mixer, w_all, preferred_element_type=jnp.float32)
    parts = parts.astype(jnp.bfloat16)
    parts, g_all, w_all = lax.optimization_barrier((parts, g_all, w_all))
    received = lax.all_to_all(parts, "ch", 0, 0, tiled=True)
    mixed = jnp.sum(received.astype(jnp.float32), axis=0).astype(jnp.bfloat16)

    grad_mixer = jnp.einsum("jtc,jrc->tr", g_all, w_all, preferred_element_type=jnp.float32)
    grad_long = grad_mixer * q_short
    bwd_sums = prefix(upper, shrink, grad_long)
    bwd_final = bwd_sums[0].astype(jnp.bfloat16).reshape(mode_count, chan_width)
    bwd_got = exchange(bwd_final, count, False, 3).reshape(count, width)
    bwd_entry = entry(source - place - 1, bwd_got) * block_decay

    grad_qshort = grad_mixer * long_out
    grad_gated = (
        over_modes(scaled_grow * (bwd_sums + bwd_entry)) + skip_gain[None, :] * grad_long
    )
    grad_stack = jnp.stack([grad_qshort, grad_gated * v_short, grad_gated * k_short])
    after = from_behind(grad_stack[:, : tap_count - 1, :], "seq", -1)
    extended_back = jnp.concatenate([grad_stack, after], axis=1)
    grads = jnp.zeros((3, tok_rows, chan_width), jnp.float32)
    for tap_index in range(tap_count):
        grads = (
            grads
            + short_taps[tap_index][:, None, :]
            * extended_back[:, tap_index : tap_index + tok_rows, :]
        )
    grads = grads.astype(jnp.bfloat16)
    return (mixed, grads[0], grads[1], grads[2])


def solution(mesh):
    in_specs = (
        P("seq", "ch"),
        P("seq", "ch"),
        P("seq", "ch"),
        P(None, None, "ch"),
        P(None, "ch"),
        P(None, "ch"),
        P("ch"),
        P("ch", "seq"),
        P("seq", "ch"),
    )
    out_specs = (P("seq", "ch"), P("seq", "ch"), P("seq", "ch"), P("seq", "ch"))
    return jax.shard_map(
        per_device, mesh=mesh, in_specs=in_specs, out_specs=out_specs, check_vma=False
    )
```

```python
import functools

import jax
import jax.numpy as jnp
from jax import lax
from jax.experimental import pallas as pl
from jax.experimental.pallas import tpu as pltpu
from jax.sharding import PartitionSpec as P

MESH = pl.DeviceIdType.MESH


def exchange_kernel(count, later, final_ref, got_ref, send_sems, recv_sems):
    me = lax.axis_index("seq")
    lane = lax.axis_index("ch")
    barrier = pltpu.get_barrier_semaphore()
    for peer in range(count):

        @pl.when(me != peer)
        def _():
            pl.semaphore_signal(barrier, inc=1, device_id=(peer, lane), device_id_type=MESH)

    pl.semaphore_wait(barrier, count - 1)

    def link(peer, slot):
        return pltpu.make_async_remote_copy(
            src_ref=final_ref,
            dst_ref=got_ref.at[slot],
            send_sem=send_sems.at[peer],
            recv_sem=recv_sems.at[slot],
            device_id=(peer, lane),
            device_id_type=MESH,
        )

    def sends_to(peer):
        return me < peer if later else me > peer

    def hears_from(peer):
        return me > peer if later else me < peer

    for peer in range(count):

        @pl.when(sends_to(peer))
        def _():
            link(peer, me).start()

    for peer in range(count):

        @pl.when(sends_to(peer))
        def _():
            link(peer, me).wait_send()

        @pl.when(hears_from(peer))
        def _():
            link(peer, peer).wait_recv()


def exchange(final, count, later, collective):
    shape = (count,) + final.shape
    return pl.pallas_call(
        functools.partial(exchange_kernel, count, later),
        out_shape=jax.ShapeDtypeStruct(shape, final.dtype),
        in_specs=[pl.BlockSpec(memory_space=pltpu.VMEM)],
        out_specs=pl.BlockSpec(memory_space=pltpu.VMEM),
        scratch_shapes=[
            pltpu.SemaphoreType.DMA((count,)),
            pltpu.SemaphoreType.DMA((count,)),
        ],
        compiler_params=pltpu.CompilerParams(collective_id=collective, has_side_effects=True),
    )(final)


def from_behind(block, axis, distance):
    devices = range(lax.axis_size(axis))
    route = [(i - distance, i) for i in devices if i - distance in devices]
    return lax.ppermute(block, axis, route)


def fetch_kernel(
    count, lanes, w_ref, g_ref, f_ref, w_all, g_all, f_got, w_send, w_recv, g_send, g_recv, own_sem, f_send, f_recv
):
    me = lax.axis_index("seq")
    lane = lax.axis_index("ch")
    half = count // 2
    core = me % 2
    ring = me // 2
    right = 2 * ((ring + 1) % half) + core
    left = 2 * ((ring + half - 1) % half) + core
    partner = me + 1 - 2 * core
    barrier = pltpu.get_barrier_semaphore()
    for peer in range(count):

        @pl.when(me != peer)
        def _():
            pl.semaphore_signal(barrier, inc=1, device_id=(peer, lane), device_id_type=MESH)

    for other in range(lanes):

        @pl.when(lane != other)
        def _():
            pl.semaphore_signal(barrier, inc=1, device_id=(me, other), device_id_type=MESH)

    pl.semaphore_wait(barrier, count - 1 + lanes - 1)

    def state_link(peer, slot):
        return pltpu.make_async_remote_copy(
            src_ref=f_ref,
            dst_ref=f_got.at[slot],
            send_sem=f_send.at[peer],
            recv_sem=f_recv.at[slot],
            device_id=(peer, lane),
            device_id_type=MESH,
        )

    for peer in range(count):

        @pl.when(me < peer)
        def _():
            state_link(peer, me).start()

    def grad_link(other):
        return pltpu.make_async_remote_copy(
            src_ref=g_ref,
            dst_ref=g_all.at[lane],
            send_sem=g_send.at[other],
            recv_sem=g_recv.at[lane],
            device_id=(me, other),
            device_id_type=MESH,
        )

    def grad_arrival(other):
        return pltpu.make_async_remote_copy(
            src_ref=g_ref,
            dst_ref=g_all.at[other],
            send_sem=g_send.at[other],
            recv_sem=g_recv.at[other],
            device_id=(me, other),
            device_id_type=MESH,
        )

    for other in range(lanes):

        @pl.when(lane != other)
        def _():
            grad_link(other).start()

    own_w = pltpu.make_async_copy(w_ref, w_all.at[me], own_sem.at[0])
    own_g = pltpu.make_async_copy(g_ref, g_all.at[lane], own_sem.at[1])
    own_w.start()
    own_g.start()

    sends = []
    pieces = w_recv.shape[0] // count
    depth = w_ref.shape[0] // pieces

    def rows(piece):
        return pl.ds(piece * depth, depth)

    def send(origin, piece, peer, own):
        source = w_ref.at[rows(piece)] if own else w_all.at[origin, rows(piece)]
        copy = pltpu.make_async_remote_copy(
            src_ref=source,
            dst_ref=w_all.at[origin, rows(piece)],
            send_sem=w_send.at[len(sends)],
            recv_sem=w_recv.at[origin * pieces + piece],
            device_id=(peer, lane),
            device_id_type=MESH,
        )
        copy.start()
        sends.append(copy)

    def arrived(origin, piece):
        pltpu.make_async_remote_copy(
            src_ref=w_all.at[origin, rows(piece)],
            dst_ref=w_all.at[origin, rows(piece)],
            send_sem=w_send.at[0],
            recv_sem=w_recv.at[origin * pieces + piece],
            device_id=(me, lane),
            device_id_type=MESH,
        ).wait_recv()

    def right_steps(piece):
        return half // 2 if piece < pieces // 2 else half - 1 - half // 2

    def left_steps(piece):
        return half - 1 - right_steps(piece)

    def right_origin(step):
        return 2 * ((ring - step + 1 + half) % half) + core

    def left_origin(step):
        return 2 * ((ring + step - 1) % half) + core

    longest = max(max(right_steps(p), left_steps(p)) for p in range(pieces))
    for piece in range(pieces):
        if right_steps(piece) >= 1:
            send(me, piece, right, True)
        if left_steps(piece) >= 1:
            send(me, piece, left, True)
        send(me, piece, partner, True)
    for step in range(2, longest + 2):
        for piece in range(pieces):
            if step <= right_steps(piece) + 1:
                origin = right_origin(step)
                arrived(origin, piece)
                if step <= right_steps(piece):
                    send(origin, piece, right, False)
                send(origin, piece, partner, False)
            if step <= left_steps(piece) + 1:
                origin = left_origin(step)
                arrived(origin, piece)
                if step <= left_steps(piece):
                    send(origin, piece, left, False)
                send(origin, piece, partner, False)

    for twin in range(half):
        for piece in range(pieces):
            arrived(2 * twin + 1 - core, piece)
    for copy in sends:
        copy.wait_send()
    for other in range(lanes):

        @pl.when(lane != other)
        def _():
            grad_link(other).wait_send()
            grad_arrival(other).wait_recv()

    for peer in range(count):

        @pl.when(me < peer)
        def _():
            state_link(peer, me).wait_send()

        @pl.when(me > peer)
        def _():
            state_link(peer, peer).wait_recv()

    own_w.wait()
    own_g.wait()


def fetch(out_weight, grad_out, final, count, lanes, pieces=4):
    half = count // 2
    sends = (half + half // 2 + (half - 1 - half // 2)) * pieces
    return pl.pallas_call(
        functools.partial(fetch_kernel, count, lanes),
        out_shape=(
            jax.ShapeDtypeStruct((count,) + out_weight.shape, out_weight.dtype),
            jax.ShapeDtypeStruct((lanes,) + grad_out.shape, grad_out.dtype),
            jax.ShapeDtypeStruct((count,) + final.shape, final.dtype),
        ),
        in_specs=[pl.BlockSpec(memory_space=pl.ANY)] * 2 + [pl.BlockSpec(memory_space=pltpu.VMEM)],
        out_specs=(
            pl.BlockSpec(memory_space=pl.ANY),
            pl.BlockSpec(memory_space=pl.ANY),
            pl.BlockSpec(memory_space=pltpu.VMEM),
        ),
        scratch_shapes=[
            pltpu.SemaphoreType.DMA((sends,)),
            pltpu.SemaphoreType.DMA((count * pieces,)),
            pltpu.SemaphoreType.DMA((lanes,)),
            pltpu.SemaphoreType.DMA((lanes,)),
            pltpu.SemaphoreType.DMA((2,)),
            pltpu.SemaphoreType.DMA((count,)),
            pltpu.SemaphoreType.DMA((count,)),
        ],
        compiler_params=pltpu.CompilerParams(collective_id=1, has_side_effects=True),
    )(out_weight, grad_out, final)


def per_device(query, key, value, short_taps, decay_rate, residue, skip_gain, out_weight, grad_out):
    tok_rows, chan_width = query.shape
    tap_count = short_taps.shape[0]
    mode_count = decay_rate.shape[0]
    highest = lax.Precision.HIGHEST
    count = lax.axis_size("seq")
    place = lax.axis_index("seq")

    lanes = lax.axis_size("ch")

    streams = jnp.stack([query, key, value])
    before = from_behind(streams[:, tok_rows - (tap_count - 1) :, :], "seq", 1)
    extended = jnp.concatenate([before, streams], axis=1).astype(jnp.float32)
    featured = jnp.zeros((3, tok_rows, chan_width), jnp.float32)
    for tap_index in range(tap_count):
        begin = tap_count - 1 - tap_index
        featured = (
            featured + short_taps[tap_index][:, None, :] * extended[:, begin : begin + tok_rows, :]
        )
    q_short = featured[0]
    k_short = featured[1]
    v_short = featured[2]
    gated = k_short * v_short

    width = mode_count * chan_width
    rate = decay_rate.reshape(1, width)
    mode_scale = (residue * jnp.sqrt(-jnp.expm1(-2.0 * decay_rate))).reshape(1, width)
    offsets = jnp.arange(tok_rows).astype(jnp.float32)[:, None]
    shrink = jnp.exp(-rate * offsets)
    grow = jnp.exp(rate * offsets)
    scaled_shrink = mode_scale * shrink
    scaled_grow = mode_scale * grow
    one_step = jnp.exp(-rate)
    block_decay = jnp.exp(-rate * tok_rows)
    rows = jnp.arange(tok_rows)
    lower = (rows[:, None] >= rows[None, :]).astype(jnp.float32)
    upper = (rows[:, None] <= rows[None, :]).astype(jnp.float32)

    def prefix(tri, weights, signal):
        spread = weights * jnp.concatenate([signal] * mode_count, axis=1)
        return jnp.dot(tri, spread, precision=highest, preferred_element_type=jnp.float32)

    def over_modes(table):
        total = table[:, :chan_width]
        for mode in range(1, mode_count):
            total = total + table[:, mode * chan_width : (mode + 1) * chan_width]
        return total

    source = jnp.arange(count)

    def entry(gap, got):
        span = (tok_rows * jnp.maximum(gap, 0)).astype(jnp.float32)[:, None]
        held = jnp.where((gap >= 0)[:, None], got.astype(jnp.float32), 0.0)
        return jnp.sum(jnp.exp(-rate * span) * held, axis=0, keepdims=True)

    fwd_sums = prefix(lower, grow, gated)
    fwd_final = (shrink[tok_rows - 1] * fwd_sums[tok_rows - 1]).astype(jnp.bfloat16)
    w_all, g_all, fwd_got = fetch(
        out_weight, grad_out, fwd_final.reshape(mode_count, chan_width), count, lanes
    )
    fwd_got = fwd_got.reshape(count, width)
    fwd_entry = entry(place - 1 - source, fwd_got) * one_step
    long_out = over_modes(scaled_shrink * (fwd_sums + fwd_entry)) + skip_gain[None, :] * gated
    mixer = (q_short * long_out).astype(jnp.bfloat16)
    parts = jnp.einsum("tr,jrc->jtc", mixer, w_all, preferred_element_type=jnp.float32)
    parts = parts.astype(jnp.bfloat16)
    parts, g_all, w_all = lax.optimization_barrier((parts, g_all, w_all))
    received = lax.all_to_all(parts, "ch", 0, 0, tiled=True)
    mixed = jnp.sum(received.astype(jnp.float32), axis=0).astype(jnp.bfloat16)

    grad_mixer = jnp.einsum("jtc,jrc->tr", g_all, w_all, preferred_element_type=jnp.float32)
    grad_long = grad_mixer * q_short
    bwd_sums = prefix(upper, shrink, grad_long)
    bwd_final = bwd_sums[0].astype(jnp.bfloat16).reshape(mode_count, chan_width)
    bwd_got = exchange(bwd_final, count, False, 3).reshape(count, width)
    bwd_entry = entry(source - place - 1, bwd_got) * block_decay

    grad_qshort = grad_mixer * long_out
    grad_gated = (
        over_modes(scaled_grow * (bwd_sums + bwd_entry)) + skip_gain[None, :] * grad_long
    )
    grad_stack = jnp.stack([grad_qshort, grad_gated * v_short, grad_gated * k_short])
    after = from_behind(grad_stack[:, : tap_count - 1, :], "seq", -1)
    extended_back = jnp.concatenate([grad_stack, after], axis=1)
    grads = jnp.zeros((3, tok_rows, chan_width), jnp.float32)
    for tap_index in range(tap_count):
        grads = (
            grads
            + short_taps[tap_index][:, None, :]
            * extended_back[:, tap_index : tap_index + tok_rows, :]
        )
    grads = grads.astype(jnp.bfloat16)
    return (mixed, grads[0], grads[1], grads[2])


def solution(mesh):
    in_specs = (
        P("seq", "ch"),
        P("seq", "ch"),
        P("seq", "ch"),
        P(None, None, "ch"),
        P(None, "ch"),
        P(None, "ch"),
        P("ch"),
        P("ch", "seq"),
        P("seq", "ch"),
    )
    out_specs = (P("seq", "ch"), P("seq", "ch"), P("seq", "ch"), P("seq", "ch"))
    return jax.shard_map(
        per_device, mesh=mesh, in_specs=in_specs, out_specs=out_specs, check_vma=False
    )
```

```python
import functools

import jax
import jax.numpy as jnp
from jax import lax
from jax.experimental import pallas as pl
from jax.experimental.pallas import tpu as pltpu
from jax.sharding import PartitionSpec as P

MESH = pl.DeviceIdType.MESH


def exchange_kernel(count, later, final_ref, got_ref, send_sems, recv_sems):
    me = lax.axis_index("seq")
    lane = lax.axis_index("ch")
    barrier = pltpu.get_barrier_semaphore()
    for peer in range(count):

        @pl.when(me != peer)
        def _():
            pl.semaphore_signal(barrier, inc=1, device_id=(peer, lane), device_id_type=MESH)

    pl.semaphore_wait(barrier, count - 1)

    def link(peer, slot):
        return pltpu.make_async_remote_copy(
            src_ref=final_ref,
            dst_ref=got_ref.at[slot],
            send_sem=send_sems.at[peer],
            recv_sem=recv_sems.at[slot],
            device_id=(peer, lane),
            device_id_type=MESH,
        )

    def sends_to(peer):
        return me < peer if later else me > peer

    def hears_from(peer):
        return me > peer if later else me < peer

    for peer in range(count):

        @pl.when(sends_to(peer))
        def _():
            link(peer, me).start()

    for peer in range(count):

        @pl.when(sends_to(peer))
        def _():
            link(peer, me).wait_send()

        @pl.when(hears_from(peer))
        def _():
            link(peer, peer).wait_recv()


def exchange(final, count, later, collective):
    shape = (count,) + final.shape
    return pl.pallas_call(
        functools.partial(exchange_kernel, count, later),
        out_shape=jax.ShapeDtypeStruct(shape, final.dtype),
        in_specs=[pl.BlockSpec(memory_space=pltpu.VMEM)],
        out_specs=pl.BlockSpec(memory_space=pltpu.VMEM),
        scratch_shapes=[
            pltpu.SemaphoreType.DMA((count,)),
            pltpu.SemaphoreType.DMA((count,)),
        ],
        compiler_params=pltpu.CompilerParams(collective_id=collective, has_side_effects=True),
    )(final)


def from_behind(block, axis, distance):
    devices = range(lax.axis_size(axis))
    route = [(i - distance, i) for i in devices if i - distance in devices]
    return lax.ppermute(block, axis, route)


def fetch_kernel(
    count, lanes, w_ref, g_ref, f_ref, w_all, g_all, f_got, w_send, w_recv, g_send, g_recv, own_sem, f_send, f_recv
):
    me = lax.axis_index("seq")
    lane = lax.axis_index("ch")
    half = count // 2
    core = me % 2
    ring = me // 2
    right = 2 * ((ring + 1) % half) + core
    left = 2 * ((ring + half - 1) % half) + core
    partner = me + 1 - 2 * core
    barrier = pltpu.get_barrier_semaphore()
    for peer in range(count):

        @pl.when(me != peer)
        def _():
            pl.semaphore_signal(barrier, inc=1, device_id=(peer, lane), device_id_type=MESH)

    for other in range(lanes):

        @pl.when(lane != other)
        def _():
            pl.semaphore_signal(barrier, inc=1, device_id=(me, other), device_id_type=MESH)

    pl.semaphore_wait(barrier, count - 1 + lanes - 1)

    def state_link(peer, slot):
        return pltpu.make_async_remote_copy(
            src_ref=f_ref,
            dst_ref=f_got.at[slot],
            send_sem=f_send.at[peer],
            recv_sem=f_recv.at[slot],
            device_id=(peer, lane),
            device_id_type=MESH,
        )

    for peer in range(count):

        @pl.when(me < peer)
        def _():
            state_link(peer, me).start()

    def grad_link(other):
        return pltpu.make_async_remote_copy(
            src_ref=g_ref,
            dst_ref=g_all.at[lane],
            send_sem=g_send.at[other],
            recv_sem=g_recv.at[lane],
            device_id=(me, other),
            device_id_type=MESH,
        )

    def grad_arrival(other):
        return pltpu.make_async_remote_copy(
            src_ref=g_ref,
            dst_ref=g_all.at[other],
            send_sem=g_send.at[other],
            recv_sem=g_recv.at[other],
            device_id=(me, other),
            device_id_type=MESH,
        )

    for other in range(lanes):

        @pl.when(lane != other)
        def _():
            grad_link(other).start()

    own_w = pltpu.make_async_copy(w_ref, w_all.at[me], own_sem.at[0])
    own_g = pltpu.make_async_copy(g_ref, g_all.at[lane], own_sem.at[1])
    own_w.start()
    own_g.start()

    sends = []
    pieces = w_recv.shape[0] // count
    depth = w_ref.shape[0] // pieces

    def rows(piece):
        return pl.ds(piece * depth, depth)

    def send(origin, piece, peer, own):
        source = w_ref.at[rows(piece)] if own else w_all.at[origin, rows(piece)]
        copy = pltpu.make_async_remote_copy(
            src_ref=source,
            dst_ref=w_all.at[origin, rows(piece)],
            send_sem=w_send.at[len(sends)],
            recv_sem=w_recv.at[origin * pieces + piece],
            device_id=(peer, lane),
            device_id_type=MESH,
        )
        copy.start()
        sends.append(copy)

    def arrived(origin, piece):
        pltpu.make_async_remote_copy(
            src_ref=w_all.at[origin, rows(piece)],
            dst_ref=w_all.at[origin, rows(piece)],
            send_sem=w_send.at[0],
            recv_sem=w_recv.at[origin * pieces + piece],
            device_id=(me, lane),
            device_id_type=MESH,
        ).wait_recv()

    def right_steps(piece):
        return half // 2 if piece < pieces // 2 else half - 1 - half // 2

    def left_steps(piece):
        return half - 1 - right_steps(piece)

    def right_origin(step):
        return 2 * ((ring - step + 1 + half) % half) + core

    def left_origin(step):
        return 2 * ((ring + step - 1) % half) + core

    longest = max(max(right_steps(p), left_steps(p)) for p in range(pieces))
    for piece in range(pieces):
        if right_steps(piece) >= 1:
            send(me, piece, right, True)
        if left_steps(piece) >= 1:
            send(me, piece, left, True)
        send(me, piece, partner, True)
    for step in range(2, longest + 2):
        for piece in range(pieces):
            if step <= right_steps(piece) + 1:
                origin = right_origin(step)
                arrived(origin, piece)
                if step <= right_steps(piece):
                    send(origin, piece, right, False)
                send(origin, piece, partner, False)
            if step <= left_steps(piece) + 1:
                origin = left_origin(step)
                arrived(origin, piece)
                if step <= left_steps(piece):
                    send(origin, piece, left, False)
                send(origin, piece, partner, False)

    for twin in range(half):
        for piece in range(pieces):
            arrived(2 * twin + 1 - core, piece)
    for copy in sends:
        copy.wait_send()
    for other in range(lanes):

        @pl.when(lane != other)
        def _():
            grad_link(other).wait_send()
            grad_arrival(other).wait_recv()

    for peer in range(count):

        @pl.when(me < peer)
        def _():
            state_link(peer, me).wait_send()

        @pl.when(me > peer)
        def _():
            state_link(peer, peer).wait_recv()

    own_w.wait()
    own_g.wait()


def fetch(out_weight, grad_out, final, count, lanes, pieces=8):
    half = count // 2
    sends = (half + half // 2 + (half - 1 - half // 2)) * pieces
    return pl.pallas_call(
        functools.partial(fetch_kernel, count, lanes),
        out_shape=(
            jax.ShapeDtypeStruct((count,) + out_weight.shape, out_weight.dtype),
            jax.ShapeDtypeStruct((lanes,) + grad_out.shape, grad_out.dtype),
            jax.ShapeDtypeStruct((count,) + final.shape, final.dtype),
        ),
        in_specs=[pl.BlockSpec(memory_space=pl.ANY)] * 2 + [pl.BlockSpec(memory_space=pltpu.VMEM)],
        out_specs=(
            pl.BlockSpec(memory_space=pl.ANY),
            pl.BlockSpec(memory_space=pl.ANY),
            pl.BlockSpec(memory_space=pltpu.VMEM),
        ),
        scratch_shapes=[
            pltpu.SemaphoreType.DMA((sends,)),
            pltpu.SemaphoreType.DMA((count * pieces,)),
            pltpu.SemaphoreType.DMA((lanes,)),
            pltpu.SemaphoreType.DMA((lanes,)),
            pltpu.SemaphoreType.DMA((2,)),
            pltpu.SemaphoreType.DMA((count,)),
            pltpu.SemaphoreType.DMA((count,)),
        ],
        compiler_params=pltpu.CompilerParams(collective_id=1, has_side_effects=True),
    )(out_weight, grad_out, final)


def per_device(query, key, value, short_taps, decay_rate, residue, skip_gain, out_weight, grad_out):
    tok_rows, chan_width = query.shape
    tap_count = short_taps.shape[0]
    mode_count = decay_rate.shape[0]
    highest = lax.Precision.HIGHEST
    count = lax.axis_size("seq")
    place = lax.axis_index("seq")

    lanes = lax.axis_size("ch")

    streams = jnp.stack([query, key, value])
    before = from_behind(streams[:, tok_rows - (tap_count - 1) :, :], "seq", 1)
    extended = jnp.concatenate([before, streams], axis=1).astype(jnp.float32)
    featured = jnp.zeros((3, tok_rows, chan_width), jnp.float32)
    for tap_index in range(tap_count):
        begin = tap_count - 1 - tap_index
        featured = (
            featured + short_taps[tap_index][:, None, :] * extended[:, begin : begin + tok_rows, :]
        )
    q_short = featured[0]
    k_short = featured[1]
    v_short = featured[2]
    gated = k_short * v_short

    width = mode_count * chan_width
    rate = decay_rate.reshape(1, width)
    mode_scale = (residue * jnp.sqrt(-jnp.expm1(-2.0 * decay_rate))).reshape(1, width)
    offsets = jnp.arange(tok_rows).astype(jnp.float32)[:, None]
    shrink = jnp.exp(-rate * offsets)
    grow = jnp.exp(rate * offsets)
    scaled_shrink = mode_scale * shrink
    scaled_grow = mode_scale * grow
    one_step = jnp.exp(-rate)
    block_decay = jnp.exp(-rate * tok_rows)
    rows = jnp.arange(tok_rows)
    lower = (rows[:, None] >= rows[None, :]).astype(jnp.float32)
    upper = (rows[:, None] <= rows[None, :]).astype(jnp.float32)

    def prefix(tri, weights, signal):
        spread = weights * jnp.concatenate([signal] * mode_count, axis=1)
        return jnp.dot(tri, spread, precision=highest, preferred_element_type=jnp.float32)

    def over_modes(table):
        total = table[:, :chan_width]
        for mode in range(1, mode_count):
            total = total + table[:, mode * chan_width : (mode + 1) * chan_width]
        return total

    source = jnp.arange(count)

    def entry(gap, got):
        span = (tok_rows * jnp.maximum(gap, 0)).astype(jnp.float32)[:, None]
        held = jnp.where((gap >= 0)[:, None], got.astype(jnp.float32), 0.0)
        return jnp.sum(jnp.exp(-rate * span) * held, axis=0, keepdims=True)

    fwd_sums = prefix(lower, grow, gated)
    fwd_final = (shrink[tok_rows - 1] * fwd_sums[tok_rows - 1]).astype(jnp.bfloat16)
    w_all, g_all, fwd_got = fetch(
        out_weight, grad_out, fwd_final.reshape(mode_count, chan_width), count, lanes
    )
    fwd_got = fwd_got.reshape(count, width)
    fwd_entry = entry(place - 1 - source, fwd_got) * one_step
    long_out = over_modes(scaled_shrink * (fwd_sums + fwd_entry)) + skip_gain[None, :] * gated
    mixer = (q_short * long_out).astype(jnp.bfloat16)
    parts = jnp.einsum("tr,jrc->jtc", mixer, w_all, preferred_element_type=jnp.float32)
    parts = parts.astype(jnp.bfloat16)
    parts, g_all, w_all = lax.optimization_barrier((parts, g_all, w_all))
    received = lax.all_to_all(parts, "ch", 0, 0, tiled=True)
    mixed = jnp.sum(received.astype(jnp.float32), axis=0).astype(jnp.bfloat16)

    grad_mixer = jnp.einsum("jtc,jrc->tr", g_all, w_all, preferred_element_type=jnp.float32)
    grad_long = grad_mixer * q_short
    bwd_sums = prefix(upper, shrink, grad_long)
    bwd_final = bwd_sums[0].astype(jnp.bfloat16).reshape(mode_count, chan_width)
    bwd_got = exchange(bwd_final, count, False, 3).reshape(count, width)
    bwd_entry = entry(source - place - 1, bwd_got) * block_decay

    grad_qshort = grad_mixer * long_out
    grad_gated = (
        over_modes(scaled_grow * (bwd_sums + bwd_entry)) + skip_gain[None, :] * grad_long
    )
    grad_stack = jnp.stack([grad_qshort, grad_gated * v_short, grad_gated * k_short])
    after = from_behind(grad_stack[:, : tap_count - 1, :], "seq", -1)
    extended_back = jnp.concatenate([grad_stack, after], axis=1)
    grads = jnp.zeros((3, tok_rows, chan_width), jnp.float32)
    for tap_index in range(tap_count):
        grads = (
            grads
            + short_taps[tap_index][:, None, :]
            * extended_back[:, tap_index : tap_index + tok_rows, :]
        )
    grads = grads.astype(jnp.bfloat16)
    return (mixed, grads[0], grads[1], grads[2])


def solution(mesh):
    in_specs = (
        P("seq", "ch"),
        P("seq", "ch"),
        P("seq", "ch"),
        P(None, None, "ch"),
        P(None, "ch"),
        P(None, "ch"),
        P("ch"),
        P("ch", "seq"),
        P("seq", "ch"),
    )
    out_specs = (P("seq", "ch"), P("seq", "ch"), P("seq", "ch"), P("seq", "ch"))
    return jax.shard_map(
        per_device, mesh=mesh, in_specs=in_specs, out_specs=out_specs, check_vma=False
    )
```

```python
import functools

import jax
import jax.numpy as jnp
from jax import lax
from jax.experimental import pallas as pl
from jax.experimental.pallas import tpu as pltpu
from jax.sharding import PartitionSpec as P

MESH = pl.DeviceIdType.MESH


def exchange_kernel(count, later, final_ref, got_ref, send_sems, recv_sems):
    me = lax.axis_index("seq")
    lane = lax.axis_index("ch")
    barrier = pltpu.get_barrier_semaphore()
    for peer in range(count):

        @pl.when(me != peer)
        def _():
            pl.semaphore_signal(barrier, inc=1, device_id=(peer, lane), device_id_type=MESH)

    pl.semaphore_wait(barrier, count - 1)

    def link(peer, slot):
        return pltpu.make_async_remote_copy(
            src_ref=final_ref,
            dst_ref=got_ref.at[slot],
            send_sem=send_sems.at[peer],
            recv_sem=recv_sems.at[slot],
            device_id=(peer, lane),
            device_id_type=MESH,
        )

    def sends_to(peer):
        return me < peer if later else me > peer

    def hears_from(peer):
        return me > peer if later else me < peer

    for peer in range(count):

        @pl.when(sends_to(peer))
        def _():
            link(peer, me).start()

    for peer in range(count):

        @pl.when(sends_to(peer))
        def _():
            link(peer, me).wait_send()

        @pl.when(hears_from(peer))
        def _():
            link(peer, peer).wait_recv()


def exchange(final, count, later, collective):
    shape = (count,) + final.shape
    return pl.pallas_call(
        functools.partial(exchange_kernel, count, later),
        out_shape=jax.ShapeDtypeStruct(shape, final.dtype),
        in_specs=[pl.BlockSpec(memory_space=pltpu.VMEM)],
        out_specs=pl.BlockSpec(memory_space=pltpu.VMEM),
        scratch_shapes=[
            pltpu.SemaphoreType.DMA((count,)),
            pltpu.SemaphoreType.DMA((count,)),
        ],
        compiler_params=pltpu.CompilerParams(collective_id=collective, has_side_effects=True),
    )(final)


def from_behind(block, axis, distance):
    devices = range(lax.axis_size(axis))
    route = [(i - distance, i) for i in devices if i - distance in devices]
    return lax.ppermute(block, axis, route)


def fetch_kernel(
    count, lanes, w_ref, g_ref, f_ref, w_all, g_all, f_got, w_send, w_recv, g_send, g_recv, own_sem, f_send, f_recv
):
    me = lax.axis_index("seq")
    lane = lax.axis_index("ch")
    half = count // 2
    core = me % 2
    ring = me // 2
    right = 2 * ((ring + 1) % half) + core
    left = 2 * ((ring + half - 1) % half) + core
    partner = me + 1 - 2 * core
    barrier = pltpu.get_barrier_semaphore()
    for peer in range(count):

        @pl.when(me != peer)
        def _():
            pl.semaphore_signal(barrier, inc=1, device_id=(peer, lane), device_id_type=MESH)

    for other in range(lanes):

        @pl.when(lane != other)
        def _():
            pl.semaphore_signal(barrier, inc=1, device_id=(me, other), device_id_type=MESH)

    pl.semaphore_wait(barrier, count - 1 + lanes - 1)

    def state_link(peer, slot):
        return pltpu.make_async_remote_copy(
            src_ref=f_ref,
            dst_ref=f_got.at[slot],
            send_sem=f_send.at[peer],
            recv_sem=f_recv.at[slot],
            device_id=(peer, lane),
            device_id_type=MESH,
        )

    for peer in range(count):

        @pl.when(me < peer)
        def _():
            state_link(peer, me).start()

    def grad_link(other):
        return pltpu.make_async_remote_copy(
            src_ref=g_ref,
            dst_ref=g_all.at[lane],
            send_sem=g_send.at[other],
            recv_sem=g_recv.at[lane],
            device_id=(me, other),
            device_id_type=MESH,
        )

    def grad_arrival(other):
        return pltpu.make_async_remote_copy(
            src_ref=g_ref,
            dst_ref=g_all.at[other],
            send_sem=g_send.at[other],
            recv_sem=g_recv.at[other],
            device_id=(me, other),
            device_id_type=MESH,
        )

    for other in range(lanes):

        @pl.when(lane != other)
        def _():
            grad_link(other).start()

    own_w = pltpu.make_async_copy(w_ref, w_all.at[me], own_sem.at[0])
    own_g = pltpu.make_async_copy(g_ref, g_all.at[lane], own_sem.at[1])
    own_w.start()
    own_g.start()

    sends = []
    pieces = w_recv.shape[0] // count
    depth = w_ref.shape[0] // pieces

    def rows(piece):
        return pl.ds(piece * depth, depth)

    def send(origin, piece, peer, own):
        source = w_ref.at[rows(piece)] if own else w_all.at[origin, rows(piece)]
        copy = pltpu.make_async_remote_copy(
            src_ref=source,
            dst_ref=w_all.at[origin, rows(piece)],
            send_sem=w_send.at[len(sends)],
            recv_sem=w_recv.at[origin * pieces + piece],
            device_id=(peer, lane),
            device_id_type=MESH,
        )
        copy.start()
        sends.append(copy)

    def arrived(origin, piece):
        pltpu.make_async_remote_copy(
            src_ref=w_all.at[origin, rows(piece)],
            dst_ref=w_all.at[origin, rows(piece)],
            send_sem=w_send.at[0],
            recv_sem=w_recv.at[origin * pieces + piece],
            device_id=(me, lane),
            device_id_type=MESH,
        ).wait_recv()

    def right_steps(piece):
        return half // 2 if piece < pieces // 2 else half - 1 - half // 2

    def left_steps(piece):
        return half - 1 - right_steps(piece)

    def right_origin(step):
        return 2 * ((ring - step + 1 + half) % half) + core

    def left_origin(step):
        return 2 * ((ring + step - 1) % half) + core

    longest = max(max(right_steps(p), left_steps(p)) for p in range(pieces))
    for piece in range(pieces):
        if right_steps(piece) >= 1:
            send(me, piece, right, True)
        if left_steps(piece) >= 1:
            send(me, piece, left, True)
        send(me, piece, partner, True)
    for step in range(2, longest + 2):
        for piece in range(pieces):
            if step <= right_steps(piece) + 1:
                origin = right_origin(step)
                arrived(origin, piece)
                if step <= right_steps(piece):
                    send(origin, piece, right, False)
                send(origin, piece, partner, False)
            if step <= left_steps(piece) + 1:
                origin = left_origin(step)
                arrived(origin, piece)
                if step <= left_steps(piece):
                    send(origin, piece, left, False)
                send(origin, piece, partner, False)

    for twin in range(half):
        for piece in range(pieces):
            arrived(2 * twin + 1 - core, piece)
    for copy in sends:
        copy.wait_send()
    for other in range(lanes):

        @pl.when(lane != other)
        def _():
            grad_link(other).wait_send()
            grad_arrival(other).wait_recv()

    for peer in range(count):

        @pl.when(me < peer)
        def _():
            state_link(peer, me).wait_send()

        @pl.when(me > peer)
        def _():
            state_link(peer, peer).wait_recv()

    own_w.wait()
    own_g.wait()


def fetch(out_weight, grad_out, final, count, lanes, pieces=4):
    half = count // 2
    sends = (half + half // 2 + (half - 1 - half // 2)) * pieces
    return pl.pallas_call(
        functools.partial(fetch_kernel, count, lanes),
        out_shape=(
            jax.ShapeDtypeStruct((count,) + out_weight.shape, out_weight.dtype),
            jax.ShapeDtypeStruct((lanes,) + grad_out.shape, grad_out.dtype),
            jax.ShapeDtypeStruct((count,) + final.shape, final.dtype),
        ),
        in_specs=[pl.BlockSpec(memory_space=pl.ANY)] * 2 + [pl.BlockSpec(memory_space=pltpu.VMEM)],
        out_specs=(
            pl.BlockSpec(memory_space=pl.ANY),
            pl.BlockSpec(memory_space=pl.ANY),
            pl.BlockSpec(memory_space=pltpu.VMEM),
        ),
        scratch_shapes=[
            pltpu.SemaphoreType.DMA((sends,)),
            pltpu.SemaphoreType.DMA((count * pieces,)),
            pltpu.SemaphoreType.DMA((lanes,)),
            pltpu.SemaphoreType.DMA((lanes,)),
            pltpu.SemaphoreType.DMA((2,)),
            pltpu.SemaphoreType.DMA((count,)),
            pltpu.SemaphoreType.DMA((count,)),
        ],
        compiler_params=pltpu.CompilerParams(collective_id=1, has_side_effects=True),
    )(out_weight, grad_out, final)


def per_device(query, key, value, short_taps, decay_rate, residue, skip_gain, out_weight, grad_out):
    tok_rows, chan_width = query.shape
    tap_count = short_taps.shape[0]
    mode_count = decay_rate.shape[0]
    highest = lax.Precision.HIGHEST
    count = lax.axis_size("seq")
    place = lax.axis_index("seq")

    lanes = lax.axis_size("ch")

    streams = jnp.stack([query, key, value])
    before = from_behind(streams[:, tok_rows - (tap_count - 1) :, :], "seq", 1)
    extended = jnp.concatenate([before, streams], axis=1).astype(jnp.float32)
    featured = jnp.zeros((3, tok_rows, chan_width), jnp.float32)
    for tap_index in range(tap_count):
        begin = tap_count - 1 - tap_index
        featured = (
            featured + short_taps[tap_index][:, None, :] * extended[:, begin : begin + tok_rows, :]
        )
    q_short = featured[0]
    k_short = featured[1]
    v_short = featured[2]
    gated = k_short * v_short

    width = mode_count * chan_width
    rate = decay_rate.reshape(1, width)
    mode_scale = (residue * jnp.sqrt(-jnp.expm1(-2.0 * decay_rate))).reshape(1, width)
    offsets = jnp.arange(tok_rows).astype(jnp.float32)[:, None]
    shrink = jnp.exp(-rate * offsets)
    grow = jnp.exp(rate * offsets)
    scaled_shrink = mode_scale * shrink
    scaled_grow = mode_scale * grow
    one_step = jnp.exp(-rate)
    block_decay = jnp.exp(-rate * tok_rows)
    rows = jnp.arange(tok_rows)
    lower = (rows[:, None] >= rows[None, :]).astype(jnp.float32)
    upper = (rows[:, None] <= rows[None, :]).astype(jnp.float32)

    def prefix(tri, weights, signal):
        spread = weights * jnp.concatenate([signal] * mode_count, axis=1)
        return jnp.dot(tri, spread, precision=highest, preferred_element_type=jnp.float32)

    def over_modes(table):
        total = table[:, :chan_width]
        for mode in range(1, mode_count):
            total = total + table[:, mode * chan_width : (mode + 1) * chan_width]
        return total

    source = jnp.arange(count)

    def entry(gap, got):
        span = (tok_rows * jnp.maximum(gap, 0)).astype(jnp.float32)[:, None]
        held = jnp.where((gap >= 0)[:, None], got.astype(jnp.float32), 0.0)
        return jnp.sum(jnp.exp(-rate * span) * held, axis=0, keepdims=True)

    spread_gated = jnp.concatenate([gated] * mode_count, axis=1)
    fwd_final = jnp.sum(shrink[::-1] * spread_gated, axis=0).astype(jnp.bfloat16)
    w_all, g_all, fwd_got = fetch(
        out_weight, grad_out, fwd_final.reshape(mode_count, chan_width), count, lanes
    )
    fwd_got = fwd_got.reshape(count, width)
    fwd_sums = prefix(lower, grow, gated)
    fwd_entry = entry(place - 1 - source, fwd_got) * one_step
    long_out = over_modes(scaled_shrink * (fwd_sums + fwd_entry)) + skip_gain[None, :] * gated
    mixer = (q_short * long_out).astype(jnp.bfloat16)
    parts = jnp.einsum("tr,jrc->jtc", mixer, w_all, preferred_element_type=jnp.float32)
    parts = parts.astype(jnp.bfloat16)
    parts, g_all, w_all = lax.optimization_barrier((parts, g_all, w_all))
    received = lax.all_to_all(parts, "ch", 0, 0, tiled=True)
    mixed = jnp.sum(received.astype(jnp.float32), axis=0).astype(jnp.bfloat16)

    grad_mixer = jnp.einsum("jtc,jrc->tr", g_all, w_all, preferred_element_type=jnp.float32)
    grad_long = grad_mixer * q_short
    bwd_sums = prefix(upper, shrink, grad_long)
    bwd_final = bwd_sums[0].astype(jnp.bfloat16).reshape(mode_count, chan_width)
    bwd_got = exchange(bwd_final, count, False, 3).reshape(count, width)
    bwd_entry = entry(source - place - 1, bwd_got) * block_decay

    grad_qshort = grad_mixer * long_out
    grad_gated = (
        over_modes(scaled_grow * (bwd_sums + bwd_entry)) + skip_gain[None, :] * grad_long
    )
    grad_stack = jnp.stack([grad_qshort, grad_gated * v_short, grad_gated * k_short])
    after = from_behind(grad_stack[:, : tap_count - 1, :], "seq", -1)
    extended_back = jnp.concatenate([grad_stack, after], axis=1)
    grads = jnp.zeros((3, tok_rows, chan_width), jnp.float32)
    for tap_index in range(tap_count):
        grads = (
            grads
            + short_taps[tap_index][:, None, :]
            * extended_back[:, tap_index : tap_index + tok_rows, :]
        )
    grads = grads.astype(jnp.bfloat16)
    return (mixed, grads[0], grads[1], grads[2])


def solution(mesh):
    in_specs = (
        P("seq", "ch"),
        P("seq", "ch"),
        P("seq", "ch"),
        P(None, None, "ch"),
        P(None, "ch"),
        P(None, "ch"),
        P("ch"),
        P("ch", "seq"),
        P("seq", "ch"),
    )
    out_specs = (P("seq", "ch"), P("seq", "ch"), P("seq", "ch"), P("seq", "ch"))
    return jax.shard_map(
        per_device, mesh=mesh, in_specs=in_specs, out_specs=out_specs, check_vma=False
    )
```

```python
import functools

import jax
import jax.numpy as jnp
from jax import lax
from jax.experimental import pallas as pl
from jax.experimental.pallas import tpu as pltpu
from jax.sharding import PartitionSpec as P

MESH = pl.DeviceIdType.MESH


def exchange_kernel(count, later, final_ref, got_ref, send_sems, recv_sems):
    me = lax.axis_index("seq")
    lane = lax.axis_index("ch")
    barrier = pltpu.get_barrier_semaphore()
    for peer in range(count):

        @pl.when(me != peer)
        def _():
            pl.semaphore_signal(barrier, inc=1, device_id=(peer, lane), device_id_type=MESH)

    pl.semaphore_wait(barrier, count - 1)

    def link(peer, slot):
        return pltpu.make_async_remote_copy(
            src_ref=final_ref,
            dst_ref=got_ref.at[slot],
            send_sem=send_sems.at[peer],
            recv_sem=recv_sems.at[slot],
            device_id=(peer, lane),
            device_id_type=MESH,
        )

    def sends_to(peer):
        return me < peer if later else me > peer

    def hears_from(peer):
        return me > peer if later else me < peer

    for peer in range(count):

        @pl.when(sends_to(peer))
        def _():
            link(peer, me).start()

    for peer in range(count):

        @pl.when(sends_to(peer))
        def _():
            link(peer, me).wait_send()

        @pl.when(hears_from(peer))
        def _():
            link(peer, peer).wait_recv()


def exchange(final, count, later, collective):
    shape = (count,) + final.shape
    return pl.pallas_call(
        functools.partial(exchange_kernel, count, later),
        out_shape=jax.ShapeDtypeStruct(shape, final.dtype),
        in_specs=[pl.BlockSpec(memory_space=pltpu.VMEM)],
        out_specs=pl.BlockSpec(memory_space=pltpu.VMEM),
        scratch_shapes=[
            pltpu.SemaphoreType.DMA((count,)),
            pltpu.SemaphoreType.DMA((count,)),
        ],
        compiler_params=pltpu.CompilerParams(collective_id=collective, has_side_effects=True),
    )(final)


def from_behind(block, axis, distance):
    devices = range(lax.axis_size(axis))
    route = [(i - distance, i) for i in devices if i - distance in devices]
    return lax.ppermute(block, axis, route)


def fetch_kernel(
    count, lanes, w_ref, g_ref, f_ref, w_all, g_all, f_got, w_send, w_recv, g_send, g_recv, own_sem, f_send, f_recv
):
    me = lax.axis_index("seq")
    lane = lax.axis_index("ch")
    half = count // 2
    core = me % 2
    ring = me // 2
    right = 2 * ((ring + 1) % half) + core
    left = 2 * ((ring + half - 1) % half) + core
    partner = me + 1 - 2 * core
    barrier = pltpu.get_barrier_semaphore()
    for peer in range(count):

        @pl.when(me != peer)
        def _():
            pl.semaphore_signal(barrier, inc=1, device_id=(peer, lane), device_id_type=MESH)

    for other in range(lanes):

        @pl.when(lane != other)
        def _():
            pl.semaphore_signal(barrier, inc=1, device_id=(me, other), device_id_type=MESH)

    pl.semaphore_wait(barrier, count - 1 + lanes - 1)

    def state_link(peer, slot):
        return pltpu.make_async_remote_copy(
            src_ref=f_ref,
            dst_ref=f_got.at[slot],
            send_sem=f_send.at[peer],
            recv_sem=f_recv.at[slot],
            device_id=(peer, lane),
            device_id_type=MESH,
        )

    for peer in range(count):

        @pl.when(me < peer)
        def _():
            state_link(peer, me).start()

    def grad_link(other):
        return pltpu.make_async_remote_copy(
            src_ref=g_ref,
            dst_ref=g_all.at[lane],
            send_sem=g_send.at[other],
            recv_sem=g_recv.at[lane],
            device_id=(me, other),
            device_id_type=MESH,
        )

    def grad_arrival(other):
        return pltpu.make_async_remote_copy(
            src_ref=g_ref,
            dst_ref=g_all.at[other],
            send_sem=g_send.at[other],
            recv_sem=g_recv.at[other],
            device_id=(me, other),
            device_id_type=MESH,
        )

    own_w = pltpu.make_async_copy(w_ref, w_all.at[me], own_sem.at[0])
    own_g = pltpu.make_async_copy(g_ref, g_all.at[lane], own_sem.at[1])
    own_w.start()
    own_g.start()

    sends = []
    pieces = w_recv.shape[0] // count
    depth = w_ref.shape[0] // pieces

    def rows(piece):
        return pl.ds(piece * depth, depth)

    def send(origin, piece, peer, own):
        source = w_ref.at[rows(piece)] if own else w_all.at[origin, rows(piece)]
        copy = pltpu.make_async_remote_copy(
            src_ref=source,
            dst_ref=w_all.at[origin, rows(piece)],
            send_sem=w_send.at[len(sends)],
            recv_sem=w_recv.at[origin * pieces + piece],
            device_id=(peer, lane),
            device_id_type=MESH,
        )
        copy.start()
        sends.append(copy)

    def arrived(origin, piece):
        pltpu.make_async_remote_copy(
            src_ref=w_all.at[origin, rows(piece)],
            dst_ref=w_all.at[origin, rows(piece)],
            send_sem=w_send.at[0],
            recv_sem=w_recv.at[origin * pieces + piece],
            device_id=(me, lane),
            device_id_type=MESH,
        ).wait_recv()

    def right_steps(piece):
        return half // 2 if piece < pieces // 2 else half - 1 - half // 2

    def left_steps(piece):
        return half - 1 - right_steps(piece)

    def right_origin(step):
        return 2 * ((ring - step + 1 + half) % half) + core

    def left_origin(step):
        return 2 * ((ring + step - 1) % half) + core

    longest = max(max(right_steps(p), left_steps(p)) for p in range(pieces))
    for piece in range(pieces):
        if right_steps(piece) >= 1:
            send(me, piece, right, True)
        if left_steps(piece) >= 1:
            send(me, piece, left, True)
        send(me, piece, partner, True)
    for other in range(lanes):

        @pl.when(lane != other)
        def _():
            grad_link(other).start()

    for step in range(2, longest + 2):
        for piece in range(pieces):
            if step <= right_steps(piece) + 1:
                origin = right_origin(step)
                arrived(origin, piece)
                if step <= right_steps(piece):
                    send(origin, piece, right, False)
                send(origin, piece, partner, False)
            if step <= left_steps(piece) + 1:
                origin = left_origin(step)
                arrived(origin, piece)
                if step <= left_steps(piece):
                    send(origin, piece, left, False)
                send(origin, piece, partner, False)

    for twin in range(half):
        for piece in range(pieces):
            arrived(2 * twin + 1 - core, piece)
    for copy in sends:
        copy.wait_send()
    for other in range(lanes):

        @pl.when(lane != other)
        def _():
            grad_link(other).wait_send()
            grad_arrival(other).wait_recv()

    for peer in range(count):

        @pl.when(me < peer)
        def _():
            state_link(peer, me).wait_send()

        @pl.when(me > peer)
        def _():
            state_link(peer, peer).wait_recv()

    own_w.wait()
    own_g.wait()


def fetch(out_weight, grad_out, final, count, lanes, pieces=4):
    half = count // 2
    sends = (half + half // 2 + (half - 1 - half // 2)) * pieces
    return pl.pallas_call(
        functools.partial(fetch_kernel, count, lanes),
        out_shape=(
            jax.ShapeDtypeStruct((count,) + out_weight.shape, out_weight.dtype),
            jax.ShapeDtypeStruct((lanes,) + grad_out.shape, grad_out.dtype),
            jax.ShapeDtypeStruct((count,) + final.shape, final.dtype),
        ),
        in_specs=[pl.BlockSpec(memory_space=pl.ANY)] * 2 + [pl.BlockSpec(memory_space=pltpu.VMEM)],
        out_specs=(
            pl.BlockSpec(memory_space=pl.ANY),
            pl.BlockSpec(memory_space=pl.ANY),
            pl.BlockSpec(memory_space=pltpu.VMEM),
        ),
        scratch_shapes=[
            pltpu.SemaphoreType.DMA((sends,)),
            pltpu.SemaphoreType.DMA((count * pieces,)),
            pltpu.SemaphoreType.DMA((lanes,)),
            pltpu.SemaphoreType.DMA((lanes,)),
            pltpu.SemaphoreType.DMA((2,)),
            pltpu.SemaphoreType.DMA((count,)),
            pltpu.SemaphoreType.DMA((count,)),
        ],
        compiler_params=pltpu.CompilerParams(collective_id=1, has_side_effects=True),
    )(out_weight, grad_out, final)


def per_device(query, key, value, short_taps, decay_rate, residue, skip_gain, out_weight, grad_out):
    tok_rows, chan_width = query.shape
    tap_count = short_taps.shape[0]
    mode_count = decay_rate.shape[0]
    highest = lax.Precision.HIGHEST
    count = lax.axis_size("seq")
    place = lax.axis_index("seq")

    lanes = lax.axis_size("ch")

    streams = jnp.stack([query, key, value])
    before = from_behind(streams[:, tok_rows - (tap_count - 1) :, :], "seq", 1)
    extended = jnp.concatenate([before, streams], axis=1).astype(jnp.float32)
    featured = jnp.zeros((3, tok_rows, chan_width), jnp.float32)
    for tap_index in range(tap_count):
        begin = tap_count - 1 - tap_index
        featured = (
            featured + short_taps[tap_index][:, None, :] * extended[:, begin : begin + tok_rows, :]
        )
    q_short = featured[0]
    k_short = featured[1]
    v_short = featured[2]
    gated = k_short * v_short

    width = mode_count * chan_width
    rate = decay_rate.reshape(1, width)
    mode_scale = (residue * jnp.sqrt(-jnp.expm1(-2.0 * decay_rate))).reshape(1, width)
    offsets = jnp.arange(tok_rows).astype(jnp.float32)[:, None]
    shrink = jnp.exp(-rate * offsets)
    grow = jnp.exp(rate * offsets)
    scaled_shrink = mode_scale * shrink
    scaled_grow = mode_scale * grow
    one_step = jnp.exp(-rate)
    block_decay = jnp.exp(-rate * tok_rows)
    rows = jnp.arange(tok_rows)
    lower = (rows[:, None] >= rows[None, :]).astype(jnp.float32)
    upper = (rows[:, None] <= rows[None, :]).astype(jnp.float32)

    def prefix(tri, weights, signal):
        spread = weights * jnp.concatenate([signal] * mode_count, axis=1)
        return jnp.dot(tri, spread, precision=highest, preferred_element_type=jnp.float32)

    def over_modes(table):
        total = table[:, :chan_width]
        for mode in range(1, mode_count):
            total = total + table[:, mode * chan_width : (mode + 1) * chan_width]
        return total

    source = jnp.arange(count)

    def entry(gap, got):
        span = (tok_rows * jnp.maximum(gap, 0)).astype(jnp.float32)[:, None]
        held = jnp.where((gap >= 0)[:, None], got.astype(jnp.float32), 0.0)
        return jnp.sum(jnp.exp(-rate * span) * held, axis=0, keepdims=True)

    fwd_sums = prefix(lower, grow, gated)
    fwd_final = (shrink[tok_rows - 1] * fwd_sums[tok_rows - 1]).astype(jnp.bfloat16)
    w_all, g_all, fwd_got = fetch(
        out_weight, grad_out, fwd_final.reshape(mode_count, chan_width), count, lanes
    )
    fwd_got = fwd_got.reshape(count, width)
    fwd_entry = entry(place - 1 - source, fwd_got) * one_step
    long_out = over_modes(scaled_shrink * (fwd_sums + fwd_entry)) + skip_gain[None, :] * gated
    mixer = (q_short * long_out).astype(jnp.bfloat16)
    parts = jnp.einsum("tr,jrc->jtc", mixer, w_all, preferred_element_type=jnp.float32)
    parts = parts.astype(jnp.bfloat16)
    parts, g_all, w_all = lax.optimization_barrier((parts, g_all, w_all))
    received = lax.all_to_all(parts, "ch", 0, 0, tiled=True)
    mixed = jnp.sum(received.astype(jnp.float32), axis=0).astype(jnp.bfloat16)

    grad_mixer = jnp.einsum("jtc,jrc->tr", g_all, w_all, preferred_element_type=jnp.float32)
    grad_long = grad_mixer * q_short
    bwd_sums = prefix(upper, shrink, grad_long)
    bwd_final = bwd_sums[0].astype(jnp.bfloat16).reshape(mode_count, chan_width)
    bwd_got = exchange(bwd_final, count, False, 3).reshape(count, width)
    bwd_entry = entry(source - place - 1, bwd_got) * block_decay

    grad_qshort = grad_mixer * long_out
    grad_gated = (
        over_modes(scaled_grow * (bwd_sums + bwd_entry)) + skip_gain[None, :] * grad_long
    )
    grad_stack = jnp.stack([grad_qshort, grad_gated * v_short, grad_gated * k_short])
    after = from_behind(grad_stack[:, : tap_count - 1, :], "seq", -1)
    extended_back = jnp.concatenate([grad_stack, after], axis=1)
    grads = jnp.zeros((3, tok_rows, chan_width), jnp.float32)
    for tap_index in range(tap_count):
        grads = (
            grads
            + short_taps[tap_index][:, None, :]
            * extended_back[:, tap_index : tap_index + tok_rows, :]
        )
    grads = grads.astype(jnp.bfloat16)
    return (mixed, grads[0], grads[1], grads[2])


def solution(mesh):
    in_specs = (
        P("seq", "ch"),
        P("seq", "ch"),
        P("seq", "ch"),
        P(None, None, "ch"),
        P(None, "ch"),
        P(None, "ch"),
        P("ch"),
        P("ch", "seq"),
        P("seq", "ch"),
    )
    out_specs = (P("seq", "ch"), P("seq", "ch"), P("seq", "ch"), P("seq", "ch"))
    return jax.shard_map(
        per_device, mesh=mesh, in_specs=in_specs, out_specs=out_specs, check_vma=False
    )
```

```python
import functools

import jax
import jax.numpy as jnp
from jax import lax
from jax.experimental import pallas as pl
from jax.experimental.pallas import tpu as pltpu
from jax.sharding import PartitionSpec as P

MESH = pl.DeviceIdType.MESH


def exchange_kernel(count, later, final_ref, got_ref, send_sems, recv_sems):
    me = lax.axis_index("seq")
    lane = lax.axis_index("ch")
    barrier = pltpu.get_barrier_semaphore()
    for peer in range(count):

        @pl.when(me != peer)
        def _():
            pl.semaphore_signal(barrier, inc=1, device_id=(peer, lane), device_id_type=MESH)

    pl.semaphore_wait(barrier, count - 1)

    def link(peer, slot):
        return pltpu.make_async_remote_copy(
            src_ref=final_ref,
            dst_ref=got_ref.at[slot],
            send_sem=send_sems.at[peer],
            recv_sem=recv_sems.at[slot],
            device_id=(peer, lane),
            device_id_type=MESH,
        )

    def sends_to(peer):
        return me < peer if later else me > peer

    def hears_from(peer):
        return me > peer if later else me < peer

    for peer in range(count):

        @pl.when(sends_to(peer))
        def _():
            link(peer, me).start()

    for peer in range(count):

        @pl.when(sends_to(peer))
        def _():
            link(peer, me).wait_send()

        @pl.when(hears_from(peer))
        def _():
            link(peer, peer).wait_recv()


def exchange(final, count, later, collective):
    shape = (count,) + final.shape
    return pl.pallas_call(
        functools.partial(exchange_kernel, count, later),
        out_shape=jax.ShapeDtypeStruct(shape, final.dtype),
        in_specs=[pl.BlockSpec(memory_space=pltpu.VMEM)],
        out_specs=pl.BlockSpec(memory_space=pltpu.VMEM),
        scratch_shapes=[
            pltpu.SemaphoreType.DMA((count,)),
            pltpu.SemaphoreType.DMA((count,)),
        ],
        compiler_params=pltpu.CompilerParams(collective_id=collective, has_side_effects=True),
    )(final)


def from_behind(block, axis, distance):
    devices = range(lax.axis_size(axis))
    route = [(i - distance, i) for i in devices if i - distance in devices]
    return lax.ppermute(block, axis, route)


def fetch_kernel(
    count, lanes, w_ref, g_ref, f_ref, w_all, g_all, f_got, w_send, w_recv, g_send, g_recv, own_sem, f_send, f_recv
):
    me = lax.axis_index("seq")
    lane = lax.axis_index("ch")
    half = count // 2
    core = me % 2
    ring = me // 2
    right = 2 * ((ring + 1) % half) + core
    left = 2 * ((ring + half - 1) % half) + core
    partner = me + 1 - 2 * core
    barrier = pltpu.get_barrier_semaphore()
    for peer in range(count):

        @pl.when(me != peer)
        def _():
            pl.semaphore_signal(barrier, inc=1, device_id=(peer, lane), device_id_type=MESH)

    for other in range(lanes):

        @pl.when(lane != other)
        def _():
            pl.semaphore_signal(barrier, inc=1, device_id=(me, other), device_id_type=MESH)

    pl.semaphore_wait(barrier, count - 1 + lanes - 1)

    def state_link(peer, slot):
        return pltpu.make_async_remote_copy(
            src_ref=f_ref,
            dst_ref=f_got.at[slot],
            send_sem=f_send.at[peer],
            recv_sem=f_recv.at[slot],
            device_id=(peer, lane),
            device_id_type=MESH,
        )

    for peer in range(count):

        @pl.when(me < peer)
        def _():
            state_link(peer, me).start()

    def grad_link(other):
        return pltpu.make_async_remote_copy(
            src_ref=g_ref,
            dst_ref=g_all.at[lane],
            send_sem=g_send.at[other],
            recv_sem=g_recv.at[lane],
            device_id=(me, other),
            device_id_type=MESH,
        )

    def grad_arrival(other):
        return pltpu.make_async_remote_copy(
            src_ref=g_ref,
            dst_ref=g_all.at[other],
            send_sem=g_send.at[other],
            recv_sem=g_recv.at[other],
            device_id=(me, other),
            device_id_type=MESH,
        )

    for other in range(lanes):

        @pl.when(lane != other)
        def _():
            grad_link(other).start()

    own_w = pltpu.make_async_copy(w_ref, w_all.at[me], own_sem.at[0])
    own_g = pltpu.make_async_copy(g_ref, g_all.at[lane], own_sem.at[1])
    own_w.start()
    own_g.start()

    sends = []
    pieces = w_recv.shape[0] // count
    depth = w_ref.shape[0] // pieces

    def rows(piece):
        return pl.ds(piece * depth, depth)

    def send(origin, piece, peer, own):
        source = w_ref.at[rows(piece)] if own else w_all.at[origin, rows(piece)]
        copy = pltpu.make_async_remote_copy(
            src_ref=source,
            dst_ref=w_all.at[origin, rows(piece)],
            send_sem=w_send.at[len(sends)],
            recv_sem=w_recv.at[origin * pieces + piece],
            device_id=(peer, lane),
            device_id_type=MESH,
        )
        copy.start()
        sends.append(copy)

    def arrived(origin, piece):
        pltpu.make_async_remote_copy(
            src_ref=w_all.at[origin, rows(piece)],
            dst_ref=w_all.at[origin, rows(piece)],
            send_sem=w_send.at[0],
            recv_sem=w_recv.at[origin * pieces + piece],
            device_id=(me, lane),
            device_id_type=MESH,
        ).wait_recv()

    def right_steps(piece):
        return half // 2 if piece < pieces // 2 else half - 1 - half // 2

    def left_steps(piece):
        return half - 1 - right_steps(piece)

    def right_origin(step):
        return 2 * ((ring - step + 1 + half) % half) + core

    def left_origin(step):
        return 2 * ((ring + step - 1) % half) + core

    longest = max(max(right_steps(p), left_steps(p)) for p in range(pieces))
    for piece in range(pieces):
        if right_steps(piece) >= 1:
            send(me, piece, right, True)
        if left_steps(piece) >= 1:
            send(me, piece, left, True)
        send(me, piece, partner, True)
    for step in range(2, longest + 2):
        for piece in range(pieces):
            if step <= right_steps(piece) + 1:
                origin = right_origin(step)
                arrived(origin, piece)
                if step <= right_steps(piece):
                    send(origin, piece, right, False)
                send(origin, piece, partner, False)
            if step <= left_steps(piece) + 1:
                origin = left_origin(step)
                arrived(origin, piece)
                if step <= left_steps(piece):
                    send(origin, piece, left, False)
                send(origin, piece, partner, False)

    for twin in range(half):
        for piece in range(pieces):
            arrived(2 * twin + 1 - core, piece)
    for copy in sends:
        copy.wait_send()
    for other in range(lanes):

        @pl.when(lane != other)
        def _():
            grad_link(other).wait_send()
            grad_arrival(other).wait_recv()

    for peer in range(count):

        @pl.when(me < peer)
        def _():
            state_link(peer, me).wait_send()

        @pl.when(me > peer)
        def _():
            state_link(peer, peer).wait_recv()

    own_w.wait()
    own_g.wait()


def fetch(out_weight, grad_out, final, count, lanes, pieces=2):
    half = count // 2
    sends = (half + half // 2 + (half - 1 - half // 2)) * pieces
    return pl.pallas_call(
        functools.partial(fetch_kernel, count, lanes),
        out_shape=(
            jax.ShapeDtypeStruct((count,) + out_weight.shape, out_weight.dtype),
            jax.ShapeDtypeStruct((lanes,) + grad_out.shape, grad_out.dtype),
            jax.ShapeDtypeStruct((count,) + final.shape, final.dtype),
        ),
        in_specs=[pl.BlockSpec(memory_space=pl.ANY)] * 2 + [pl.BlockSpec(memory_space=pltpu.VMEM)],
        out_specs=(
            pl.BlockSpec(memory_space=pl.ANY),
            pl.BlockSpec(memory_space=pl.ANY),
            pl.BlockSpec(memory_space=pltpu.VMEM),
        ),
        scratch_shapes=[
            pltpu.SemaphoreType.DMA((sends,)),
            pltpu.SemaphoreType.DMA((count * pieces,)),
            pltpu.SemaphoreType.DMA((lanes,)),
            pltpu.SemaphoreType.DMA((lanes,)),
            pltpu.SemaphoreType.DMA((2,)),
            pltpu.SemaphoreType.DMA((count,)),
            pltpu.SemaphoreType.DMA((count,)),
        ],
        compiler_params=pltpu.CompilerParams(collective_id=1, has_side_effects=True),
    )(out_weight, grad_out, final)


def per_device(query, key, value, short_taps, decay_rate, residue, skip_gain, out_weight, grad_out):
    tok_rows, chan_width = query.shape
    tap_count = short_taps.shape[0]
    mode_count = decay_rate.shape[0]
    highest = lax.Precision.HIGHEST
    count = lax.axis_size("seq")
    place = lax.axis_index("seq")

    lanes = lax.axis_size("ch")

    streams = jnp.stack([query, key, value])
    before = from_behind(streams[:, tok_rows - (tap_count - 1) :, :], "seq", 1)
    extended = jnp.concatenate([before, streams], axis=1).astype(jnp.float32)
    featured = jnp.zeros((3, tok_rows, chan_width), jnp.float32)
    for tap_index in range(tap_count):
        begin = tap_count - 1 - tap_index
        featured = (
            featured + short_taps[tap_index][:, None, :] * extended[:, begin : begin + tok_rows, :]
        )
    q_short = featured[0]
    k_short = featured[1]
    v_short = featured[2]
    gated = k_short * v_short

    width = mode_count * chan_width
    rate = decay_rate.reshape(1, width)
    mode_scale = (residue * jnp.sqrt(-jnp.expm1(-2.0 * decay_rate))).reshape(1, width)
    offsets = jnp.arange(tok_rows).astype(jnp.float32)[:, None]
    shrink = jnp.exp(-rate * offsets)
    grow = jnp.exp(rate * offsets)
    scaled_shrink = mode_scale * shrink
    scaled_grow = mode_scale * grow
    one_step = jnp.exp(-rate)
    block_decay = jnp.exp(-rate * tok_rows)
    rows = jnp.arange(tok_rows)
    lower = (rows[:, None] >= rows[None, :]).astype(jnp.float32)
    upper = (rows[:, None] <= rows[None, :]).astype(jnp.float32)

    def prefix(tri, weights, signal):
        spread = weights * jnp.concatenate([signal] * mode_count, axis=1)
        return jnp.dot(tri, spread, precision=highest, preferred_element_type=jnp.float32)

    def over_modes(table):
        total = table[:, :chan_width]
        for mode in range(1, mode_count):
            total = total + table[:, mode * chan_width : (mode + 1) * chan_width]
        return total

    source = jnp.arange(count)

    def entry(gap, got):
        span = (tok_rows * jnp.maximum(gap, 0)).astype(jnp.float32)[:, None]
        held = jnp.where((gap >= 0)[:, None], got.astype(jnp.float32), 0.0)
        return jnp.sum(jnp.exp(-rate * span) * held, axis=0, keepdims=True)

    fwd_sums = prefix(lower, grow, gated)
    fwd_final = (shrink[tok_rows - 1] * fwd_sums[tok_rows - 1]).astype(jnp.bfloat16)
    w_all, g_all, fwd_got = fetch(
        out_weight, grad_out, fwd_final.reshape(mode_count, chan_width), count, lanes
    )
    fwd_got = fwd_got.reshape(count, width)
    fwd_entry = entry(place - 1 - source, fwd_got) * one_step
    long_out = over_modes(scaled_shrink * (fwd_sums + fwd_entry)) + skip_gain[None, :] * gated
    mixer = (q_short * long_out).astype(jnp.bfloat16)
    parts = jnp.einsum("tr,jrc->jtc", mixer, w_all, preferred_element_type=jnp.float32)
    parts = parts.astype(jnp.bfloat16)
    parts, g_all, w_all = lax.optimization_barrier((parts, g_all, w_all))
    received = lax.all_to_all(parts, "ch", 0, 0, tiled=True)
    mixed = jnp.sum(received.astype(jnp.float32), axis=0).astype(jnp.bfloat16)

    grad_mixer = jnp.einsum("jtc,jrc->tr", g_all, w_all, preferred_element_type=jnp.float32)
    grad_long = grad_mixer * q_short
    bwd_sums = prefix(upper, shrink, grad_long)
    bwd_final = bwd_sums[0].astype(jnp.bfloat16).reshape(mode_count, chan_width)
    bwd_got = exchange(bwd_final, count, False, 3).reshape(count, width)
    bwd_entry = entry(source - place - 1, bwd_got) * block_decay

    grad_qshort = grad_mixer * long_out
    grad_gated = (
        over_modes(scaled_grow * (bwd_sums + bwd_entry)) + skip_gain[None, :] * grad_long
    )
    grad_stack = jnp.stack([grad_qshort, grad_gated * v_short, grad_gated * k_short])
    after = from_behind(grad_stack[:, : tap_count - 1, :], "seq", -1)
    extended_back = jnp.concatenate([grad_stack, after], axis=1)
    grads = jnp.zeros((3, tok_rows, chan_width), jnp.float32)
    for tap_index in range(tap_count):
        grads = (
            grads
            + short_taps[tap_index][:, None, :]
            * extended_back[:, tap_index : tap_index + tok_rows, :]
        )
    grads = grads.astype(jnp.bfloat16)
    return (mixed, grads[0], grads[1], grads[2])


def solution(mesh):
    in_specs = (
        P("seq", "ch"),
        P("seq", "ch"),
        P("seq", "ch"),
        P(None, None, "ch"),
        P(None, "ch"),
        P(None, "ch"),
        P("ch"),
        P("ch", "seq"),
        P("seq", "ch"),
    )
    out_specs = (P("seq", "ch"), P("seq", "ch"), P("seq", "ch"), P("seq", "ch"))
    return jax.shard_map(
        per_device, mesh=mesh, in_specs=in_specs, out_specs=out_specs, check_vma=False
    )
```

```python
import functools

import jax
import jax.numpy as jnp
from jax import lax
from jax.experimental import pallas as pl
from jax.experimental.pallas import tpu as pltpu
from jax.sharding import PartitionSpec as P

MESH = pl.DeviceIdType.MESH


def exchange_kernel(count, later, final_ref, got_ref, send_sems, recv_sems):
    me = lax.axis_index("seq")
    lane = lax.axis_index("ch")
    barrier = pltpu.get_barrier_semaphore()
    for peer in range(count):

        @pl.when(me != peer)
        def _():
            pl.semaphore_signal(barrier, inc=1, device_id=(peer, lane), device_id_type=MESH)

    pl.semaphore_wait(barrier, count - 1)

    def link(peer, slot):
        return pltpu.make_async_remote_copy(
            src_ref=final_ref,
            dst_ref=got_ref.at[slot],
            send_sem=send_sems.at[peer],
            recv_sem=recv_sems.at[slot],
            device_id=(peer, lane),
            device_id_type=MESH,
        )

    def sends_to(peer):
        return me < peer if later else me > peer

    def hears_from(peer):
        return me > peer if later else me < peer

    for peer in range(count):

        @pl.when(sends_to(peer))
        def _():
            link(peer, me).start()

    for peer in range(count):

        @pl.when(sends_to(peer))
        def _():
            link(peer, me).wait_send()

        @pl.when(hears_from(peer))
        def _():
            link(peer, peer).wait_recv()


def exchange(final, count, later, collective):
    shape = (count,) + final.shape
    return pl.pallas_call(
        functools.partial(exchange_kernel, count, later),
        out_shape=jax.ShapeDtypeStruct(shape, final.dtype),
        in_specs=[pl.BlockSpec(memory_space=pltpu.VMEM)],
        out_specs=pl.BlockSpec(memory_space=pltpu.VMEM),
        scratch_shapes=[
            pltpu.SemaphoreType.DMA((count,)),
            pltpu.SemaphoreType.DMA((count,)),
        ],
        compiler_params=pltpu.CompilerParams(collective_id=collective, has_side_effects=True),
    )(final)


def from_behind(block, axis, distance):
    devices = range(lax.axis_size(axis))
    route = [(i - distance, i) for i in devices if i - distance in devices]
    return lax.ppermute(block, axis, route)


def fetch_kernel(
    count, lanes, w_ref, g_ref, f_ref, w_all, g_all, f_got, w_send, w_recv, g_send, g_recv, own_sem, f_send, f_recv
):
    me = lax.axis_index("seq")
    lane = lax.axis_index("ch")
    half = count // 2
    core = me % 2
    ring = me // 2
    right = 2 * ((ring + 1) % half) + core
    left = 2 * ((ring + half - 1) % half) + core
    partner = me + 1 - 2 * core
    barrier = pltpu.get_barrier_semaphore()
    for peer in range(count):

        @pl.when(me != peer)
        def _():
            pl.semaphore_signal(barrier, inc=1, device_id=(peer, lane), device_id_type=MESH)

    for other in range(lanes):

        @pl.when(lane != other)
        def _():
            pl.semaphore_signal(barrier, inc=1, device_id=(me, other), device_id_type=MESH)

    pl.semaphore_wait(barrier, count - 1 + lanes - 1)

    def state_link(peer, slot):
        return pltpu.make_async_remote_copy(
            src_ref=f_ref,
            dst_ref=f_got.at[slot],
            send_sem=f_send.at[peer],
            recv_sem=f_recv.at[slot],
            device_id=(peer, lane),
            device_id_type=MESH,
        )

    for peer in range(count):

        @pl.when(me < peer)
        def _():
            state_link(peer, me).start()

    def grad_link(other):
        return pltpu.make_async_remote_copy(
            src_ref=g_ref,
            dst_ref=g_all.at[lane],
            send_sem=g_send.at[other],
            recv_sem=g_recv.at[lane],
            device_id=(me, other),
            device_id_type=MESH,
        )

    def grad_arrival(other):
        return pltpu.make_async_remote_copy(
            src_ref=g_ref,
            dst_ref=g_all.at[other],
            send_sem=g_send.at[other],
            recv_sem=g_recv.at[other],
            device_id=(me, other),
            device_id_type=MESH,
        )

    for other in range(lanes):

        @pl.when(lane != other)
        def _():
            grad_link(other).start()


    sends = []
    pieces = w_recv.shape[0] // count
    depth = w_ref.shape[0] // pieces

    def rows(piece):
        return pl.ds(piece * depth, depth)

    def send(origin, piece, peer, own):
        source = w_ref.at[rows(piece)] if own else w_all.at[origin, rows(piece)]
        copy = pltpu.make_async_remote_copy(
            src_ref=source,
            dst_ref=w_all.at[origin, rows(piece)],
            send_sem=w_send.at[len(sends)],
            recv_sem=w_recv.at[origin * pieces + piece],
            device_id=(peer, lane),
            device_id_type=MESH,
        )
        copy.start()
        sends.append(copy)

    def arrived(origin, piece):
        pltpu.make_async_remote_copy(
            src_ref=w_all.at[origin, rows(piece)],
            dst_ref=w_all.at[origin, rows(piece)],
            send_sem=w_send.at[0],
            recv_sem=w_recv.at[origin * pieces + piece],
            device_id=(me, lane),
            device_id_type=MESH,
        ).wait_recv()

    def right_steps(piece):
        return half // 2 if piece < pieces // 2 else half - 1 - half // 2

    def left_steps(piece):
        return half - 1 - right_steps(piece)

    def right_origin(step):
        return 2 * ((ring - step + 1 + half) % half) + core

    def left_origin(step):
        return 2 * ((ring + step - 1) % half) + core

    longest = max(max(right_steps(p), left_steps(p)) for p in range(pieces))
    for piece in range(pieces):
        if right_steps(piece) >= 1:
            send(me, piece, right, True)
        if left_steps(piece) >= 1:
            send(me, piece, left, True)
        send(me, piece, partner, True)
    own_w = pltpu.make_async_copy(w_ref, w_all.at[me], own_sem.at[0])
    own_g = pltpu.make_async_copy(g_ref, g_all.at[lane], own_sem.at[1])
    own_w.start()
    own_g.start()
    for step in range(2, longest + 2):
        for piece in range(pieces):
            if step <= right_steps(piece) + 1:
                origin = right_origin(step)
                arrived(origin, piece)
                if step <= right_steps(piece):
                    send(origin, piece, right, False)
                send(origin, piece, partner, False)
            if step <= left_steps(piece) + 1:
                origin = left_origin(step)
                arrived(origin, piece)
                if step <= left_steps(piece):
                    send(origin, piece, left, False)
                send(origin, piece, partner, False)

    for twin in range(half):
        for piece in range(pieces):
            arrived(2 * twin + 1 - core, piece)
    for copy in sends:
        copy.wait_send()
    for other in range(lanes):

        @pl.when(lane != other)
        def _():
            grad_link(other).wait_send()
            grad_arrival(other).wait_recv()

    for peer in range(count):

        @pl.when(me < peer)
        def _():
            state_link(peer, me).wait_send()

        @pl.when(me > peer)
        def _():
            state_link(peer, peer).wait_recv()

    own_w.wait()
    own_g.wait()


def fetch(out_weight, grad_out, final, count, lanes, pieces=4):
    half = count // 2
    sends = (half + half // 2 + (half - 1 - half // 2)) * pieces
    return pl.pallas_call(
        functools.partial(fetch_kernel, count, lanes),
        out_shape=(
            jax.ShapeDtypeStruct((count,) + out_weight.shape, out_weight.dtype),
            jax.ShapeDtypeStruct((lanes,) + grad_out.shape, grad_out.dtype),
            jax.ShapeDtypeStruct((count,) + final.shape, final.dtype),
        ),
        in_specs=[pl.BlockSpec(memory_space=pl.ANY)] * 2 + [pl.BlockSpec(memory_space=pltpu.VMEM)],
        out_specs=(
            pl.BlockSpec(memory_space=pl.ANY),
            pl.BlockSpec(memory_space=pl.ANY),
            pl.BlockSpec(memory_space=pltpu.VMEM),
        ),
        scratch_shapes=[
            pltpu.SemaphoreType.DMA((sends,)),
            pltpu.SemaphoreType.DMA((count * pieces,)),
            pltpu.SemaphoreType.DMA((lanes,)),
            pltpu.SemaphoreType.DMA((lanes,)),
            pltpu.SemaphoreType.DMA((2,)),
            pltpu.SemaphoreType.DMA((count,)),
            pltpu.SemaphoreType.DMA((count,)),
        ],
        compiler_params=pltpu.CompilerParams(collective_id=1, has_side_effects=True),
    )(out_weight, grad_out, final)


def per_device(query, key, value, short_taps, decay_rate, residue, skip_gain, out_weight, grad_out):
    tok_rows, chan_width = query.shape
    tap_count = short_taps.shape[0]
    mode_count = decay_rate.shape[0]
    highest = lax.Precision.HIGHEST
    count = lax.axis_size("seq")
    place = lax.axis_index("seq")

    lanes = lax.axis_size("ch")

    streams = jnp.stack([query, key, value])
    before = from_behind(streams[:, tok_rows - (tap_count - 1) :, :], "seq", 1)
    extended = jnp.concatenate([before, streams], axis=1).astype(jnp.float32)
    featured = jnp.zeros((3, tok_rows, chan_width), jnp.float32)
    for tap_index in range(tap_count):
        begin = tap_count - 1 - tap_index
        featured = (
            featured + short_taps[tap_index][:, None, :] * extended[:, begin : begin + tok_rows, :]
        )
    q_short = featured[0]
    k_short = featured[1]
    v_short = featured[2]
    gated = k_short * v_short

    width = mode_count * chan_width
    rate = decay_rate.reshape(1, width)
    mode_scale = (residue * jnp.sqrt(-jnp.expm1(-2.0 * decay_rate))).reshape(1, width)
    offsets = jnp.arange(tok_rows).astype(jnp.float32)[:, None]
    shrink = jnp.exp(-rate * offsets)
    grow = jnp.exp(rate * offsets)
    scaled_shrink = mode_scale * shrink
    scaled_grow = mode_scale * grow
    one_step = jnp.exp(-rate)
    block_decay = jnp.exp(-rate * tok_rows)
    rows = jnp.arange(tok_rows)
    lower = (rows[:, None] >= rows[None, :]).astype(jnp.float32)
    upper = (rows[:, None] <= rows[None, :]).astype(jnp.float32)

    def prefix(tri, weights, signal):
        spread = weights * jnp.concatenate([signal] * mode_count, axis=1)
        return jnp.dot(tri, spread, precision=highest, preferred_element_type=jnp.float32)

    def over_modes(table):
        total = table[:, :chan_width]
        for mode in range(1, mode_count):
            total = total + table[:, mode * chan_width : (mode + 1) * chan_width]
        return total

    source = jnp.arange(count)

    def entry(gap, got):
        span = (tok_rows * jnp.maximum(gap, 0)).astype(jnp.float32)[:, None]
        held = jnp.where((gap >= 0)[:, None], got.astype(jnp.float32), 0.0)
        return jnp.sum(jnp.exp(-rate * span) * held, axis=0, keepdims=True)

    fwd_sums = prefix(lower, grow, gated)
    fwd_final = (shrink[tok_rows - 1] * fwd_sums[tok_rows - 1]).astype(jnp.bfloat16)
    w_all, g_all, fwd_got = fetch(
        out_weight, grad_out, fwd_final.reshape(mode_count, chan_width), count, lanes
    )
    fwd_got = fwd_got.reshape(count, width)
    fwd_entry = entry(place - 1 - source, fwd_got) * one_step
    long_out = over_modes(scaled_shrink * (fwd_sums + fwd_entry)) + skip_gain[None, :] * gated
    mixer = (q_short * long_out).astype(jnp.bfloat16)
    parts = jnp.einsum("tr,jrc->jtc", mixer, w_all, preferred_element_type=jnp.float32)
    parts = parts.astype(jnp.bfloat16)
    parts, g_all, w_all = lax.optimization_barrier((parts, g_all, w_all))
    received = lax.all_to_all(parts, "ch", 0, 0, tiled=True)
    mixed = jnp.sum(received.astype(jnp.float32), axis=0).astype(jnp.bfloat16)

    grad_mixer = jnp.einsum("jtc,jrc->tr", g_all, w_all, preferred_element_type=jnp.float32)
    grad_long = grad_mixer * q_short
    bwd_sums = prefix(upper, shrink, grad_long)
    bwd_final = bwd_sums[0].astype(jnp.bfloat16).reshape(mode_count, chan_width)
    bwd_got = exchange(bwd_final, count, False, 3).reshape(count, width)
    bwd_entry = entry(source - place - 1, bwd_got) * block_decay

    grad_qshort = grad_mixer * long_out
    grad_gated = (
        over_modes(scaled_grow * (bwd_sums + bwd_entry)) + skip_gain[None, :] * grad_long
    )
    grad_stack = jnp.stack([grad_qshort, grad_gated * v_short, grad_gated * k_short])
    after = from_behind(grad_stack[:, : tap_count - 1, :], "seq", -1)
    extended_back = jnp.concatenate([grad_stack, after], axis=1)
    grads = jnp.zeros((3, tok_rows, chan_width), jnp.float32)
    for tap_index in range(tap_count):
        grads = (
            grads
            + short_taps[tap_index][:, None, :]
            * extended_back[:, tap_index : tap_index + tok_rows, :]
        )
    grads = grads.astype(jnp.bfloat16)
    return (mixed, grads[0], grads[1], grads[2])


def solution(mesh):
    in_specs = (
        P("seq", "ch"),
        P("seq", "ch"),
        P("seq", "ch"),
        P(None, None, "ch"),
        P(None, "ch"),
        P(None, "ch"),
        P("ch"),
        P("ch", "seq"),
        P("seq", "ch"),
    )
    out_specs = (P("seq", "ch"), P("seq", "ch"), P("seq", "ch"), P("seq", "ch"))
    return jax.shard_map(
        per_device, mesh=mesh, in_specs=in_specs, out_specs=out_specs, check_vma=False
    )
```

```python
import functools

import jax
import jax.numpy as jnp
from jax import lax
from jax.experimental import pallas as pl
from jax.experimental.pallas import tpu as pltpu
from jax.sharding import PartitionSpec as P

MESH = pl.DeviceIdType.MESH


def exchange_kernel(count, later, final_ref, got_ref, send_sems, recv_sems):
    me = lax.axis_index("seq")
    lane = lax.axis_index("ch")
    barrier = pltpu.get_barrier_semaphore()
    for peer in range(count):

        @pl.when(me != peer)
        def _():
            pl.semaphore_signal(barrier, inc=1, device_id=(peer, lane), device_id_type=MESH)

    pl.semaphore_wait(barrier, count - 1)

    def link(peer, slot):
        return pltpu.make_async_remote_copy(
            src_ref=final_ref,
            dst_ref=got_ref.at[slot],
            send_sem=send_sems.at[peer],
            recv_sem=recv_sems.at[slot],
            device_id=(peer, lane),
            device_id_type=MESH,
        )

    def sends_to(peer):
        return me < peer if later else me > peer

    def hears_from(peer):
        return me > peer if later else me < peer

    for peer in range(count):

        @pl.when(sends_to(peer))
        def _():
            link(peer, me).start()

    for peer in range(count):

        @pl.when(sends_to(peer))
        def _():
            link(peer, me).wait_send()

        @pl.when(hears_from(peer))
        def _():
            link(peer, peer).wait_recv()


def exchange(final, count, later, collective):
    shape = (count,) + final.shape
    return pl.pallas_call(
        functools.partial(exchange_kernel, count, later),
        out_shape=jax.ShapeDtypeStruct(shape, final.dtype),
        in_specs=[pl.BlockSpec(memory_space=pltpu.VMEM)],
        out_specs=pl.BlockSpec(memory_space=pltpu.VMEM),
        scratch_shapes=[
            pltpu.SemaphoreType.DMA((count,)),
            pltpu.SemaphoreType.DMA((count,)),
        ],
        compiler_params=pltpu.CompilerParams(collective_id=collective, has_side_effects=True),
    )(final)


def from_behind(block, axis, distance):
    devices = range(lax.axis_size(axis))
    route = [(i - distance, i) for i in devices if i - distance in devices]
    return lax.ppermute(block, axis, route)


def fetch_kernel(
    count, lanes, w_ref, g_ref, f_ref, w_all, g_all, f_got, w_send, w_recv, g_send, g_recv, own_sem, f_send, f_recv
):
    me = lax.axis_index("seq")
    lane = lax.axis_index("ch")
    half = count // 2
    core = me % 2
    ring = me // 2
    right = 2 * ((ring + 1) % half) + core
    left = 2 * ((ring + half - 1) % half) + core
    partner = me + 1 - 2 * core
    barrier = pltpu.get_barrier_semaphore()
    for peer in range(count):

        @pl.when(me != peer)
        def _():
            pl.semaphore_signal(barrier, inc=1, device_id=(peer, lane), device_id_type=MESH)

    for other in range(lanes):

        @pl.when(lane != other)
        def _():
            pl.semaphore_signal(barrier, inc=1, device_id=(me, other), device_id_type=MESH)

    pl.semaphore_wait(barrier, count - 1 + lanes - 1)

    def state_link(peer, slot):
        return pltpu.make_async_remote_copy(
            src_ref=f_ref,
            dst_ref=f_got.at[slot],
            send_sem=f_send.at[peer],
            recv_sem=f_recv.at[slot],
            device_id=(peer, lane),
            device_id_type=MESH,
        )

    def grad_link(other):
        return pltpu.make_async_remote_copy(
            src_ref=g_ref,
            dst_ref=g_all.at[lane],
            send_sem=g_send.at[other],
            recv_sem=g_recv.at[lane],
            device_id=(me, other),
            device_id_type=MESH,
        )

    def grad_arrival(other):
        return pltpu.make_async_remote_copy(
            src_ref=g_ref,
            dst_ref=g_all.at[other],
            send_sem=g_send.at[other],
            recv_sem=g_recv.at[other],
            device_id=(me, other),
            device_id_type=MESH,
        )

    for other in range(lanes):

        @pl.when(lane != other)
        def _():
            grad_link(other).start()

    own_w = pltpu.make_async_copy(w_ref, w_all.at[me], own_sem.at[0])
    own_g = pltpu.make_async_copy(g_ref, g_all.at[lane], own_sem.at[1])
    own_w.start()
    own_g.start()

    sends = []
    pieces = w_recv.shape[0] // count
    depth = w_ref.shape[0] // pieces

    def rows(piece):
        return pl.ds(piece * depth, depth)

    def send(origin, piece, peer, own):
        source = w_ref.at[rows(piece)] if own else w_all.at[origin, rows(piece)]
        copy = pltpu.make_async_remote_copy(
            src_ref=source,
            dst_ref=w_all.at[origin, rows(piece)],
            send_sem=w_send.at[len(sends)],
            recv_sem=w_recv.at[origin * pieces + piece],
            device_id=(peer, lane),
            device_id_type=MESH,
        )
        copy.start()
        sends.append(copy)

    def arrived(origin, piece):
        pltpu.make_async_remote_copy(
            src_ref=w_all.at[origin, rows(piece)],
            dst_ref=w_all.at[origin, rows(piece)],
            send_sem=w_send.at[0],
            recv_sem=w_recv.at[origin * pieces + piece],
            device_id=(me, lane),
            device_id_type=MESH,
        ).wait_recv()

    def right_steps(piece):
        return half // 2 if piece < pieces // 2 else half - 1 - half // 2

    def left_steps(piece):
        return half - 1 - right_steps(piece)

    def right_origin(step):
        return 2 * ((ring - step + 1 + half) % half) + core

    def left_origin(step):
        return 2 * ((ring + step - 1) % half) + core

    longest = max(max(right_steps(p), left_steps(p)) for p in range(pieces))
    for piece in range(pieces):
        if right_steps(piece) >= 1:
            send(me, piece, right, True)
        if left_steps(piece) >= 1:
            send(me, piece, left, True)
        send(me, piece, partner, True)
    for peer in range(count):

        @pl.when(me < peer)
        def _():
            state_link(peer, me).start()

    for step in range(2, longest + 2):
        for piece in range(pieces):
            if step <= right_steps(piece) + 1:
                origin = right_origin(step)
                arrived(origin, piece)
                if step <= right_steps(piece):
                    send(origin, piece, right, False)
                send(origin, piece, partner, False)
            if step <= left_steps(piece) + 1:
                origin = left_origin(step)
                arrived(origin, piece)
                if step <= left_steps(piece):
                    send(origin, piece, left, False)
                send(origin, piece, partner, False)

    for twin in range(half):
        for piece in range(pieces):
            arrived(2 * twin + 1 - core, piece)
    for copy in sends:
        copy.wait_send()
    for other in range(lanes):

        @pl.when(lane != other)
        def _():
            grad_link(other).wait_send()
            grad_arrival(other).wait_recv()

    for peer in range(count):

        @pl.when(me < peer)
        def _():
            state_link(peer, me).wait_send()

        @pl.when(me > peer)
        def _():
            state_link(peer, peer).wait_recv()

    own_w.wait()
    own_g.wait()


def fetch(out_weight, grad_out, final, count, lanes, pieces=4):
    half = count // 2
    sends = (half + half // 2 + (half - 1 - half // 2)) * pieces
    return pl.pallas_call(
        functools.partial(fetch_kernel, count, lanes),
        out_shape=(
            jax.ShapeDtypeStruct((count,) + out_weight.shape, out_weight.dtype),
            jax.ShapeDtypeStruct((lanes,) + grad_out.shape, grad_out.dtype),
            jax.ShapeDtypeStruct((count,) + final.shape, final.dtype),
        ),
        in_specs=[pl.BlockSpec(memory_space=pl.ANY)] * 2 + [pl.BlockSpec(memory_space=pltpu.VMEM)],
        out_specs=(
            pl.BlockSpec(memory_space=pl.ANY),
            pl.BlockSpec(memory_space=pl.ANY),
            pl.BlockSpec(memory_space=pltpu.VMEM),
        ),
        scratch_shapes=[
            pltpu.SemaphoreType.DMA((sends,)),
            pltpu.SemaphoreType.DMA((count * pieces,)),
            pltpu.SemaphoreType.DMA((lanes,)),
            pltpu.SemaphoreType.DMA((lanes,)),
            pltpu.SemaphoreType.DMA((2,)),
            pltpu.SemaphoreType.DMA((count,)),
            pltpu.SemaphoreType.DMA((count,)),
        ],
        compiler_params=pltpu.CompilerParams(collective_id=1, has_side_effects=True),
    )(out_weight, grad_out, final)


def per_device(query, key, value, short_taps, decay_rate, residue, skip_gain, out_weight, grad_out):
    tok_rows, chan_width = query.shape
    tap_count = short_taps.shape[0]
    mode_count = decay_rate.shape[0]
    highest = lax.Precision.HIGHEST
    count = lax.axis_size("seq")
    place = lax.axis_index("seq")

    lanes = lax.axis_size("ch")

    streams = jnp.stack([query, key, value])
    before = from_behind(streams[:, tok_rows - (tap_count - 1) :, :], "seq", 1)
    extended = jnp.concatenate([before, streams], axis=1).astype(jnp.float32)
    featured = jnp.zeros((3, tok_rows, chan_width), jnp.float32)
    for tap_index in range(tap_count):
        begin = tap_count - 1 - tap_index
        featured = (
            featured + short_taps[tap_index][:, None, :] * extended[:, begin : begin + tok_rows, :]
        )
    q_short = featured[0]
    k_short = featured[1]
    v_short = featured[2]
    gated = k_short * v_short

    width = mode_count * chan_width
    rate = decay_rate.reshape(1, width)
    mode_scale = (residue * jnp.sqrt(-jnp.expm1(-2.0 * decay_rate))).reshape(1, width)
    offsets = jnp.arange(tok_rows).astype(jnp.float32)[:, None]
    shrink = jnp.exp(-rate * offsets)
    grow = jnp.exp(rate * offsets)
    scaled_shrink = mode_scale * shrink
    scaled_grow = mode_scale * grow
    one_step = jnp.exp(-rate)
    block_decay = jnp.exp(-rate * tok_rows)
    rows = jnp.arange(tok_rows)
    lower = (rows[:, None] >= rows[None, :]).astype(jnp.float32)
    upper = (rows[:, None] <= rows[None, :]).astype(jnp.float32)

    def prefix(tri, weights, signal):
        spread = weights * jnp.concatenate([signal] * mode_count, axis=1)
        return jnp.dot(tri, spread, precision=highest, preferred_element_type=jnp.float32)

    def over_modes(table):
        total = table[:, :chan_width]
        for mode in range(1, mode_count):
            total = total + table[:, mode * chan_width : (mode + 1) * chan_width]
        return total

    source = jnp.arange(count)

    def entry(gap, got):
        span = (tok_rows * jnp.maximum(gap, 0)).astype(jnp.float32)[:, None]
        held = jnp.where((gap >= 0)[:, None], got.astype(jnp.float32), 0.0)
        return jnp.sum(jnp.exp(-rate * span) * held, axis=0, keepdims=True)

    fwd_sums = prefix(lower, grow, gated)
    fwd_final = (shrink[tok_rows - 1] * fwd_sums[tok_rows - 1]).astype(jnp.bfloat16)
    w_all, g_all, fwd_got = fetch(
        out_weight, grad_out, fwd_final.reshape(mode_count, chan_width), count, lanes
    )
    fwd_got = fwd_got.reshape(count, width)
    fwd_entry = entry(place - 1 - source, fwd_got) * one_step
    long_out = over_modes(scaled_shrink * (fwd_sums + fwd_entry)) + skip_gain[None, :] * gated
    mixer = (q_short * long_out).astype(jnp.bfloat16)
    parts = jnp.einsum("tr,jrc->jtc", mixer, w_all, preferred_element_type=jnp.float32)
    parts = parts.astype(jnp.bfloat16)
    parts, g_all, w_all = lax.optimization_barrier((parts, g_all, w_all))
    received = lax.all_to_all(parts, "ch", 0, 0, tiled=True)
    mixed = jnp.sum(received.astype(jnp.float32), axis=0).astype(jnp.bfloat16)

    grad_mixer = jnp.einsum("jtc,jrc->tr", g_all, w_all, preferred_element_type=jnp.float32)
    grad_long = grad_mixer * q_short
    bwd_sums = prefix(upper, shrink, grad_long)
    bwd_final = bwd_sums[0].astype(jnp.bfloat16).reshape(mode_count, chan_width)
    bwd_got = exchange(bwd_final, count, False, 3).reshape(count, width)
    bwd_entry = entry(source - place - 1, bwd_got) * block_decay

    grad_qshort = grad_mixer * long_out
    grad_gated = (
        over_modes(scaled_grow * (bwd_sums + bwd_entry)) + skip_gain[None, :] * grad_long
    )
    grad_stack = jnp.stack([grad_qshort, grad_gated * v_short, grad_gated * k_short])
    after = from_behind(grad_stack[:, : tap_count - 1, :], "seq", -1)
    extended_back = jnp.concatenate([grad_stack, after], axis=1)
    grads = jnp.zeros((3, tok_rows, chan_width), jnp.float32)
    for tap_index in range(tap_count):
        grads = (
            grads
            + short_taps[tap_index][:, None, :]
            * extended_back[:, tap_index : tap_index + tok_rows, :]
        )
    grads = grads.astype(jnp.bfloat16)
    return (mixed, grads[0], grads[1], grads[2])


def solution(mesh):
    in_specs = (
        P("seq", "ch"),
        P("seq", "ch"),
        P("seq", "ch"),
        P(None, None, "ch"),
        P(None, "ch"),
        P(None, "ch"),
        P("ch"),
        P("ch", "seq"),
        P("seq", "ch"),
    )
    out_specs = (P("seq", "ch"), P("seq", "ch"), P("seq", "ch"), P("seq", "ch"))
    return jax.shard_map(
        per_device, mesh=mesh, in_specs=in_specs, out_specs=out_specs, check_vma=False
    )
```
